32 devices in a mesh: dp: 16 (over z, y, x), tensor: 2 (over core).
Axes of the slice: x: 2, y: 2, z: 4, core: 2. Of those that a mesh axis runs over, the one named last changes fastest.
Arguments:
- inputs: bfloat16 [16, 1024, 768], P('dp', 'tensor'), may hold values from -6 to 6
- cotangent: bfloat16 [16, 1024, 768], P('dp', 'tensor'), may hold values from -6 to 6
- qkv_weight: bfloat16 [3, 768, 768], P(None, 'dp', 'tensor'), may hold values from -0.3125 to 0.3125
- out_weight: bfloat16 [768, 768], P('tensor', 'dp'), may hold values from -2.5 to 2.5
- fc1_weight: bfloat16 [768, 3072], P('dp', 'tensor'), may hold values from -0.21875 to 0.21875
- fc2_weight: bfloat16 [3072, 768], P('tensor', 'dp'), may hold values from -0.109375 to 0.109375
- norm_gains: bfloat16 [2, 768], P(None, 'dp'), may hold values from 0.25 to 1.75
- shifts: bfloat16 [4, 768], P(None, 'dp'), may hold values from -3 to 3
- qv_bias: bfloat16 [2, 768], P(None, 'tensor'), may hold values from -3 to 3
- fc1_bias: bfloat16 [3072], P('tensor'), may hold values from -3 to 3
Outputs:
- outputs: float32 [16, 1024, 768], P('dp', 'tensor')
- input_grad: float32 [16, 1024, 768], P('dp', 'tensor')
- qkv_grad: float32 [3, 768, 768], P(None, 'dp', 'tensor')
- out_grad: float32 [768, 768], P('tensor', 'dp')
- fc1_grad: float32 [768, 3072], P('dp', 'tensor')
- fc2_grad: float32 [3072, 768], P('tensor', 'dp')
- gains_grad: float32 [2, 768], P(None, 'dp')
- shifts_grad: float32 [4, 768], P(None, 'dp')
- qv_grad: float32 [2, 768], P(None, 'tensor')
- fc1_bias_grad: float32 [3072], P('tensor')
The draws below stay inside these ranges and needn't reach their ends.
All inputs are finite; a program needn't handle non-finite values.
Results may differ from the reference program's by a relative error of at most 0.012.
The reference program's roundings to bfloat16 on the way count: a program that leaves them out, or rounds other values in their place, can miss the bound.
Values may be sent and summed in bfloat16 or wider, within the bound.
No kernel may reach another device: no remote copies, remote signals or barrier semaphores. Data moves between devices by JAX's collectives and lax.ppermute only.
A program may use at most 192 MiB of HBM per device.

```python
import math
import jax
import jax.numpy as jnp
from jax import lax

D = 768
HEADS = 12
HEAD = 64
FF = 3072
FRAMES = 1024
CLIPS = 16


def strengthened(values, key, source, target, blocks, factor):
    def block_of(position):
        return (jnp.arange(values.shape[position]) // (values.shape[position] // blocks)).reshape((-1,) + (1,) * (values.ndim - 1 - position))

    one_side = jax.random.permutation(key, blocks)[block_of(target)]
    other_side = (block_of(target) + blocks // 2) % blocks
    return jnp.where((block_of(source) == one_side) | (block_of(source) == other_side), factor * values, values)


def block_scale(own_key, extent, cuts, smallest, top_value):
    def one(dim, parts):
        steps = jax.random.uniform(jax.random.fold_in(jax.random.fold_in(own_key, 6), dim), (parts,), jnp.float32, smallest / len(cuts), top_value / len(cuts))
        return jnp.repeat(jnp.exp(steps), extent[dim] // parts).reshape((-1,) + (1,) * (len(extent) - dim - 1))

    level = one(*cuts[0])
    for cut in cuts[1:]:
        level = level * one(*cut)
    return level


def noise(key, dims, scale, reach, shards=(), held_as=jnp.bfloat16):
    gain = block_scale(key, dims, shards, -0.22, 0.18) if shards else 1.0
    array = jax.random.normal(key, dims, jnp.float32) * scale * gain
    return jnp.minimum(jnp.maximum(array, -reach), reach).astype(held_as)


def noise_with(own_key, shape, deviation, most, split, heavy, held_as=jnp.bfloat16):
    drawn = deviation * jax.random.normal(own_key, shape, jnp.float32)
    if split:
        drawn = drawn * block_scale(own_key, shape, split, -0.22, 0.18)
    return jnp.clip(strengthened(drawn, jax.random.fold_in(own_key, 3), *heavy), -most, most).astype(held_as)


def setup_inputs(seed: int = 0) -> dict:
    seeds = jax.random.split(jax.random.key(seed), 11)
    return {
        "inputs": noise(seeds[0], (CLIPS, FRAMES, D), 1.0, 6.0, ((0, 16), (1, 2))),
        "cotangent": noise_with(seeds[1], (CLIPS, FRAMES, D), 1.0, 6.0, ((0, 16), (1, 2)), (0, 2, 16, 2.0)),
        "qkv_weight": noise(seeds[2], (3, D, D), (D // 2) ** -0.5, 0.3125, ((1, 16), (2, 2))),
        "out_weight": noise(seeds[3], (D, D), (max(D // 128, 2)) ** -0.5, 2.5, ((0, 2), (1, 16))),
        "fc1_weight": noise(seeds[4], (D, FF), D ** -0.5, 0.21875, ((0, 16), (1, 2))),
        "fc2_weight": noise(seeds[5], (FF, D), FF ** -0.5, 0.109375, ((0, 2), (1, 16))),
        "norm_gains": jnp.clip(1.0 + 0.15 * jax.random.normal(seeds[6], (2, D), jnp.float32), 0.25, 1.75).astype(jnp.bfloat16),
        "shifts": noise(seeds[7], (4, D), 0.5, 3.0, ((1, 16),)),
        "qv_bias": noise(seeds[8], (2, D), 0.5, 3.0, ((1, 2),)),
        "fc1_bias": noise(seeds[9], (FF,), 0.5, 3.0, ((0, 2),)),
    }


EPS = 1e-05
HIGH = lax.Precision.HIGHEST

@jax.custom_vjp
def low(v):
    return lax.optimization_barrier(v.astype(jnp.bfloat16)).astype(jnp.float32)

@jax.custom_vjp
def low_back(v):
    return v

def low_keep(v):
    return (low(v), None)

def low_pass(kept, grad):
    return (grad,)

def back_keep(v):
    return (v, None)

def back_low(kept, grad):
    return (low(grad),)
low.defvjp(low_keep, low_pass)
low_back.defvjp(back_keep, back_low)

def layer_norm(frames, scale_vec, shift_vec):
    center = frames - lax.optimization_barrier(jnp.mean(frames, axis=-1, keepdims=True))
    inv_std = lax.rsqrt(lax.optimization_barrier(jnp.mean(center * center, axis=-1, keepdims=True)) + EPS)
    return center * inv_std * scale_vec + shift_vec

def project(left, right):
    return jnp.einsum('cfd,de->cfe', left, right, precision=HIGH)

def attend(clip_data):
    queries, keys_all, values = clip_data
    scores = low_back(jnp.einsum('qhe,khe->hqk', queries, keys_all, precision=HIGH) * HEAD ** (-0.5))
    attn_probs = jax.nn.softmax(scores, axis=-1)
    return jnp.einsum('hqk,khe->qhe', low(attn_probs), values, precision=HIGH)

def forward(params, frames):
    qkv_weight, out_weight, fc1_weight, fc2_weight, norm_gains, shifts, qv_bias, fc1_bias = params
    clips_now = frames.shape[0]
    normed = low(layer_norm(frames, norm_gains[0], shifts[0]))
    queries = low(low_back(project(normed, qkv_weight[0]) + qv_bias[0]))
    keys_all = low(low_back(project(normed, qkv_weight[1])))
    values = low(low_back(project(normed, qkv_weight[2]) + qv_bias[1]))
    head_shape = (clips_now, FRAMES, HEADS, HEAD)
    attended = lax.map(jax.checkpoint(attend), (queries.reshape(head_shape), keys_all.reshape(head_shape), values.reshape(head_shape)))
    attended = low(low_back(attended.reshape(clips_now, FRAMES, D)))
    hidden = frames + low_back(project(attended, out_weight) + shifts[1])
    normed_two = low(layer_norm(hidden, norm_gains[1], shifts[2]))
    hidden_pre = low_back(project(normed_two, fc1_weight) + fc1_bias)
    hidden_act = low(jax.nn.gelu(hidden_pre, approximate=False))
    return hidden + low_back(project(hidden_act, fc2_weight) + shifts[3])

def reference(inputs, cotangent, qkv_weight, out_weight, fc1_weight, fc2_weight, norm_gains, shifts, qv_bias, fc1_bias):
    params = tuple((item.astype(jnp.float32) for item in (qkv_weight, out_weight, fc1_weight, fc2_weight, norm_gains, shifts, qv_bias, fc1_bias)))
    per_step = math.gcd(CLIPS, max(1, 4096 // FRAMES))
    num_steps = CLIPS // per_step
    frames_all = inputs.astype(jnp.float32).reshape(num_steps, per_step, FRAMES, D)
    back_all = cotangent.astype(jnp.float32).reshape(num_steps, per_step, FRAMES, D)

    def group_step(totals, pair):
        frames_grp, back_grp = pair
        result, pullback = jax.vjp(forward, params, frames_grp)
        d_params, d_frames = pullback(back_grp)
        totals = jax.tree.map(jnp.add, totals, d_params)
        return (totals, (result, d_frames))
    zero_grads = tuple((jnp.zeros_like(item) for item in params))
    totals, (outs_all, grads_in) = lax.scan(group_step, zero_grads, (frames_all, back_all))
    return (outs_all.reshape(CLIPS, FRAMES, D), grads_in.reshape(CLIPS, FRAMES, D), totals[0], totals[1], totals[2], totals[3], totals[4], totals[5], totals[6], totals[7])
```

```python
import jax
import jax.numpy as jnp
from jax import lax
from jax.sharding import PartitionSpec as P

HEAD = 64
EPS = 1e-05
BF = jnp.bfloat16
F32 = jnp.float32


def layer_norm(frames, scale_vec, shift_vec):
    center = frames - jnp.mean(frames, axis=-1, keepdims=True)
    inv_std = lax.rsqrt(jnp.mean(center * center, axis=-1, keepdims=True) + EPS)
    return center * inv_std * scale_vec + shift_vec


def gelu_exact(values):
    return jax.nn.gelu(values, approximate=False)


def digits_of(n):
    found, stride = [], 1
    while n > 1:
        radix = 4 if n % 4 == 0 else n
        found.append((stride, radix))
        stride *= radix
        n //= radix
    return found


def swap_dp(x, step):
    n = lax.axis_size("dp")
    return lax.ppermute(x, "dp", [(i, i ^ step) for i in range(n)])


def swap_core(x):
    return lax.ppermute(x, "tensor", [(0, 1), (1, 0)])


def pick(options, digit):
    while len(options) > 1:
        bit = (digit & 1) == 1
        options = [jnp.where(bit, b, a) for a, b in zip(options[0::2], options[1::2])]
        digit = digit >> 1
    return options[0]


def gather_rows(x):
    me = lax.axis_index("dp")
    cur = x[None]
    for stride, radix in reversed(digits_of(lax.axis_size("dp"))):
        mine = (me // stride) % radix
        got = [cur] + [swap_dp(cur, stride * k) for k in range(1, radix)]
        placed = [pick([got[i ^ m] for m in range(radix)], mine) for i in range(radix)]
        cur = jnp.stack(placed, axis=1).reshape((-1,) + x.shape)
    return cur.reshape((-1,) + x.shape[1:])


def scatter_rows(x, wire):
    me = lax.axis_index("dp")
    n = lax.axis_size("dp")
    shape = (x.shape[0] // n,) + x.shape[1:]
    cur = x.reshape((n,) + shape)
    for stride, radix in digits_of(n):
        mine = (me // stride) % radix
        view = cur.astype(wire).reshape((-1, radix) + shape)
        parts = [lax.dynamic_index_in_dim(view, mine ^ k, 1, keepdims=False) for k in range(radix)]
        total = parts[0].astype(F32)
        for k in range(1, radix):
            total = total + swap_dp(parts[k], stride * k).astype(F32)
        cur = total
    return cur.reshape(shape)


def sum_dp(x):
    for stride, radix in digits_of(lax.axis_size("dp")):
        total = x
        for k in range(1, radix):
            total = total + swap_dp(x, stride * k)
        x = total
    return x


def spread_frames(local):
    return jnp.concatenate([local, swap_core(local)], axis=0)


def fold_frames(terms):
    half = terms.shape[0] // 2
    return terms[:half] + swap_core(terms[half:])


def attend(queries, keys_all, values):
    frames_n = queries.shape[0]
    heads_here = queries.shape[1] // HEAD
    head_split = (frames_n, heads_here, HEAD)
    queries = queries.reshape(head_split)
    keys_all = keys_all.reshape(head_split)
    values = values.reshape(head_split)
    scores = jnp.einsum(
        "qhe,khe->hqk", queries, keys_all, preferred_element_type=F32
    ) * HEAD ** (-0.5)
    row_max = jnp.max(scores, axis=-1, keepdims=True)
    powers = jnp.exp(scores - row_max)
    summed = jnp.sum(powers, axis=-1, keepdims=True)
    attn_probs = (powers / summed).astype(BF)
    attended = jnp.einsum("hqk,khe->qhe", attn_probs, values, preferred_element_type=F32)
    return (
        attended.reshape(frames_n, heads_here * HEAD).astype(BF),
        (row_max + jnp.log(summed))[..., 0],
    )


def attend_back(queries, keys_all, values, log_sums, d_attended):
    frames_n = queries.shape[0]
    heads_here = queries.shape[1] // HEAD
    head_split = (frames_n, heads_here, HEAD)
    queries = queries.reshape(head_split)
    keys_all = keys_all.reshape(head_split)
    values = values.reshape(head_split)
    d_attended = d_attended.reshape(head_split)
    factor = HEAD ** (-0.5)
    scores = (
        jnp.einsum("qhe,khe->hqk", queries, keys_all, preferred_element_type=F32) * factor
    )
    attn_probs = jnp.exp(scores - log_sums[..., None])
    d_values = jnp.einsum(
        "hqk,qhe->khe", attn_probs.astype(BF), d_attended, preferred_element_type=F32
    )
    d_probs = jnp.einsum("qhe,khe->hqk", d_attended, values, preferred_element_type=F32)
    d_scores = (
        attn_probs * (d_probs - jnp.sum(d_probs * attn_probs, axis=-1, keepdims=True))
    ).astype(BF)
    d_queries = (
        jnp.einsum("hqk,khe->qhe", d_scores, keys_all, preferred_element_type=F32) * factor
    )
    d_keys = jnp.einsum("hqk,qhe->khe", d_scores, queries, preferred_element_type=F32) * factor
    width = heads_here * HEAD
    return [x.reshape(frames_n, width).astype(BF) for x in (d_queries, d_keys, d_values)]


def mm(spec, a, b):
    return jnp.einsum(spec, a, b, preferred_element_type=F32)


def body(
    inputs,
    cotangent,
    qkv_weight,
    out_weight,
    fc1_weight,
    fc2_weight,
    norm_gains,
    shifts,
    qv_bias,
    fc1_bias,
):
    inputs = inputs[0]
    cotangent = cotangent[0]
    own = norm_gains.shape[1]
    wide = qkv_weight.shape[2]
    half = inputs.shape[0]
    small = jnp.concatenate([norm_gains, shifts], axis=0)
    vectors = gather_rows(small).reshape(-1, 6, own).transpose(1, 0, 2).reshape(6, -1)
    vectors = vectors.astype(F32)
    gains, moves = vectors[:2], vectors[2:]
    qkv_full = gather_rows(qkv_weight.transpose(1, 0, 2).reshape(own, 3 * wide))
    out_full = gather_rows(out_weight.T)
    fc1_full = gather_rows(fc1_weight)
    fc2_full = gather_rows(fc2_weight.T)
    qv_wide = qv_bias.astype(F32)
    fc1_wide = fc1_bias.astype(F32)
    inputs_all = spread_frames(inputs)
    d_out_all = spread_frames(cotangent)
    frames = inputs.astype(F32)
    normed_all = layer_norm(inputs_all.astype(F32), gains[0], moves[0]).astype(BF)
    proj = mm("fd,de->fe", normed_all, qkv_full)
    queries = (proj[:, :wide] + qv_wide[0]).astype(BF)
    keys_all = proj[:, wide : 2 * wide].astype(BF)
    values = (proj[:, 2 * wide :] + qv_wide[1]).astype(BF)
    attended, log_sums = attend(queries, keys_all, values)
    branch = fold_frames(mm("fe,de->fd", attended, out_full))
    hidden = frames + (branch + moves[1])
    normed_two = layer_norm(hidden, gains[1], moves[2]).astype(BF)
    normed_two_all = spread_frames(normed_two)
    hidden_pre = mm("fd,dh->fh", normed_two_all, fc1_full) + fc1_wide
    hidden_act = gelu_exact(hidden_pre).astype(BF)
    mlp_out = fold_frames(mm("fh,dh->fd", hidden_act, fc2_full))
    outputs = hidden + (mlp_out + moves[3])

    d_out = cotangent.astype(F32)
    fc2_grad = scatter_rows(mm("fd,fh->dh", d_out_all, hidden_act), BF)
    d_act = mm("fd,dh->fh", d_out_all, fc2_full)
    _, gelu_pull = jax.vjp(gelu_exact, hidden_pre)
    d_pre = gelu_pull(d_act)[0].astype(BF)
    fc1_bias_grad = jnp.sum(d_pre.astype(F32), axis=0)
    fc1_grad = scatter_rows(mm("fd,fh->dh", normed_two_all, d_pre), BF)
    d_normed_two = fold_frames(mm("fh,dh->fd", d_pre, fc1_full))
    _, norm_pull = jax.vjp(layer_norm, hidden, gains[1], moves[2])
    d_hid_norm, gain_two, shift_two = norm_pull(d_normed_two)
    shift_last = jnp.sum(d_out, axis=0)
    d_hidden = d_out + d_hid_norm
    d_branch = d_hidden.astype(BF)
    shift_attn = jnp.sum(d_branch.astype(F32), axis=0)
    d_branch_all = spread_frames(d_branch)
    out_grad = scatter_rows(mm("fd,fe->de", d_branch_all, attended), BF)
    d_attended = mm("fd,de->fe", d_branch_all, out_full).astype(BF)
    d_proj = attend_back(queries, keys_all, values, log_sums, d_attended)
    qkv_grad = scatter_rows(
        jnp.concatenate([mm("fd,fe->de", normed_all, x) for x in d_proj], axis=1), BF
    )
    qv_grad = [jnp.sum(x.astype(F32), axis=0) for x in (d_proj[0], d_proj[2])]
    d_normed = fold_frames(mm("fe,de->fd", jnp.concatenate(d_proj, axis=1), qkv_full))
    _, first_pull = jax.vjp(layer_norm, frames, gains[0], moves[0])
    d_in_norm, gain_one, shift_one = first_pull(d_normed)
    input_grad = d_hidden + d_in_norm
    rows = jnp.stack([gain_one, gain_two, shift_one, shift_attn, shift_two, shift_last])
    rows = rows + swap_core(rows)
    flat = sum_dp(jnp.concatenate([rows.reshape(-1), *qv_grad, fc1_bias_grad]))
    rows = flat[: rows.size].reshape(rows.shape)
    rest = flat[rows.size :]
    rows = lax.dynamic_slice_in_dim(rows, lax.axis_index("dp") * own, own, axis=1)
    return (
        outputs[None],
        input_grad[None],
        qkv_grad.reshape(own, 3, wide).transpose(1, 0, 2),
        out_grad.T,
        fc1_grad,
        fc2_grad.T,
        rows[:2],
        rows[2:],
        rest[: 2 * wide].reshape(2, wide),
        rest[2 * wide :],
    )


def solution(mesh):
    specs_in = (
        P("dp", "tensor", None),
        P("dp", "tensor", None),
        P(None, "dp", "tensor"),
        P("tensor", "dp"),
        P("dp", "tensor"),
        P("tensor", "dp"),
        P(None, "dp"),
        P(None, "dp"),
        P(None, "tensor"),
        P("tensor"),
    )
    return jax.shard_map(
        body, mesh=mesh, in_specs=specs_in, out_specs=specs_in, check_vma=False
    )
```

```python
import jax
import jax.numpy as jnp
from jax import lax
from jax.experimental import pallas as pl
from jax.experimental.pallas import tpu as pltpu
from jax.sharding import PartitionSpec as P

HEAD = 64
PAIR = 2 * HEAD
ATTEND_VMEM = 20 * 2**20
BACK_VMEM = 24 * 2**20
ROWS_VMEM = 24 * 2**20
PIECES = 2
ROW_BLOCK = 256
FREE = pl.CostEstimate(flops=0, bytes_accessed=0, transcendentals=0)
EPS = 1e-05
BF = jnp.bfloat16
F32 = jnp.float32


def after(x, *others):
    return lax.optimization_barrier((x, others))[0]


def stage(*values):
    return lax.optimization_barrier(values)


def digits_of(n):
    low = 4 if n % 4 == 0 else n
    found, stride = [(1, low)], low
    while stride < n:
        found.append((stride, 2))
        stride *= 2
    return found


def swap_dp(x, step):
    n = lax.axis_size("dp")
    return lax.ppermute(x, "dp", [(i, i ^ step) for i in range(n)])


def swap_core(x):
    return lax.ppermute(x, "tensor", [(0, 1), (1, 0)])


def digit(stride, radix):
    return (lax.axis_index("dp") // stride) % radix


def pick(options, index):
    while len(options) > 1:
        bit = (index & 1) == 1
        options = [jnp.where(bit, b, a) for a, b in zip(options[0::2], options[1::2])]
        index = index >> 1
    return options[0]


def place(got, stride):
    radix = len(got)
    mine = digit(stride, radix)
    placed = [pick([got[i ^ m] for m in range(radix)], mine) for i in range(radix)]
    return jnp.stack(placed, axis=1).reshape((-1,) + got[0].shape[1:])


def gather_high_at_once(x):
    n = lax.axis_size("dp")
    low = digits_of(n)[0][1]
    stride = n // 4
    cur = place([x[None]] + [swap_dp(x[None], stride * k) for k in range(1, 4)], stride)
    while stride > low:
        stride //= 2
        cur = place([cur, swap_dp(cur, stride)], stride)
    return cur


def gather_near(cur):
    return swap_dp(cur, 1), swap_dp(cur, 2)


def gather_far(near):
    half = near[0].shape[0] // 2
    return swap_dp(near[0][:half], 2), swap_dp(near[1][half:], 1)


def gather_low(cur):
    return [swap_dp(cur, k) for k in range(1, digits_of(lax.axis_size("dp"))[0][1])]


def rows_kernel(mine_ref, *refs):
    sources, out_ref = refs[:-1], refs[-1]
    mine = mine_ref[0]
    for k, source in enumerate(sources[:3]):
        out_ref[0, mine ^ k] = source[0]
    far = sources[3][0]
    if len(sources) > 4:
        far = jnp.where(pl.program_id(0) < pl.num_programs(0) // 2, far, sources[4][0])
    out_ref[0, mine ^ 3] = far


def all_rows(sources, start, columns):
    high, rows, _ = sources[0].shape
    half = high // 2
    column = start // columns

    def spec(source):
        if source.shape[0] == high:
            return pl.BlockSpec((1, rows, columns), lambda i, m: (i, 0, column))
        return pl.BlockSpec((1, rows, columns), lambda i, m: (i % half, 0, 0))

    full = pl.pallas_call(
        rows_kernel,
        grid_spec=pltpu.PrefetchScalarGridSpec(
            num_scalar_prefetch=1,
            grid=(high,),
            in_specs=[spec(x) for x in sources],
            out_specs=pl.BlockSpec((1, 4, rows, columns), lambda i, m: (i, 0, 0, 0)),
        ),
        out_shape=jax.ShapeDtypeStruct((high, 4, rows, columns), BF),
        cost_estimate=FREE,
        compiler_params=pltpu.CompilerParams(vmem_limit_bytes=8 * 2**20),
        name="all_rows",
    )(digit(1, 4).astype(jnp.int32).reshape(1), *sources)
    return full.reshape(-1, columns)


def split_low(x):
    n = lax.axis_size("dp")
    radix = digits_of(n)[0][1]
    view = x.reshape(n // radix, radix, x.shape[0] // n, x.shape[1])
    mine = digit(1, radix)
    return [lax.dynamic_index_in_dim(view, mine ^ k, 1, keepdims=False) for k in range(radix)]


def total_of(parts):
    total = parts[0].astype(F32)
    for part in parts[1:]:
        total = total + part.astype(F32)
    return total


def scatter_operands(x):
    mine, one, two, across = split_low(x)
    half = mine.shape[0] // 2
    return (mine, one, two), (across[:half], across[half:])


def scatter_low_across(operands):
    return swap_dp(operands[0], 1), swap_dp(operands[1], 2)


def near_operands(parts, across):
    mine, one, two = parts
    half = mine.shape[0] // 2
    one = jnp.concatenate([one[:half], total_of([one[half:], across[1]]).astype(BF)], axis=0)
    two = jnp.concatenate([total_of([two[:half], across[0]]).astype(BF), two[half:]], axis=0)
    return mine, one, two


def scatter_low_near(operands):
    mine, one, two = operands
    return mine, swap_dp(one, 1), swap_dp(two, 2)


def high_operands(cur, index):
    stride, radix = digits_of(lax.axis_size("dp"))[1 + index]
    view = cur.reshape((-1, radix) + cur.shape[1:])
    mine = digit(stride, radix)
    return [
        lax.dynamic_index_in_dim(view, mine ^ k, 1, keepdims=False).astype((F32, BF)[k])
        for k in range(radix)
    ]


def scatter_high_step(operands, index):
    stride, _ = digits_of(lax.axis_size("dp"))[1 + index]
    return operands[0] + swap_dp(operands[1], stride).astype(F32)


def scatter_high_rest(cur, index):
    for i in range(index, len(digits_of(lax.axis_size("dp"))) - 1):
        cur = scatter_high_step(high_operands(cur, i), i)
    return cur.reshape(cur.shape[1:])


def sum_dp(x):
    for stride, radix in digits_of(lax.axis_size("dp")):
        x = total_of([x] + [swap_dp(x, stride * k) for k in range(1, radix)])
    return x


def swap_pieces(x, count):
    rows = x.shape[0] // count
    return [swap_core(x[i * rows : (i + 1) * rows]) for i in range(count)]


def dot(a, b, ca, cb):
    return lax.dot_general(a, b, (((ca,), (cb,)), ((), ())), preferred_element_type=F32)


def attend_kernel(qkv_ref, *refs):
    out_ref, lse_ref = refs[-2:]
    queries = qkv_ref[:, :PAIR]
    keys_all = qkv_ref[:, PAIR : 2 * PAIR] * jnp.asarray(HEAD**-0.5, BF)
    values = qkv_ref[:, 2 * PAIR :]
    first = lax.broadcasted_iota(jnp.int32, (1, PAIR), 1) < HEAD
    outs, logs = [], []
    for own in (first, ~first):
        here = jnp.where(own, queries, jnp.zeros_like(queries))
        scores = dot(keys_all, here, 1, 1)
        row_max = jnp.max(scores, axis=0, keepdims=True)
        powers = jnp.exp(scores - row_max)
        summed = jnp.sum(powers, axis=0, keepdims=True)
        probs = (powers * (1.0 / summed)).astype(BF)
        outs.append(dot(values, probs, 0, 0))
        logs.append(row_max + jnp.log(summed))
    both = jnp.concatenate([outs[0][:HEAD], outs[1][HEAD:]], axis=0)
    out_ref[...] = both.T.astype(BF)
    lse_ref[...] = jnp.concatenate(logs, axis=0)[None]


def attend(qkv, start, count, kept=()):
    n, width = qkv.shape
    pairs = width // (3 * PAIR)
    return pl.pallas_call(
        attend_kernel,
        grid=(count,),
        in_specs=[pl.BlockSpec((n, 3 * PAIR), lambda p: (0, p + start))]
        + [pl.BlockSpec(memory_space=pl.ANY)] * len(kept),
        out_specs=[
            pl.BlockSpec((n, PAIR), lambda p: (0, p + start)),
            pl.BlockSpec((1, 2, n), lambda p: (p + start, 0, 0)),
        ],
        out_shape=[
            jax.ShapeDtypeStruct((n, pairs * PAIR), BF),
            jax.ShapeDtypeStruct((pairs, 2, n), F32),
        ],
        input_output_aliases={1 + i: i for i in range(len(kept))},
        compiler_params=pltpu.CompilerParams(vmem_limit_bytes=ATTEND_VMEM),
        cost_estimate=FREE,
        name="attend",
    )(qkv, *kept)


def attend_back_kernel(qkv_ref, lse_ref, grad_ref, *refs):
    out_ref, sum_ref = refs[-2:]
    factor = jnp.asarray(HEAD**-0.5, BF)
    queries = qkv_ref[:, :PAIR]
    keys_small = qkv_ref[:, PAIR : 2 * PAIR] * factor
    values = qkv_ref[:, 2 * PAIR :]
    grad = grad_ref[...]
    first = lax.broadcasted_iota(jnp.int32, (1, PAIR), 1) < HEAD
    parts = []
    for own in (first, ~first):
        q_here = jnp.where(own, queries, jnp.zeros_like(queries))
        g_here = jnp.where(own, grad, jnp.zeros_like(grad))
        parts.append((q_here, g_here, dot(keys_small, q_here, 1, 1), dot(values, g_here, 1, 1)))
    d_q, d_k, d_v = [], [], []
    for head, (q_here, g_here, scores, d_probs) in enumerate(parts):
        probs = jnp.exp(scores - lse_ref[0, head : head + 1, :])
        product = probs * d_probs
        row_sum = jnp.sum(product, axis=0, keepdims=True)
        d_scores = (product - probs * row_sum).astype(BF)
        d_v.append(dot(probs.astype(BF), g_here, 1, 0))
        d_k.append(dot(d_scores, q_here, 1, 0))
        d_q.append(dot(keys_small, d_scores, 0, 0))
    queries_t = jnp.concatenate([d_q[0][:HEAD], d_q[1][HEAD:]], axis=0)
    d_queries = queries_t.T.astype(BF)
    d_keys = ((d_k[0] + d_k[1]) * HEAD**-0.5).astype(BF)
    d_values = (d_v[0] + d_v[1]).astype(BF)
    for i, x in enumerate((d_queries, d_keys, d_values)):
        out_ref[:, i * PAIR : (i + 1) * PAIR] = x
        sum_ref[0, :, i * PAIR : (i + 1) * PAIR] = jnp.sum(x.astype(F32), axis=0, keepdims=True)


def attend_back(qkv, lse, grad, start, count, kept=()):
    n, width = qkv.shape
    pairs = width // (3 * PAIR)
    return pl.pallas_call(
        attend_back_kernel,
        grid=(count,),
        in_specs=[
            pl.BlockSpec((n, 3 * PAIR), lambda p: (0, p + start)),
            pl.BlockSpec((1, 2, n), lambda p: (p + start, 0, 0)),
            pl.BlockSpec((n, PAIR), lambda p: (0, p + start)),
        ]
        + [pl.BlockSpec(memory_space=pl.ANY)] * len(kept),
        out_specs=[
            pl.BlockSpec((n, 3 * PAIR), lambda p: (0, p + start)),
            pl.BlockSpec((1, 1, 3 * PAIR), lambda p: (p + start, 0, 0)),
        ],
        out_shape=[
            jax.ShapeDtypeStruct((n, width), BF),
            jax.ShapeDtypeStruct((pairs, 1, 3 * PAIR), F32),
        ],
        input_output_aliases={3 + i: i for i in range(len(kept))},
        compiler_params=pltpu.CompilerParams(vmem_limit_bytes=BACK_VMEM),
        cost_estimate=FREE,
        name="attend_back",
    )(qkv, lse, grad, *kept)


def row_block(rows, columns, shift=0, total=0):
    if shift:
        return pl.BlockSpec((rows, columns), lambda i: ((i + shift) % total, 0))
    return pl.BlockSpec((rows, columns), lambda i: (i, 0))


def whole(shape):
    zero = (0,) * len(shape)
    return pl.BlockSpec(shape, lambda i: zero)


def rows_call(kernel, grid, in_specs, out_specs, out_shape, name):
    return pl.pallas_call(
        kernel,
        grid=(grid,),
        in_specs=in_specs,
        out_specs=out_specs,
        out_shape=out_shape,
        cost_estimate=FREE,
        compiler_params=pltpu.CompilerParams(vmem_limit_bytes=ROWS_VMEM),
        name=name,
    )


def join_kernel(mine_ref, other_ref, out_ref):
    half = mine_ref.shape[0]
    out_ref[:half] = mine_ref[...]
    out_ref[half:] = other_ref[...]


def join(mine, other):
    rows, columns = mine.shape
    return rows_call(
        join_kernel,
        1,
        [whole(mine.shape)] * 2,
        whole((2 * rows, columns)),
        jax.ShapeDtypeStruct((2 * rows, columns), mine.dtype),
        "join",
    )(mine, other)


def standardized(x):
    center = x - jnp.mean(x, axis=-1, keepdims=True)
    inv_std = lax.rsqrt(jnp.mean(center * center, axis=-1, keepdims=True) + EPS)
    return center * inv_std, inv_std


def project_kernel(x_ref, weight_ref, small_ref, bias_ref, normed_ref, qkv_ref, vectors_ref):
    vectors = small_ref[...].astype(F32).T[:8]
    vectors_ref[...] = vectors
    unit, _ = standardized(x_ref[...].astype(F32))
    normed = (unit * vectors[0:1] + vectors[2:3]).astype(BF)
    normed_ref[...] = normed
    qkv_ref[...] = (dot(normed, weight_ref[...], 1, 0) + bias_ref[...]).astype(BF)


def project(x, first_full, bias, width):
    rows, columns = x.shape
    block = rows // 4
    small = first_full.shape[1] // PAIR - 1
    return rows_call(
        project_kernel,
        4,
        [
            row_block(block, columns),
            whole((columns, width)),
            pl.BlockSpec((columns, PAIR), lambda i: (0, small)),
            whole(bias.shape),
        ],
        [row_block(block, columns), row_block(block, width), whole((8, columns))],
        [
            jax.ShapeDtypeStruct((rows, columns), BF),
            jax.ShapeDtypeStruct((rows, width), BF),
            jax.ShapeDtypeStruct((8, columns), F32),
        ],
        "project",
    )(x, first_full, first_full, bias)


def blocks_of(x_ref, others):
    rows = x_ref.shape[0] // PIECES
    found = []
    for i in range(0, x_ref.shape[0], ROW_BLOCK):
        other = others[(i // rows + PIECES // 2) % PIECES]
        found.append((pl.ds(i, ROW_BLOCK), other, pl.ds(i % rows, ROW_BLOCK)))
    return found


def mid_norm_kernel(x_ref, mine_ref, vectors_ref, *refs):
    others, (hidden_ref, normed_ref) = refs[:PIECES], refs[PIECES:]
    for here, other_ref, there in blocks_of(x_ref, others):
        branch = mine_ref[here].astype(F32) + other_ref[there].astype(F32)
        hidden = x_ref[here].astype(F32) + (branch + vectors_ref[3:4])
        hidden_ref[here] = hidden
        unit, _ = standardized(hidden)
        normed_ref[here] = (unit * vectors_ref[1:2] + vectors_ref[4:5]).astype(BF)


def mid_norm(x, mine, others, vectors):
    args = (x, mine, vectors, *others)
    return rows_call(
        mid_norm_kernel,
        1,
        [whole(a.shape) for a in args],
        [whole(x.shape)] * 2,
        [jax.ShapeDtypeStruct(x.shape, t) for t in (F32, BF)],
        "mid_norm",
    )(*args)


def norm_back(unit, inv_std, gain, grad):
    scaled = grad * gain
    return inv_std * (
        scaled
        - jnp.mean(scaled, axis=-1, keepdims=True)
        - unit * jnp.mean(scaled * unit, axis=-1, keepdims=True)
    )


def total_rows(x):
    return jnp.sum(x, axis=0, keepdims=True)


def mid_norm_back_kernel(mine_ref, hidden_ref, d_out_ref, vectors_ref, *refs):
    others, (branch_ref, d_hidden_ref, sums_ref) = refs[:PIECES], refs[PIECES:]
    sums = [jnp.zeros((1, hidden_ref.shape[1]), F32)] * 4
    for here, other_ref, there in blocks_of(hidden_ref, others):
        grad = mine_ref[here].astype(F32) + other_ref[there].astype(F32)
        unit, inv_std = standardized(hidden_ref[here])
        d_out = d_out_ref[here].astype(F32)
        d_hidden = d_out + norm_back(unit, inv_std, vectors_ref[1:2], grad)
        d_branch = d_hidden.astype(BF)
        branch_ref[here] = d_branch
        if here.start < d_hidden_ref.shape[0]:
            d_hidden_ref[here] = d_hidden
            terms = (grad * unit, d_branch.astype(F32), grad, d_out)
            sums = [a + total_rows(b) for a, b in zip(sums, terms)]
    sums_ref[...] = jnp.concatenate(sums, axis=0)


def mid_norm_back(mine, others, hidden, d_out, vectors):
    rows, columns = hidden.shape
    args = (mine, hidden, d_out, vectors, *others)
    shapes = (
        jax.ShapeDtypeStruct((rows, columns), BF),
        jax.ShapeDtypeStruct((rows // 2, columns), F32),
        jax.ShapeDtypeStruct((4, columns), F32),
    )
    return rows_call(
        mid_norm_back_kernel,
        1,
        [whole(a.shape) for a in args],
        [whole(x.shape) for x in shapes],
        shapes,
        "mid_norm_back",
    )(*args)


def first_norm_back_kernel(
    qkv_ref, weight_ref, x_ref, d_hidden_ref, vectors_ref, first_ref, second_ref, grad_ref, sums_ref
):
    other = jnp.where(pl.program_id(0) == 0, first_ref[...], second_ref[...])
    grad = dot(qkv_ref[...], weight_ref[...], 1, 1) + other.astype(F32)
    unit, inv_std = standardized(x_ref[...].astype(F32))
    grad_ref[...] = d_hidden_ref[...] + norm_back(unit, inv_std, vectors_ref[0:1], grad)

    @pl.when(pl.program_id(0) == 0)
    def _():
        sums_ref[...] = jnp.zeros_like(sums_ref)

    sums_ref[0:1] += total_rows(grad * unit)
    sums_ref[1:2] += total_rows(grad)


def first_norm_back(d_qkv, first_full, others, x, d_hidden, vectors):
    rows, columns = x.shape
    width = d_qkv.shape[1]
    block = rows // 2
    plain = row_block(block, columns)
    return rows_call(
        first_norm_back_kernel,
        2,
        [
            row_block(block, width),
            whole((columns, width)),
            plain,
            plain,
            whole(vectors.shape),
            whole((block, columns)),
            whole((block, columns)),
        ],
        [plain, whole((2, columns))],
        [jax.ShapeDtypeStruct((rows, columns), F32), jax.ShapeDtypeStruct((2, columns), F32)],
        "first_norm_back",
    )(d_qkv, first_full, x, d_hidden, vectors, *others)


def mm(spec, a, b):
    return jnp.einsum(spec, a, b, preferred_element_type=F32)


def body(
    inputs,
    cotangent,
    qkv_weight,
    out_weight,
    fc1_weight,
    fc2_weight,
    norm_gains,
    shifts,
    qv_bias,
    fc1_bias,
):
    inputs = inputs[0]
    cotangent = cotangent[0]
    own = norm_gains.shape[1]
    wide = qkv_weight.shape[2]
    pairs = wide // PAIR

    first_own = (
        qkv_weight.reshape(3, own, pairs, PAIR).transpose(1, 2, 0, 3).reshape(own, 3 * wide)
    )
    small = jnp.concatenate([norm_gains, shifts, jnp.zeros((PAIR - 6, own), BF)], axis=0)
    first_own = jnp.concatenate([first_own, out_weight.T, small.T], axis=1)
    zeros = jnp.zeros((wide,), BF)
    qkv_bias = jnp.stack([qv_bias[0], zeros, qv_bias[1]]).reshape(3, pairs, PAIR)
    qkv_bias = qkv_bias.transpose(1, 0, 2).reshape(1, 3 * wide).astype(F32)
    half = inputs.shape[0]
    hidden_n = fc1_weight.shape[1]
    high = [stride for stride, _ in reversed(digits_of(lax.axis_size("dp"))[1:])]
    first_part = gather_high_at_once(first_own)
    inputs_other = swap_core(inputs)

    ff_own = jnp.concatenate([fc1_weight, fc2_weight.T], axis=1)

    first_part, inputs_other, ff_part = stage(first_part, inputs_other, ff_own[None])
    first_near = gather_near(first_part)
    inputs_all = join(inputs, inputs_other)
    for stride in high[:-1]:
        ff_part = place([ff_part, swap_dp(ff_part, stride)], stride)

    first_part, first_near, ff_part, inputs_all = stage(
        first_part, first_near, ff_part, inputs_all
    )
    first_far = gather_far(first_near)
    for stride in high[-1:]:
        ff_part = place([ff_part, swap_dp(ff_part, stride)], stride)

    first_part, first_near, first_far, ff_part = stage(first_part, first_near, first_far, ff_part)
    ff_near = gather_near(ff_part)
    cotangent_other = swap_core(after(cotangent, first_part))
    first_full = all_rows([first_part, *first_near, *first_far], 0, first_part.shape[2])
    out_full = first_full[:, 3 * wide : 4 * wide]
    normed_all, qkv, vectors = project(inputs_all, first_full, qkv_bias, 3 * wide)
    attended, log_sums = attend(qkv, 0, pairs)
    branch = mm("fe,de->fd", attended, out_full).astype(BF)
    branch_other = swap_pieces(branch, PIECES)
    hidden_all, normed_two_all = mid_norm(inputs_all, branch, branch_other, vectors)

    ff_part, ff_near, normed_two_all, cotangent_other = stage(
        ff_part, ff_near, normed_two_all, cotangent_other
    )
    mid_far = gather_far([x[:, :, :hidden_n] for x in ff_near])
    d_out_all = join(cotangent, cotangent_other)

    ff_part, ff_near, mid_far, d_out_all = stage(ff_part, ff_near, mid_far, d_out_all)
    end_far = gather_far([x[:, :, hidden_n:] for x in ff_near])
    mid_full = all_rows([ff_part, *ff_near, *mid_far], 0, hidden_n)
    hidden_pre = mm("fd,dh->fh", normed_two_all, mid_full) + fc1_bias.astype(F32)
    cdf = 0.5 * (1.0 + lax.erf(hidden_pre * 0.5**0.5))
    hidden_act = (hidden_pre * cdf).astype(BF)
    slope = cdf + hidden_pre * jnp.exp(-0.5 * hidden_pre * hidden_pre) * 0.3989422804014327
    hidden_act, slope, d_out_all = stage(hidden_act, slope.astype(BF), d_out_all)
    fc2_grad = mm("fd,fh->dh", d_out_all, hidden_act).astype(BF)
    fc2_parts, fc2_ops = scatter_operands(fc2_grad)

    ff_part, ff_near, end_far, d_out_all, fc2_ops = stage(
        ff_part, ff_near, end_far, d_out_all, fc2_ops
    )
    fc2_far = scatter_low_across(fc2_ops)
    end_full = all_rows([ff_part, *ff_near, *end_far], hidden_n, hidden_n)
    d_act = mm("fd,dh->fh", d_out_all, end_full)
    d_pre = (d_act * slope).astype(BF)
    fc1_bias_grad = jnp.sum(d_pre.astype(F32), axis=0, keepdims=True)
    d_two = mm("fh,dh->fd", d_pre, mid_full).astype(BF)

    d_two, fc2_far, d_pre = stage(d_two, fc2_far, d_pre)
    fc2_near = scatter_low_near(near_operands(fc2_parts, fc2_far))
    d_two_other = swap_pieces(d_two, PIECES)
    fc1_grad = mm("fd,fh->dh", normed_two_all, d_pre).astype(BF)
    d_branch_all, d_hidden, mid_sums = mid_norm_back(
        d_two, d_two_other, hidden_all, d_out_all, vectors
    )
    d_attended = mm("fd,de->fe", d_branch_all, out_full).astype(BF)
    out_grad = mm("fd,fe->de", d_branch_all, attended).astype(BF)
    mid_parts, mid_ops = scatter_operands(jnp.concatenate([fc1_grad, out_grad], axis=1))

    d_attended, mid_ops = stage(d_attended, mid_ops)
    mid_far = scatter_low_across(mid_ops)
    d_proj = attend_back(qkv, log_sums, d_attended, 0, pairs - 1)

    d_proj, mid_far, fc2_near = stage(d_proj, mid_far, fc2_near)
    mid_near = scatter_low_near(near_operands(mid_parts, mid_far))
    fc2_sum = scatter_high_step(high_operands(total_of(fc2_near), 0), 0)
    d_qkv, d_sums = attend_back(qkv, log_sums, d_attended, pairs - 1, 1, d_proj)
    d_other = mm("fe,de->fd", d_qkv[half:], first_full[:, : 3 * wide]).astype(BF)
    d_other_got = swap_pieces(d_other, 2)
    qkv_grad = mm("fd,fe->de", normed_all, d_qkv).astype(BF)
    qkv_parts, qkv_ops = scatter_operands(qkv_grad)

    qkv_ops, d_other_got = stage(qkv_ops, d_other_got)
    qkv_far = scatter_low_across(qkv_ops)
    input_grad, first_sums = first_norm_back(
        d_qkv, first_full, d_other_got, inputs, d_hidden, vectors
    )

    qkv_far, mid_near, first_sums, hidden_act, fc2_sum = stage(
        qkv_far, mid_near, first_sums, hidden_act, fc2_sum
    )
    qkv_near = scatter_low_near(near_operands(qkv_parts, qkv_far))
    mid_sum = scatter_high_step(high_operands(total_of(mid_near), 0), 0)
    fc2_out = scatter_high_rest(fc2_sum, 1)
    mlp_other = mm("fh,dh->fd", hidden_act[half:], end_full).astype(BF)
    mlp_got = swap_core(mlp_other)
    mlp_mine = mm("fh,dh->fd", hidden_act[:half], end_full)
    outputs = hidden_all[:half] + ((mlp_mine + mlp_got.astype(F32)) + vectors[5:6])

    mid_sum, qkv_near, first_sums, outputs = stage(mid_sum, qkv_near, first_sums, outputs)
    mid_out = scatter_high_rest(mid_sum, 1)
    qkv_out = scatter_high_rest(total_of(qkv_near), 0)

    rows = jnp.concatenate([first_sums, mid_sums], axis=0)
    rows = rows + swap_core(rows)
    width = rows.shape[1]
    flat = [rows, jnp.pad(d_sums[:, 0], ((0, 0), (0, width - 3 * PAIR)))]
    flat += [fc1_bias_grad[:, i : i + width] for i in range(0, fc1_bias_grad.shape[1], width)]
    flat = sum_dp(jnp.concatenate(flat, axis=0))
    rows = lax.dynamic_slice_in_dim(flat[:6], lax.axis_index("dp") * own, own, axis=1)
    sums = flat[6 : 6 + pairs, : 3 * PAIR].reshape(pairs, 3, PAIR)
    return (
        outputs[None],
        input_grad[None],
        qkv_out.reshape(own, pairs, 3, PAIR).transpose(2, 0, 1, 3).reshape(3, own, wide),
        mid_out[:, hidden_n:].T,
        mid_out[:, :hidden_n],
        fc2_out.T,
        rows[0:3:2],
        jnp.concatenate([rows[1:2], rows[3:6]], axis=0),
        sums[:, 0::2].transpose(1, 0, 2).reshape(2, wide),
        flat[6 + pairs :].reshape(-1),
    )


def solution(mesh):
    specs = (
        P("dp", "tensor", None),
        P("dp", "tensor", None),
        P(None, "dp", "tensor"),
        P("tensor", "dp"),
        P("dp", "tensor"),
        P("tensor", "dp"),
        P(None, "dp"),
        P(None, "dp"),
        P(None, "tensor"),
        P("tensor"),
    )
    return jax.shard_map(body, mesh=mesh, in_specs=specs, out_specs=specs, check_vma=False)
```

```python
import functools

import jax
import jax.numpy as jnp
from jax import lax
from jax.experimental import pallas as pl
from jax.experimental.pallas import tpu as pltpu
from jax.sharding import PartitionSpec as P

HEAD = 64
PAIR = 2 * HEAD
ATTEND_VMEM = 20 * 2**20
BACK_VMEM = 24 * 2**20
ROWS_VMEM = 16 * 2**20
PIECES = 2
ROW_BLOCK = 256
FREE = pl.CostEstimate(flops=0, bytes_accessed=0, transcendentals=0)
EPS = 1e-05
BF = jnp.bfloat16
F32 = jnp.float32


def after(x, *others):
    return lax.optimization_barrier((x, others))[0]


def stage(*values):
    return lax.optimization_barrier(values)


def digits_of(n):
    low = 4 if n % 4 == 0 else n
    found, stride = [(1, low)], low
    while stride < n:
        found.append((stride, 2))
        stride *= 2
    return found


def swap_dp(x, step):
    n = lax.axis_size("dp")
    return lax.ppermute(x, "dp", [(i, i ^ step) for i in range(n)])


def swap_core(x):
    return lax.ppermute(x, "tensor", [(0, 1), (1, 0)])


def digit(stride, radix):
    return (lax.axis_index("dp") // stride) % radix


def pick(options, index):
    while len(options) > 1:
        bit = (index & 1) == 1
        options = [jnp.where(bit, b, a) for a, b in zip(options[0::2], options[1::2])]
        index = index >> 1
    return options[0]


def place(got, stride):
    radix = len(got)
    mine = digit(stride, radix)
    placed = [pick([got[i ^ m] for m in range(radix)], mine) for i in range(radix)]
    return jnp.stack(placed, axis=1).reshape((-1,) + got[0].shape[1:])


def gather_high_at_once(x):
    n = lax.axis_size("dp")
    low = digits_of(n)[0][1]
    stride = n // 4
    cur = place([x[None]] + [swap_dp(x[None], stride * k) for k in range(1, 4)], stride)
    while stride > low:
        stride //= 2
        cur = place([cur, swap_dp(cur, stride)], stride)
    return cur


def gather_near(cur):
    return swap_dp(cur, 1), swap_dp(cur, 2)


def gather_far(near):
    half = near[0].shape[0] // 2
    return swap_dp(near[0][:half], 2), swap_dp(near[1][half:], 1)


def gather_low(cur):
    return [swap_dp(cur, k) for k in range(1, digits_of(lax.axis_size("dp"))[0][1])]


def rows_kernel(start, mine_ref, *refs):
    sources, out_ref = refs[:-1], refs[-1]
    high, _, _, columns = out_ref.shape
    mine = mine_ref[0]
    here = pl.ds(start, columns)
    for i in range(high):
        for k, source in enumerate(sources[:3]):
            out_ref[i, mine ^ k] = source[i, :, here]
        far = sources[3 + i * (len(sources) - 3) // high]
        out_ref[i, mine ^ 3] = far[i % far.shape[0]]


def all_rows(sources, start, columns):
    high, rows, _ = sources[0].shape
    full = pl.pallas_call(
        functools.partial(rows_kernel, start),
        in_specs=[pl.BlockSpec(memory_space=pltpu.SMEM)]
        + [pl.BlockSpec(memory_space=pltpu.VMEM)] * len(sources),
        out_specs=pl.BlockSpec(memory_space=pltpu.VMEM),
        out_shape=jax.ShapeDtypeStruct((high, 4, rows, columns), BF),
        cost_estimate=FREE,
        compiler_params=pltpu.CompilerParams(vmem_limit_bytes=ROWS_VMEM),
        name="all_rows",
    )(digit(1, 4).astype(jnp.int32).reshape(1), *sources)
    return full.reshape(-1, columns)


def split_low(x):
    n = lax.axis_size("dp")
    radix = digits_of(n)[0][1]
    view = x.reshape(n // radix, radix, x.shape[0] // n, x.shape[1])
    mine = digit(1, radix)
    return [lax.dynamic_index_in_dim(view, mine ^ k, 1, keepdims=False) for k in range(radix)]


def total_of(parts):
    total = parts[0].astype(F32)
    for part in parts[1:]:
        total = total + part.astype(F32)
    return total


def scatter_operands(x):
    mine, one, two, across = split_low(x)
    half = mine.shape[0] // 2
    return (mine, one, two), (across[:half], across[half:])


def scatter_low_across(operands):
    return swap_dp(operands[0], 1), swap_dp(operands[1], 2)


def near_operands(parts, across):
    mine, one, two = parts
    half = mine.shape[0] // 2
    one = jnp.concatenate([one[:half], total_of([one[half:], across[1]]).astype(BF)], axis=0)
    two = jnp.concatenate([total_of([two[:half], across[0]]).astype(BF), two[half:]], axis=0)
    return mine, one, two


def scatter_low_near(operands):
    mine, one, two = operands
    return mine, swap_dp(one, 1), swap_dp(two, 2)


def high_operands(cur, index):
    stride, radix = digits_of(lax.axis_size("dp"))[1 + index]
    view = cur.reshape((-1, radix) + cur.shape[1:])
    mine = digit(stride, radix)
    return [
        lax.dynamic_index_in_dim(view, mine ^ k, 1, keepdims=False).astype((F32, BF)[k])
        for k in range(radix)
    ]


def scatter_high_step(operands, index):
    stride, _ = digits_of(lax.axis_size("dp"))[1 + index]
    return operands[0] + swap_dp(operands[1], stride).astype(F32)


def scatter_high_last(cur, index):
    digits = digits_of(lax.axis_size("dp"))[1:]
    for i in range(index, len(digits) - 1):
        cur = scatter_high_step(high_operands(cur, i), i)
    kept, sent = high_operands(cur, len(digits) - 1)
    return kept[0], swap_dp(sent, digits[-1][0])[0]


def sum_low(x):
    return total_of([x] + [swap_dp(x, k) for k in range(1, digits_of(lax.axis_size("dp"))[0][1])])


def sum_high(x):
    strides = [stride for stride, _ in digits_of(lax.axis_size("dp"))[1:]]
    for pair in (strides[i : i + 2] for i in range(0, len(strides), 2)):
        steps = pair + ([sum(pair)] if len(pair) > 1 else [])
        x = total_of([x] + [swap_dp(x, step) for step in steps])
    return x


def swap_pieces(x, count):
    rows = x.shape[0] // count
    return [swap_core(x[i * rows : (i + 1) * rows]) for i in range(count)]


def dot(a, b, ca, cb):
    return lax.dot_general(a, b, (((ca,), (cb,)), ((), ())), preferred_element_type=F32)


def attend_kernel(qkv_ref, *refs):
    out_ref, lse_ref = refs[-2:]
    queries = qkv_ref[:, :PAIR]
    keys_all = qkv_ref[:, PAIR : 2 * PAIR] * jnp.asarray(HEAD**-0.5, BF)
    values = qkv_ref[:, 2 * PAIR :]
    first = lax.broadcasted_iota(jnp.int32, (1, PAIR), 1) < HEAD
    outs, logs = [], []
    for own in (first, ~first):
        here = jnp.where(own, queries, jnp.zeros_like(queries))
        scores = dot(keys_all, here, 1, 1)
        row_max = jnp.max(scores, axis=0, keepdims=True)
        powers = jnp.exp(scores - row_max)
        summed = jnp.sum(powers, axis=0, keepdims=True)
        probs = (powers * (1.0 / summed)).astype(BF)
        outs.append(dot(values, probs, 0, 0))
        logs.append(row_max + jnp.log(summed))
    both = jnp.concatenate([outs[0][:HEAD], outs[1][HEAD:]], axis=0)
    out_ref[...] = both.T.astype(BF)
    lse_ref[...] = jnp.concatenate(logs, axis=0)[None]


def attend(qkv, start, count, kept=()):
    n, width = qkv.shape
    pairs = width // (3 * PAIR)
    return pl.pallas_call(
        attend_kernel,
        grid=(count,),
        in_specs=[pl.BlockSpec((n, 3 * PAIR), lambda p: (0, p + start))]
        + [pl.BlockSpec(memory_space=pl.ANY)] * len(kept),
        out_specs=[
            pl.BlockSpec((n, PAIR), lambda p: (0, p + start)),
            pl.BlockSpec((1, 2, n), lambda p: (p + start, 0, 0)),
        ],
        out_shape=[
            jax.ShapeDtypeStruct((n, pairs * PAIR), BF),
            jax.ShapeDtypeStruct((pairs, 2, n), F32),
        ],
        input_output_aliases={1 + i: i for i in range(len(kept))},
        compiler_params=pltpu.CompilerParams(vmem_limit_bytes=ATTEND_VMEM),
        cost_estimate=FREE,
        name="attend",
    )(qkv, *kept)


def attend_back_kernel(qkv_ref, lse_ref, grad_ref, *refs):
    out_ref, sum_ref = refs[-2:]
    factor = jnp.asarray(HEAD**-0.5, BF)
    queries = qkv_ref[:, :PAIR]
    keys_small = qkv_ref[:, PAIR : 2 * PAIR] * factor
    values = qkv_ref[:, 2 * PAIR :]
    grad = grad_ref[...]
    first = lax.broadcasted_iota(jnp.int32, (1, PAIR), 1) < HEAD
    parts = []
    for own in (first, ~first):
        q_here = jnp.where(own, queries, jnp.zeros_like(queries))
        g_here = jnp.where(own, grad, jnp.zeros_like(grad))
        parts.append((q_here, g_here, dot(keys_small, q_here, 1, 1), dot(values, g_here, 1, 1)))
    d_q, d_k, d_v = [], [], []
    for head, (q_here, g_here, scores, d_probs) in enumerate(parts):
        probs = jnp.exp(scores - lse_ref[0, head : head + 1, :])
        product = probs * d_probs
        row_sum = jnp.sum(product, axis=0, keepdims=True)
        d_scores = (product - probs * row_sum).astype(BF)
        d_v.append(dot(probs.astype(BF), g_here, 1, 0))
        d_k.append(dot(d_scores, q_here, 1, 0))
        d_q.append(dot(keys_small, d_scores, 0, 0))
    queries_t = jnp.concatenate([d_q[0][:HEAD], d_q[1][HEAD:]], axis=0)
    d_queries = queries_t.T.astype(BF)
    d_keys = ((d_k[0] + d_k[1]) * HEAD**-0.5).astype(BF)
    d_values = (d_v[0] + d_v[1]).astype(BF)
    for i, x in enumerate((d_queries, d_keys, d_values)):
        out_ref[:, i * PAIR : (i + 1) * PAIR] = x
        sum_ref[0, :, i * PAIR : (i + 1) * PAIR] = jnp.sum(x.astype(F32), axis=0, keepdims=True)


def attend_back(qkv, lse, grad, start, count, kept=()):
    n, width = qkv.shape
    pairs = width // (3 * PAIR)
    return pl.pallas_call(
        attend_back_kernel,
        grid=(count,),
        in_specs=[
            pl.BlockSpec((n, 3 * PAIR), lambda p: (0, p + start)),
            pl.BlockSpec((1, 2, n), lambda p: (p + start, 0, 0)),
            pl.BlockSpec((n, PAIR), lambda p: (0, p + start)),
        ]
        + [pl.BlockSpec(memory_space=pl.ANY)] * len(kept),
        out_specs=[
            pl.BlockSpec((n, 3 * PAIR), lambda p: (0, p + start)),
            pl.BlockSpec((1, 1, 3 * PAIR), lambda p: (p + start, 0, 0)),
        ],
        out_shape=[
            jax.ShapeDtypeStruct((n, width), BF),
            jax.ShapeDtypeStruct((pairs, 1, 3 * PAIR), F32),
        ],
        input_output_aliases={3 + i: i for i in range(len(kept))},
        compiler_params=pltpu.CompilerParams(vmem_limit_bytes=BACK_VMEM),
        cost_estimate=FREE,
        name="attend_back",
    )(qkv, lse, grad, *kept)


def rows_call(kernel, out_shape, name):
    return pl.pallas_call(
        kernel,
        out_shape=out_shape,
        cost_estimate=FREE,
        compiler_params=pltpu.CompilerParams(vmem_limit_bytes=ROWS_VMEM),
        name=name,
    )


def row_blocks(rows):
    return [pl.ds(i, ROW_BLOCK) for i in range(0, rows, ROW_BLOCK)]


def pack_kernel(qkv_ref, out_ref, gains_ref, shifts_ref, packed_ref, small_ref):
    rows, wide = out_ref.shape
    for pair in range(wide // PAIR):
        for i in range(3):
            start = (3 * pair + i) * PAIR
            packed_ref[:, start : start + PAIR] = qkv_ref[i, :, pair * PAIR : (pair + 1) * PAIR]
    packed_ref[:, 3 * wide : 4 * wide] = out_ref[...]
    small_ref[...] = jnp.zeros_like(small_ref)
    small_ref[0:2, :rows] = gains_ref[...].astype(F32)
    small_ref[2:6, :rows] = shifts_ref[...].astype(F32)
    packed_ref[:, 4 * wide :] = jnp.zeros_like(packed_ref[:, 4 * wide :])
    packed_ref[:, 4 * wide : 4 * wide + 8] = small_ref[...].T[:rows].astype(BF)


def pack(qkv_weight, out_weight, gains, shifts):
    rows, wide = out_weight.shape
    args = (qkv_weight, out_weight, gains, shifts)
    shape = (rows, 4 * wide + PAIR)
    return pl.pallas_call(
        pack_kernel,
        out_shape=jax.ShapeDtypeStruct(shape, BF),
        scratch_shapes=[pltpu.VMEM((8, PAIR), F32)],
        cost_estimate=FREE,
        compiler_params=pltpu.CompilerParams(vmem_limit_bytes=4 * 2**20),
        name="pack",
    )(*args)


def finish_qkv_kernel(kept_ref, got_ref, out_ref):
    total = kept_ref[...] + got_ref[...].astype(F32)
    for pair in range(out_ref.shape[2] // PAIR):
        for i in range(3):
            start = (3 * pair + i) * PAIR
            out_ref[i, :, pair * PAIR : (pair + 1) * PAIR] = total[:, start : start + PAIR]


def finish_ff_kernel(kept_ref, got_ref, *out_refs):
    total = kept_ref[...] + got_ref[...].astype(F32)
    start = 0
    for out_ref in out_refs:
        columns = out_ref.shape[1]
        out_ref[...] = total[:, start : start + columns]
        start += columns


def finish(kernel, kept, got, shapes, name):
    return pl.pallas_call(
        kernel,
        out_shape=[jax.ShapeDtypeStruct(x, F32) for x in shapes],
        cost_estimate=FREE,
        compiler_params=pltpu.CompilerParams(vmem_limit_bytes=8 * 2**20),
        name=name,
    )(kept, got)


def join_kernel(mine_ref, other_ref, out_ref):
    half = mine_ref.shape[0]
    out_ref[:half] = mine_ref[...]
    out_ref[half:] = other_ref[...]


def join(mine, other):
    rows, columns = mine.shape
    shape = jax.ShapeDtypeStruct((2 * rows, columns), mine.dtype)
    return rows_call(join_kernel, shape, "join")(mine, other)


def standardized(x):
    center = x - jnp.mean(x, axis=-1, keepdims=True)
    inv_std = lax.rsqrt(jnp.mean(center * center, axis=-1, keepdims=True) + EPS)
    return center * inv_std, inv_std


def project_kernel(x_ref, weight_ref, bias_ref, normed_ref, qkv_ref, vectors_ref):
    width = qkv_ref.shape[1]
    small = weight_ref.shape[1] - PAIR
    vectors = weight_ref[:, small:].astype(F32).T[:8]
    vectors_ref[...] = vectors
    for here in row_blocks(x_ref.shape[0]):
        unit, _ = standardized(x_ref[here].astype(F32))
        normed = (unit * vectors[0:1] + vectors[2:3]).astype(BF)
        normed_ref[here] = normed
        qkv_ref[here] = (dot(normed, weight_ref[:, :width], 1, 0) + bias_ref[...]).astype(BF)


def project(x, first_full, bias, width):
    rows, columns = x.shape
    shapes = [
        jax.ShapeDtypeStruct((rows, columns), BF),
        jax.ShapeDtypeStruct((rows, width), BF),
        jax.ShapeDtypeStruct((8, columns), F32),
    ]
    return rows_call(project_kernel, shapes, "project")(x, first_full, bias)


def blocks_of(x_ref, others):
    rows = x_ref.shape[0] // PIECES
    found = []
    for i in range(0, x_ref.shape[0], ROW_BLOCK):
        other = others[(i // rows + PIECES // 2) % PIECES]
        found.append((pl.ds(i, ROW_BLOCK), other, pl.ds(i % rows, ROW_BLOCK)))
    return found


def mid_norm_kernel(x_ref, mine_ref, vectors_ref, *refs):
    others, (hidden_ref, normed_ref) = refs[:PIECES], refs[PIECES:]
    for here, other_ref, there in blocks_of(x_ref, others):
        branch = mine_ref[here].astype(F32) + other_ref[there].astype(F32)
        hidden = x_ref[here].astype(F32) + (branch + vectors_ref[3:4])
        hidden_ref[here] = hidden
        unit, _ = standardized(hidden)
        normed_ref[here] = (unit * vectors_ref[1:2] + vectors_ref[4:5]).astype(BF)


def mid_norm(x, mine, others, vectors):
    shapes = [jax.ShapeDtypeStruct(x.shape, t) for t in (F32, BF)]
    return rows_call(mid_norm_kernel, shapes, "mid_norm")(x, mine, vectors, *others)


def norm_back(unit, inv_std, gain, grad):
    scaled = grad * gain
    return inv_std * (
        scaled
        - jnp.mean(scaled, axis=-1, keepdims=True)
        - unit * jnp.mean(scaled * unit, axis=-1, keepdims=True)
    )


def total_rows(x):
    return jnp.sum(x, axis=0, keepdims=True)


def mid_norm_back_kernel(mine_ref, hidden_ref, d_out_ref, vectors_ref, *refs):
    others, (branch_ref, d_hidden_ref, sums_ref) = refs[:PIECES], refs[PIECES:]
    sums = [jnp.zeros((1, hidden_ref.shape[1]), F32)] * 4
    for here, other_ref, there in blocks_of(hidden_ref, others):
        grad = mine_ref[here].astype(F32) + other_ref[there].astype(F32)
        unit, inv_std = standardized(hidden_ref[here])
        d_out = d_out_ref[here].astype(F32)
        d_hidden = d_out + norm_back(unit, inv_std, vectors_ref[1:2], grad)
        d_branch = d_hidden.astype(BF)
        branch_ref[here] = d_branch
        if here.start < d_hidden_ref.shape[0]:
            d_hidden_ref[here] = d_hidden
            terms = (grad * unit, d_branch.astype(F32), grad, d_out)
            sums = [a + total_rows(b) for a, b in zip(sums, terms)]
    sums_ref[...] = jnp.concatenate(sums, axis=0)


def mid_norm_back(mine, others, hidden, d_out, vectors):
    rows, columns = hidden.shape
    shapes = [
        jax.ShapeDtypeStruct((rows, columns), BF),
        jax.ShapeDtypeStruct((rows // 2, columns), F32),
        jax.ShapeDtypeStruct((4, columns), F32),
    ]
    return rows_call(mid_norm_back_kernel, shapes, "mid_norm_back")(
        mine, hidden, d_out, vectors, *others
    )


def first_norm_back_kernel(
    qkv_ref, weight_ref, x_ref, d_hidden_ref, vectors_ref, first_ref, second_ref, grad_ref, sums_ref
):
    sums = [jnp.zeros((1, x_ref.shape[1]), F32)] * 2
    width = qkv_ref.shape[1]
    for i, here in enumerate(row_blocks(x_ref.shape[0])):
        rows = first_ref.shape[0]
        other_ref = (first_ref, second_ref)[i * ROW_BLOCK // rows]
        other = other_ref[pl.ds(i * ROW_BLOCK % rows, ROW_BLOCK)].astype(F32)
        grad = dot(qkv_ref[here], weight_ref[:, :width], 1, 1) + other
        unit, inv_std = standardized(x_ref[here].astype(F32))
        grad_ref[here] = d_hidden_ref[here] + norm_back(unit, inv_std, vectors_ref[0:1], grad)
        sums = [a + total_rows(b) for a, b in zip(sums, (grad * unit, grad))]
    sums_ref[...] = jnp.concatenate(sums, axis=0)


def first_norm_back(d_qkv, first_full, others, x, d_hidden, vectors):
    rows, columns = x.shape
    shapes = [jax.ShapeDtypeStruct((n, columns), F32) for n in (rows, 2)]
    return rows_call(first_norm_back_kernel, shapes, "first_norm_back")(
        d_qkv, first_full, x, d_hidden, vectors, *others
    )


def mm(spec, a, b):
    return jnp.einsum(spec, a, b, preferred_element_type=F32)


def body(
    inputs,
    cotangent,
    qkv_weight,
    out_weight,
    fc1_weight,
    fc2_weight,
    norm_gains,
    shifts,
    qv_bias,
    fc1_bias,
):
    inputs = inputs[0]
    cotangent = cotangent[0]
    own = norm_gains.shape[1]
    wide = qkv_weight.shape[2]
    pairs = wide // PAIR

    first_own = pack(qkv_weight, out_weight.T, norm_gains, shifts)
    zeros = jnp.zeros((wide,), BF)
    qkv_bias = jnp.stack([qv_bias[0], zeros, qv_bias[1]]).reshape(3, pairs, PAIR)
    qkv_bias = qkv_bias.transpose(1, 0, 2).reshape(1, 3 * wide).astype(F32)
    half = inputs.shape[0]
    hidden_n = fc1_weight.shape[1]
    high = [stride for stride, _ in reversed(digits_of(lax.axis_size("dp"))[1:])]
    first_part = gather_high_at_once(first_own)
    inputs_other = swap_core(inputs)

    ff_own = jnp.concatenate([fc1_weight, fc2_weight.T], axis=1)

    first_part, inputs_other, ff_part = stage(first_part, inputs_other, ff_own[None])
    first_near = gather_near(first_part)
    inputs_all = join(inputs, inputs_other)
    for stride in high[:-1]:
        ff_part = place([ff_part, swap_dp(ff_part, stride)], stride)

    first_part, first_near, ff_part, inputs_all = stage(
        first_part, first_near, ff_part, inputs_all
    )
    first_far = gather_far(first_near)
    for stride in high[-1:]:
        ff_part = place([ff_part, swap_dp(ff_part, stride)], stride)

    first_part, first_near, first_far, ff_part = stage(first_part, first_near, first_far, ff_part)
    ff_near = gather_near(ff_part)
    cotangent_other = swap_core(after(cotangent, first_part))
    first_full = all_rows([first_part, *first_near, *first_far], 0, first_part.shape[2])
    out_full = first_full[:, 3 * wide : 4 * wide]
    normed_all, qkv, vectors = project(inputs_all, first_full, qkv_bias, 3 * wide)
    attended, log_sums = attend(qkv, 0, pairs)
    branch = mm("fe,de->fd", attended, out_full).astype(BF)
    branch_other = swap_pieces(branch, PIECES)
    hidden_all, normed_two_all = mid_norm(inputs_all, branch, branch_other, vectors)

    ff_part, ff_near, normed_two_all, cotangent_other = stage(
        ff_part, ff_near, normed_two_all, cotangent_other
    )
    mid_far = gather_far([x[:, :, :hidden_n] for x in ff_near])
    d_out_all = join(cotangent, cotangent_other)

    ff_part, ff_near, mid_far, d_out_all = stage(ff_part, ff_near, mid_far, d_out_all)
    end_far = gather_far([x[:, :, hidden_n:] for x in ff_near])
    mid_full = all_rows([ff_part, *ff_near, *mid_far], 0, hidden_n)
    hidden_pre = mm("fd,dh->fh", normed_two_all, mid_full) + fc1_bias.astype(F32)
    cdf = 0.5 * (1.0 + lax.erf(hidden_pre * 0.5**0.5))
    hidden_act = (hidden_pre * cdf).astype(BF)
    slope = cdf + hidden_pre * jnp.exp(-0.5 * hidden_pre * hidden_pre) * 0.3989422804014327
    hidden_act, slope, d_out_all, end_far = stage(hidden_act, slope.astype(BF), d_out_all, end_far)
    fc2_grad = mm("fd,fh->dh", d_out_all, hidden_act).astype(BF)
    fc2_parts, fc2_ops = scatter_operands(fc2_grad)

    ff_part, ff_near, end_far, d_out_all, fc2_ops = stage(
        ff_part, ff_near, end_far, d_out_all, fc2_ops
    )
    fc2_far = scatter_low_across(fc2_ops)
    end_full = all_rows([ff_part, *ff_near, *end_far], hidden_n, hidden_n)
    d_act = mm("fd,dh->fh", d_out_all, end_full)
    d_pre = (d_act * slope).astype(BF)
    fc1_bias_grad = jnp.sum(d_pre.astype(F32), axis=0, keepdims=True)
    d_two = mm("fh,dh->fd", d_pre, mid_full).astype(BF)

    d_two, fc2_far, d_pre = stage(d_two, fc2_far, d_pre)
    fc2_near = scatter_low_near(near_operands(fc2_parts, fc2_far))
    d_two_other = swap_pieces(d_two, PIECES)
    fc1_grad = mm("fd,fh->dh", normed_two_all, d_pre).astype(BF)
    d_branch_all, d_hidden, mid_sums = mid_norm_back(
        d_two, d_two_other, hidden_all, d_out_all, vectors
    )
    d_attended = mm("fd,de->fe", d_branch_all, out_full).astype(BF)
    out_grad = mm("fd,fe->de", d_branch_all, attended).astype(BF)
    mid_parts, mid_ops = scatter_operands(jnp.concatenate([fc1_grad, out_grad], axis=1))

    d_attended, mid_ops = stage(d_attended, mid_ops)
    mid_far = scatter_low_across(mid_ops)
    d_proj = attend_back(qkv, log_sums, d_attended, 0, pairs - 1)

    d_proj, mid_far, fc2_near = stage(d_proj, mid_far, fc2_near)
    mid_near = scatter_low_near(near_operands(mid_parts, mid_far))
    fc2_sum = scatter_high_step(high_operands(total_of(fc2_near), 0), 0)
    d_qkv, d_sums = attend_back(qkv, log_sums, d_attended, pairs - 1, 1, d_proj)
    qkv_grad = mm("fd,fe->de", normed_all, d_qkv).astype(BF)
    qkv_parts, qkv_ops = scatter_operands(qkv_grad)

    qkv_ops, d_qkv, fc2_sum, hidden_act = stage(qkv_ops, d_qkv, fc2_sum, hidden_act)
    qkv_far = scatter_low_across(qkv_ops)
    d_other = mm("fe,de->fd", d_qkv[half:], first_full[:, : 3 * wide]).astype(BF)
    mlp_other = mm("fh,dh->fd", hidden_act[half:], end_full).astype(BF)
    mlp_mine = mm("fh,dh->fd", hidden_act[:half], end_full)

    fc2_last = scatter_high_last(fc2_sum, 1)

    qkv_far, mid_near, d_other, mlp_other, mlp_mine, fc2_last = stage(
        qkv_far, mid_near, d_other, mlp_other, mlp_mine, fc2_last
    )
    qkv_near = scatter_low_near(near_operands(qkv_parts, qkv_far))
    mid_sum = scatter_high_step(high_operands(total_of(mid_near), 0), 0)
    d_other_got = swap_pieces(d_other, 2)
    input_grad, first_sums = first_norm_back(
        d_qkv, first_full, d_other_got, inputs, d_hidden, vectors
    )
    rows = jnp.concatenate([first_sums, mid_sums], axis=0)
    rows = rows + swap_core(rows)

    mid_sum, qkv_near, rows = stage(mid_sum, qkv_near, rows)
    width = rows.shape[1]
    flat = [rows, jnp.pad(d_sums[:, 0], ((0, 0), (0, width - 3 * PAIR)))]
    flat += [fc1_bias_grad[:, i : i + width] for i in range(0, fc1_bias_grad.shape[1], width)]
    flat = sum_low(jnp.concatenate(flat, axis=0))
    qkv_sum = scatter_high_step(high_operands(total_of(qkv_near), 0), 0)
    mlp_got = swap_core(mlp_other)
    mid_last = scatter_high_last(mid_sum, 1)

    qkv_sum, flat, mlp_got = stage(qkv_sum, flat, mlp_got)
    outputs = hidden_all[:half] + ((mlp_mine + mlp_got.astype(F32)) + vectors[5:6])
    flat = sum_high(flat)
    (qkv_out,) = finish(
        finish_qkv_kernel, *scatter_high_last(qkv_sum, 1), [qkv_weight.shape], "finish_qkv"
    )
    (fc2_out,) = finish(finish_ff_kernel, *fc2_last, [(own, hidden_n)], "finish_fc2")
    fc1_out, out_out = finish(
        finish_ff_kernel, *mid_last, [(own, n) for n in (hidden_n, wide)], "finish_mid"
    )
    rows = lax.dynamic_slice_in_dim(flat[:6], lax.axis_index("dp") * own, own, axis=1)
    sums = flat[6 : 6 + pairs, : 3 * PAIR].reshape(pairs, 3, PAIR)
    return (
        outputs[None],
        input_grad[None],
        qkv_out,
        out_out.T,
        fc1_out,
        fc2_out.T,
        rows[0:3:2],
        jnp.concatenate([rows[1:2], rows[3:6]], axis=0),
        sums[:, 0::2].transpose(1, 0, 2).reshape(2, wide),
        flat[6 + pairs :].reshape(-1),
    )


def solution(mesh):
    specs = (
        P("dp", "tensor", None),
        P("dp", "tensor", None),
        P(None, "dp", "tensor"),
        P("tensor", "dp"),
        P("dp", "tensor"),
        P("tensor", "dp"),
        P(None, "dp"),
        P(None, "dp"),
        P(None, "tensor"),
        P("tensor"),
    )
    return jax.shard_map(body, mesh=mesh, in_specs=specs, out_specs=specs, check_vma=False)
```

```python
import functools

import jax
import jax.numpy as jnp
from jax import lax
from jax.experimental import pallas as pl
from jax.experimental.pallas import tpu as pltpu
from jax.sharding import PartitionSpec as P

HEAD = 64
PAIR = 2 * HEAD
ATTEND_VMEM = 20 * 2**20
BACK_VMEM = 24 * 2**20
ROWS_VMEM = 16 * 2**20
PIECES = 2
ROW_BLOCK = 256
COLUMN_BLOCK = 384
FREE = pl.CostEstimate(flops=0, bytes_accessed=0, transcendentals=0)
EPS = 1e-05
BF = jnp.bfloat16
F32 = jnp.float32


def after(x, *others):
    return lax.optimization_barrier((x, others))[0]


def stage(*values):
    return lax.optimization_barrier(values)


def digits_of(n):
    low = 4 if n % 4 == 0 else n
    found, stride = [(1, low)], low
    while stride < n:
        found.append((stride, 2))
        stride *= 2
    return found


def swap_dp(x, step):
    n = lax.axis_size("dp")
    return lax.ppermute(x, "dp", [(i, i ^ step) for i in range(n)])


def swap_core(x):
    return lax.ppermute(x, "tensor", [(0, 1), (1, 0)])


def position(own):
    n = lax.axis_size("dp")
    me = lax.axis_index("dp")
    bits = [(me >> i) & 1 for i in range(n.bit_length() - 1)]
    low = me & 3
    return {
        "bits": [(me & (1 << i)) != 0 for i in range(len(bits))],
        "low": [low ^ k for k in range(4)],
        "high": [[bit, 1 - bit] for bit in bits[2:]],
        "digit": low.reshape(1),
        "start": (me * own).reshape(1),
    }


def pick(options, bits):
    for bit in bits:
        options = [jnp.where(bit, b, a) for a, b in zip(options[0::2], options[1::2])]
    return options[0]


def place(got, stride, at):
    radix = len(got)
    first = stride.bit_length() - 1
    bits = at["bits"][first : first + radix.bit_length() - 1]
    placed = [pick([got[i ^ m] for m in range(radix)], bits) for i in range(radix)]
    return jnp.stack(placed, axis=1).reshape((-1,) + got[0].shape[1:])


def gather_high_at_once(x, at):
    n = lax.axis_size("dp")
    low = digits_of(n)[0][1]
    stride = n // 4
    cur = place([x[None]] + [swap_dp(x[None], stride * k) for k in range(1, 4)], stride, at)
    while stride > low:
        stride //= 2
        cur = place([cur, swap_dp(cur, stride)], stride, at)
    return cur


def gather_near(cur):
    return swap_dp(cur, 1), swap_dp(cur, 2)


def gather_far(near):
    half = near[0].shape[0] // 2
    return swap_dp(near[0][:half], 2), swap_dp(near[1][half:], 1)


def gather_low(cur):
    return [swap_dp(cur, k) for k in range(1, digits_of(lax.axis_size("dp"))[0][1])]


def rows_kernel(start, mine_ref, *refs):
    sources, out_ref = refs[:-1], refs[-1]
    high, _, _, columns = out_ref.shape
    mine = mine_ref[0]
    here = pl.ds(start, columns)
    for i in range(high):
        for k, source in enumerate(sources[:3]):
            out_ref[i, mine ^ k] = source[i, :, here]
        far = sources[3 + i * (len(sources) - 3) // high]
        out_ref[i, mine ^ 3] = far[i % far.shape[0]]


def all_rows(sources, start, columns, at):
    high, rows, _ = sources[0].shape
    full = pl.pallas_call(
        functools.partial(rows_kernel, start),
        in_specs=[pl.BlockSpec(memory_space=pltpu.SMEM)]
        + [pl.BlockSpec(memory_space=pltpu.VMEM)] * len(sources),
        out_specs=pl.BlockSpec(memory_space=pltpu.VMEM),
        out_shape=jax.ShapeDtypeStruct((high, 4, rows, columns), BF),
        cost_estimate=FREE,
        compiler_params=pltpu.CompilerParams(vmem_limit_bytes=ROWS_VMEM),
        name="all_rows",
    )(at["digit"], *sources)
    return full.reshape(-1, columns)


def part_of(view, index, first=0, count=0):
    sizes = (count or view.shape[0], 1) + view.shape[2:]
    starts = [jnp.int32(first), index] + [jnp.int32(0)] * (view.ndim - 2)
    piece = lax.dynamic_slice(view, starts, sizes, allow_negative_indices=False)
    return piece.reshape(sizes[:1] + sizes[2:])


def total_of(parts):
    total = parts[0].astype(F32)
    for part in parts[1:]:
        total = total + part.astype(F32)
    return total


def scatter_operands(x, at):
    n = lax.axis_size("dp")
    view = x.reshape(n // 4, 4, x.shape[0] // n, x.shape[1])
    half = view.shape[0] // 2
    one, two, across = (
        [part_of(view, index, first, half) for first in (0, half)] for index in at["low"][1:]
    )
    return (part_of(view, at["low"][0]), one, two), across


def scatter_low_across(operands):
    return swap_dp(operands[0], 1), swap_dp(operands[1], 2)


def near_operands(parts, across):
    mine, one, two = parts
    one = jnp.concatenate([one[0], total_of([one[1], across[1]]).astype(BF)], axis=0)
    two = jnp.concatenate([total_of([two[0], across[0]]).astype(BF), two[1]], axis=0)
    return mine, one, two


def scatter_low_near(operands):
    mine, one, two = operands
    return mine, swap_dp(one, 1), swap_dp(two, 2)


def high_operands(cur, index, at):
    view = cur.reshape((-1, 2) + cur.shape[1:])
    kept, sent = (part_of(view, i) for i in at["high"][index])
    return kept, sent.astype(BF)


def scatter_high_step(operands, index):
    stride, _ = digits_of(lax.axis_size("dp"))[1 + index]
    return operands[0] + swap_dp(operands[1], stride).astype(F32)


def scatter_high_last(cur, index, at):
    digits = digits_of(lax.axis_size("dp"))[1:]
    for i in range(index, len(digits) - 1):
        cur = scatter_high_step(high_operands(cur, i, at), i)
    kept, sent = high_operands(cur, len(digits) - 1, at)
    return kept[0], swap_dp(sent, digits[-1][0])[0]


def sum_over(x, steps):
    for step in steps:
        x = x + swap_dp(x, step)
    return x


def swap_pieces(x, count):
    rows = x.shape[0] // count
    return [swap_core(x[i * rows : (i + 1) * rows]) for i in range(count)]


def dot(a, b, ca, cb):
    return lax.dot_general(a, b, (((ca,), (cb,)), ((), ())), preferred_element_type=F32)


def attend_kernel(qkv_ref, *refs):
    out_ref, lse_ref = refs[-2:]
    queries = qkv_ref[:, :PAIR]
    keys_all = qkv_ref[:, PAIR : 2 * PAIR] * jnp.asarray(HEAD**-0.5, BF)
    values = qkv_ref[:, 2 * PAIR :]
    first = lax.broadcasted_iota(jnp.int32, (1, PAIR), 1) < HEAD
    outs, logs = [], []
    for own in (first, ~first):
        here = jnp.where(own, queries, jnp.zeros_like(queries))
        scores = dot(keys_all, here, 1, 1)
        row_max = jnp.max(scores, axis=0, keepdims=True)
        powers = jnp.exp(scores - row_max)
        summed = jnp.sum(powers, axis=0, keepdims=True)
        probs = (powers * (1.0 / summed)).astype(BF)
        outs.append(dot(values, probs, 0, 0))
        logs.append(row_max + jnp.log(summed))
    both = jnp.concatenate([outs[0][:HEAD], outs[1][HEAD:]], axis=0)
    out_ref[...] = both.T.astype(BF)
    lse_ref[...] = jnp.concatenate(logs, axis=0)[None]


def attend(qkv, start, count, kept=()):
    n, width = qkv.shape
    pairs = width // (3 * PAIR)
    return pl.pallas_call(
        attend_kernel,
        grid=(count,),
        in_specs=[pl.BlockSpec((n, 3 * PAIR), lambda p: (0, p + start))]
        + [pl.BlockSpec(memory_space=pl.ANY)] * len(kept),
        out_specs=[
            pl.BlockSpec((n, PAIR), lambda p: (0, p + start)),
            pl.BlockSpec((1, 2, n), lambda p: (p + start, 0, 0)),
        ],
        out_shape=[
            jax.ShapeDtypeStruct((n, pairs * PAIR), BF),
            jax.ShapeDtypeStruct((pairs, 2, n), F32),
        ],
        input_output_aliases={1 + i: i for i in range(len(kept))},
        compiler_params=pltpu.CompilerParams(vmem_limit_bytes=ATTEND_VMEM),
        cost_estimate=FREE,
        name="attend",
    )(qkv, *kept)


def attend_back_kernel(qkv_ref, lse_ref, grad_ref, *refs):
    out_ref, sum_ref = refs[-2:]
    factor = jnp.asarray(HEAD**-0.5, BF)
    queries = qkv_ref[:, :PAIR]
    keys_small = qkv_ref[:, PAIR : 2 * PAIR] * factor
    values = qkv_ref[:, 2 * PAIR :]
    grad = grad_ref[...]
    first = lax.broadcasted_iota(jnp.int32, (1, PAIR), 1) < HEAD
    parts = []
    for own in (first, ~first):
        q_here = jnp.where(own, queries, jnp.zeros_like(queries))
        g_here = jnp.where(own, grad, jnp.zeros_like(grad))
        parts.append((q_here, g_here, dot(keys_small, q_here, 1, 1), dot(values, g_here, 1, 1)))
    d_q, d_k, d_v = [], [], []
    for head, (q_here, g_here, scores, d_probs) in enumerate(parts):
        probs = jnp.exp(scores - lse_ref[0, head : head + 1, :])
        product = probs * d_probs
        row_sum = jnp.sum(product, axis=0, keepdims=True)
        d_scores = (product - probs * row_sum).astype(BF)
        d_v.append(dot(probs.astype(BF), g_here, 1, 0))
        d_k.append(dot(d_scores, q_here, 1, 0))
        d_q.append(dot(keys_small, d_scores, 0, 0))
    queries_t = jnp.concatenate([d_q[0][:HEAD], d_q[1][HEAD:]], axis=0)
    d_queries = queries_t.T.astype(BF)
    d_keys = ((d_k[0] + d_k[1]) * HEAD**-0.5).astype(BF)
    d_values = (d_v[0] + d_v[1]).astype(BF)
    for i, x in enumerate((d_queries, d_keys, d_values)):
        out_ref[:, i * PAIR : (i + 1) * PAIR] = x
        sum_ref[0, :, i * PAIR : (i + 1) * PAIR] = jnp.sum(x.astype(F32), axis=0, keepdims=True)


def attend_back(qkv, lse, grad, start, count, kept=()):
    n, width = qkv.shape
    pairs = width // (3 * PAIR)
    return pl.pallas_call(
        attend_back_kernel,
        grid=(count,),
        in_specs=[
            pl.BlockSpec((n, 3 * PAIR), lambda p: (0, p + start)),
            pl.BlockSpec((1, 2, n), lambda p: (p + start, 0, 0)),
            pl.BlockSpec((n, PAIR), lambda p: (0, p + start)),
        ]
        + [pl.BlockSpec(memory_space=pl.ANY)] * len(kept),
        out_specs=[
            pl.BlockSpec((n, 3 * PAIR), lambda p: (0, p + start)),
            pl.BlockSpec((1, 1, 3 * PAIR), lambda p: (p + start, 0, 0)),
        ],
        out_shape=[
            jax.ShapeDtypeStruct((n, width), BF),
            jax.ShapeDtypeStruct((pairs, 1, 3 * PAIR), F32),
        ],
        input_output_aliases={3 + i: i for i in range(len(kept))},
        compiler_params=pltpu.CompilerParams(vmem_limit_bytes=BACK_VMEM),
        cost_estimate=FREE,
        name="attend_back",
    )(qkv, lse, grad, *kept)


def rows_call(kernel, out_shape, name):
    return pl.pallas_call(
        kernel,
        out_shape=out_shape,
        cost_estimate=FREE,
        compiler_params=pltpu.CompilerParams(vmem_limit_bytes=ROWS_VMEM),
        name=name,
    )


def each_block(rows, step):
    @pl.loop(0, rows // ROW_BLOCK)
    def _(i):
        step(pl.ds(pl.multiple_of(i * ROW_BLOCK, ROW_BLOCK), ROW_BLOCK))


def pack_kernel(qkv_ref, out_ref, gains_ref, shifts_ref, packed_ref, small_ref):
    rows, wide = out_ref.shape
    for pair in range(wide // PAIR):
        for i in range(3):
            start = (3 * pair + i) * PAIR
            packed_ref[:, start : start + PAIR] = qkv_ref[i, :, pair * PAIR : (pair + 1) * PAIR]
    packed_ref[:, 3 * wide : 4 * wide] = out_ref[...]
    small_ref[...] = jnp.zeros_like(small_ref)
    small_ref[0:2, :rows] = gains_ref[...].astype(F32)
    small_ref[2:6, :rows] = shifts_ref[...].astype(F32)
    packed_ref[:, 4 * wide :] = jnp.zeros_like(packed_ref[:, 4 * wide :])
    packed_ref[:, 4 * wide : 4 * wide + 8] = small_ref[...].T[:rows].astype(BF)


def pack(qkv_weight, out_weight, gains, shifts):
    rows, wide = out_weight.shape
    args = (qkv_weight, out_weight, gains, shifts)
    shape = (rows, 4 * wide + PAIR)
    return pl.pallas_call(
        pack_kernel,
        out_shape=jax.ShapeDtypeStruct(shape, BF),
        scratch_shapes=[pltpu.VMEM((8, PAIR), F32)],
        cost_estimate=FREE,
        compiler_params=pltpu.CompilerParams(vmem_limit_bytes=4 * 2**20),
        name="pack",
    )(*args)


def finish_qkv_kernel(kept_ref, got_ref, out_ref):
    total = kept_ref[...] + got_ref[...].astype(F32)
    for pair in range(out_ref.shape[2] // PAIR):
        for i in range(3):
            start = (3 * pair + i) * PAIR
            out_ref[i, :, pair * PAIR : (pair + 1) * PAIR] = total[:, start : start + PAIR]


def finish_ff_kernel(kept_ref, got_ref, *out_refs):
    total = kept_ref[...] + got_ref[...].astype(F32)
    start = 0
    for out_ref in out_refs:
        columns = out_ref.shape[1]
        out_ref[...] = total[:, start : start + columns]
        start += columns


def finish_sums_kernel(kept_ref, got_ref, start_ref, gains_ref, shifts_ref, qv_ref, bias_ref):
    own = gains_ref.shape[1]
    total = kept_ref[...] + got_ref[...]
    columns = total.shape[1]
    rows = pltpu.roll(total[:8], columns - start_ref[0], 1)[:, :own]
    gains_ref[...] = jnp.concatenate([rows[0:1], rows[2:3]], axis=0)
    shifts_ref[...] = jnp.concatenate([rows[1:2], rows[3:6]], axis=0)
    pairs = qv_ref.shape[1] // PAIR
    for pair in range(pairs):
        for i in range(2):
            here = slice(2 * i * PAIR, (2 * i + 1) * PAIR)
            qv_ref[i : i + 1, pair * PAIR : (pair + 1) * PAIR] = total[6 + pair : 7 + pair, here]
    bias_ref[...] = total[6 + pairs :]


def finish_sums(kept, got, start, shapes):
    return pl.pallas_call(
        finish_sums_kernel,
        in_specs=[pl.BlockSpec(memory_space=pltpu.VMEM)] * 2
        + [pl.BlockSpec(memory_space=pltpu.SMEM)],
        out_specs=[pl.BlockSpec(memory_space=pltpu.VMEM)] * 4,
        out_shape=[jax.ShapeDtypeStruct(x, F32) for x in shapes],
        cost_estimate=FREE,
        compiler_params=pltpu.CompilerParams(vmem_limit_bytes=4 * 2**20),
        name="finish_sums",
    )(kept, got, start)


def finish(kernel, kept, got, shapes, name):
    return pl.pallas_call(
        kernel,
        out_shape=[jax.ShapeDtypeStruct(x, F32) for x in shapes],
        cost_estimate=FREE,
        compiler_params=pltpu.CompilerParams(vmem_limit_bytes=8 * 2**20),
        name=name,
    )(kept, got)


def join_kernel(mine_ref, other_ref, out_ref):
    half = mine_ref.shape[0]
    out_ref[:half] = mine_ref[...]
    out_ref[half:] = other_ref[...]


def join(mine, other):
    rows, columns = mine.shape
    shape = jax.ShapeDtypeStruct((2 * rows, columns), mine.dtype)
    return rows_call(join_kernel, shape, "join")(mine, other)


def standardized(x):
    center = x - jnp.mean(x, axis=-1, keepdims=True)
    inv_std = lax.rsqrt(jnp.mean(center * center, axis=-1, keepdims=True) + EPS)
    return center * inv_std, inv_std


def project_kernel(x_ref, weight_ref, bias_ref, normed_ref, qkv_ref, vectors_ref):
    width = qkv_ref.shape[1]
    small = weight_ref.shape[1] - PAIR
    vectors = weight_ref[:, small:].astype(F32).T[:8]
    vectors_ref[...] = vectors

    def step(here):
        unit, _ = standardized(x_ref[here].astype(F32))
        normed = (unit * vectors_ref[0:1] + vectors_ref[2:3]).astype(BF)
        normed_ref[here] = normed
        qkv_ref[here] = (dot(normed, weight_ref[:, :width], 1, 0) + bias_ref[...]).astype(BF)

    for i in range(0, x_ref.shape[0], ROW_BLOCK):
        step(pl.ds(i, ROW_BLOCK))


def project(x, first_full, bias, width):
    rows, columns = x.shape
    shapes = [
        jax.ShapeDtypeStruct((rows, columns), BF),
        jax.ShapeDtypeStruct((rows, width), BF),
        jax.ShapeDtypeStruct((8, columns), F32),
    ]
    return rows_call(project_kernel, shapes, "project")(x, first_full, bias)


def halves_of(refs, others):
    half = others[0].shape[0]
    return [
        ([ref.at[pl.ds(i * half, half)] for ref in refs], others[1 - i]) for i in range(PIECES)
    ]


def mid_norm_kernel(x_ref, mine_ref, vectors_ref, *refs):
    others, (hidden_ref, normed_ref) = refs[:PIECES], refs[PIECES:]
    for refs, other_ref in halves_of((x_ref, mine_ref, hidden_ref, normed_ref), others):
        frames, mine, hidden_half, normed_half = refs

        def step(here):
            branch = mine[here].astype(F32) + other_ref[here].astype(F32)
            hidden = frames[here].astype(F32) + (branch + vectors_ref[3:4])
            hidden_half[here] = hidden
            unit, _ = standardized(hidden)
            normed_half[here] = (unit * vectors_ref[1:2] + vectors_ref[4:5]).astype(BF)

        each_block(other_ref.shape[0], step)


def mid_norm(x, mine, others, vectors):
    shapes = [jax.ShapeDtypeStruct(x.shape, t) for t in (F32, BF)]
    return rows_call(mid_norm_kernel, shapes, "mid_norm")(x, mine, vectors, *others)


def act_back_kernel(d_out_ref, weight_ref, slope_ref, d_pre_ref, sums_ref):
    @pl.loop(0, d_pre_ref.shape[1] // COLUMN_BLOCK)
    def _(i):
        here = pl.ds(pl.multiple_of(i * COLUMN_BLOCK, COLUMN_BLOCK), COLUMN_BLOCK)
        d_act = dot(d_out_ref[...], weight_ref[:, here], 1, 0)
        d_pre = (d_act * slope_ref[:, here].astype(F32)).astype(BF)
        d_pre_ref[:, here] = d_pre
        sums_ref[:, here] = total_rows(d_pre.astype(F32))


def act_back(d_out, weight, slope):
    shapes = [jax.ShapeDtypeStruct(slope.shape, BF), jax.ShapeDtypeStruct((1, slope.shape[1]), F32)]
    return rows_call(act_back_kernel, shapes, "act_back")(d_out, weight, slope)


def norm_back(unit, inv_std, gain, grad):
    scaled = grad * gain
    return inv_std * (
        scaled
        - jnp.mean(scaled, axis=-1, keepdims=True)
        - unit * jnp.mean(scaled * unit, axis=-1, keepdims=True)
    )


def total_rows(x):
    return jnp.sum(x, axis=0, keepdims=True)


def mid_norm_back_kernel(mine_ref, hidden_ref, d_out_ref, vectors_ref, *refs):
    others, (branch_ref, d_hidden_ref, sums_ref) = refs[:PIECES], refs[PIECES:]
    sums_ref[...] = jnp.zeros_like(sums_ref)
    halves = halves_of((mine_ref, hidden_ref, d_out_ref, branch_ref), others)
    for i, (refs, other_ref) in enumerate(halves):
        mine, hidden, d_outs, branch = refs

        def step(here):
            grad = mine[here].astype(F32) + other_ref[here].astype(F32)
            unit, inv_std = standardized(hidden[here])
            d_out = d_outs[here].astype(F32)
            d_hidden = d_out + norm_back(unit, inv_std, vectors_ref[1:2], grad)
            d_branch = d_hidden.astype(BF)
            branch[here] = d_branch
            if i == 0:
                d_hidden_ref[here] = d_hidden
                terms = (grad * unit, d_branch.astype(F32), grad, d_out)
                sums_ref[...] += jnp.concatenate([total_rows(x) for x in terms], axis=0)

        each_block(other_ref.shape[0], step)


def mid_norm_back(mine, others, hidden, d_out, vectors):
    rows, columns = hidden.shape
    shapes = [
        jax.ShapeDtypeStruct((rows, columns), BF),
        jax.ShapeDtypeStruct((rows // 2, columns), F32),
        jax.ShapeDtypeStruct((4, columns), F32),
    ]
    return rows_call(mid_norm_back_kernel, shapes, "mid_norm_back")(
        mine, hidden, d_out, vectors, *others
    )


def first_norm_back_kernel(
    qkv_ref, weight_ref, x_ref, d_hidden_ref, vectors_ref, first_ref, second_ref, grad_ref, sums_ref
):
    sums = [jnp.zeros((1, x_ref.shape[1]), F32)] * 2
    width = qkv_ref.shape[1]
    rows = first_ref.shape[0]
    for i in range(x_ref.shape[0] // ROW_BLOCK):
        here = pl.ds(i * ROW_BLOCK, ROW_BLOCK)
        other_ref = (first_ref, second_ref)[i * ROW_BLOCK // rows]
        other = other_ref[pl.ds(i * ROW_BLOCK % rows, ROW_BLOCK)].astype(F32)
        grad = dot(qkv_ref[here], weight_ref[:, :width], 1, 1) + other
        unit, inv_std = standardized(x_ref[here].astype(F32))
        grad_ref[here] = d_hidden_ref[here] + norm_back(unit, inv_std, vectors_ref[0:1], grad)
        sums = [a + total_rows(b) for a, b in zip(sums, (grad * unit, grad))]
    sums_ref[...] = jnp.concatenate(sums, axis=0)


def first_norm_back(d_qkv, first_full, others, x, d_hidden, vectors):
    rows, columns = x.shape
    shapes = [jax.ShapeDtypeStruct((n, columns), F32) for n in (rows, 2)]
    return rows_call(first_norm_back_kernel, shapes, "first_norm_back")(
        d_qkv, first_full, x, d_hidden, vectors, *others
    )


def mm(spec, a, b):
    return jnp.einsum(spec, a, b, preferred_element_type=F32)


def body(
    inputs,
    cotangent,
    qkv_weight,
    out_weight,
    fc1_weight,
    fc2_weight,
    norm_gains,
    shifts,
    qv_bias,
    fc1_bias,
):
    inputs = inputs[0]
    cotangent = cotangent[0]
    own = norm_gains.shape[1]
    wide = qkv_weight.shape[2]
    pairs = wide // PAIR

    first_own = pack(qkv_weight, out_weight.T, norm_gains, shifts)
    at = position(own)
    zeros = jnp.zeros((wide,), BF)
    qkv_bias = jnp.stack([qv_bias[0], zeros, qv_bias[1]]).reshape(3, pairs, PAIR)
    qkv_bias = qkv_bias.transpose(1, 0, 2).reshape(1, 3 * wide).astype(F32)
    half = inputs.shape[0]
    hidden_n = fc1_weight.shape[1]
    high = [stride for stride, _ in reversed(digits_of(lax.axis_size("dp"))[1:])]
    first_own, at, qkv_bias = stage(first_own, at, qkv_bias)
    first_part = gather_high_at_once(first_own, at)
    inputs_other = swap_core(inputs)

    ff_own = jnp.concatenate([fc1_weight, fc2_weight.T], axis=1)

    first_part, inputs_other, ff_part = stage(first_part, inputs_other, ff_own[None])
    first_near = gather_near(first_part)
    inputs_all = join(inputs, inputs_other)
    for stride in high[:-1]:
        ff_part = place([ff_part, swap_dp(ff_part, stride)], stride, at)

    first_part, first_near, ff_part, inputs_all = stage(
        first_part, first_near, ff_part, inputs_all
    )
    first_far = gather_far(first_near)
    for stride in high[-1:]:
        ff_part = place([ff_part, swap_dp(ff_part, stride)], stride, at)

    first_part, first_near, first_far, ff_part = stage(first_part, first_near, first_far, ff_part)
    ff_near = gather_near(ff_part)
    cotangent_other = swap_core(after(cotangent, first_part))
    first_full = all_rows([first_part, *first_near, *first_far], 0, first_part.shape[2], at)
    out_full = first_full[:, 3 * wide : 4 * wide]
    normed_all, qkv, vectors = project(inputs_all, first_full, qkv_bias, 3 * wide)
    attended, log_sums = attend(qkv, 0, pairs)
    branch = mm("fe,de->fd", attended, out_full).astype(BF)
    branch_other = swap_pieces(branch, PIECES)
    hidden_all, normed_two_all = mid_norm(inputs_all, branch, branch_other, vectors)

    ff_part, ff_near, normed_two_all, cotangent_other = stage(
        ff_part, ff_near, normed_two_all, cotangent_other
    )
    mid_far = gather_far([x[:, :, :hidden_n] for x in ff_near])
    d_out_all = join(cotangent, cotangent_other)

    ff_part, ff_near, mid_far, d_out_all = stage(ff_part, ff_near, mid_far, d_out_all)
    end_far = gather_far([x[:, :, hidden_n:] for x in ff_near])
    mid_full = all_rows([ff_part, *ff_near, *mid_far], 0, hidden_n, at)
    hidden_pre = mm("fd,dh->fh", normed_two_all, mid_full) + fc1_bias.astype(F32)
    cdf = 0.5 * (1.0 + lax.erf(hidden_pre * 0.5**0.5))
    hidden_act = (hidden_pre * cdf).astype(BF)
    slope = cdf + hidden_pre * jnp.exp(-0.5 * hidden_pre * hidden_pre) * 0.3989422804014327
    hidden_act, slope, d_out_all, end_far = stage(hidden_act, slope.astype(BF), d_out_all, end_far)
    fc2_grad = mm("fd,fh->dh", d_out_all, hidden_act).astype(BF)
    fc2_parts, fc2_ops = scatter_operands(fc2_grad, at)

    ff_part, ff_near, end_far, d_out_all, fc2_ops = stage(
        ff_part, ff_near, end_far, d_out_all, fc2_ops
    )
    fc2_far = scatter_low_across(fc2_ops)
    end_full = all_rows([ff_part, *ff_near, *end_far], hidden_n, hidden_n, at)
    d_pre, fc1_bias_grad = act_back(d_out_all, end_full, slope)
    d_two = mm("fh,dh->fd", d_pre, mid_full).astype(BF)

    d_two, fc2_far, d_pre = stage(d_two, fc2_far, d_pre)
    fc2_near = scatter_low_near(near_operands(fc2_parts, fc2_far))
    d_two_other = swap_pieces(d_two, PIECES)
    fc1_grad = mm("fd,fh->dh", normed_two_all, d_pre).astype(BF)
    d_branch_all, d_hidden, mid_sums = mid_norm_back(
        d_two, d_two_other, hidden_all, d_out_all, vectors
    )
    d_attended = mm("fd,de->fe", d_branch_all, out_full).astype(BF)
    out_grad = mm("fd,fe->de", d_branch_all, attended).astype(BF)
    mid_parts, mid_ops = scatter_operands(jnp.concatenate([fc1_grad, out_grad], axis=1), at)

    d_attended, mid_ops = stage(d_attended, mid_ops)
    mid_far = scatter_low_across(mid_ops)
    d_proj = attend_back(qkv, log_sums, d_attended, 0, pairs - 1)

    d_proj, mid_far, fc2_near = stage(d_proj, mid_far, fc2_near)
    mid_near = scatter_low_near(near_operands(mid_parts, mid_far))
    fc2_sum = scatter_high_step(high_operands(total_of(fc2_near), 0, at), 0)
    d_qkv, d_sums = attend_back(qkv, log_sums, d_attended, pairs - 1, 1, d_proj)
    qkv_grad = mm("fd,fe->de", normed_all, d_qkv).astype(BF)
    qkv_parts, qkv_ops = scatter_operands(qkv_grad, at)

    qkv_ops, d_qkv, fc2_sum, hidden_act = stage(qkv_ops, d_qkv, fc2_sum, hidden_act)
    qkv_far = scatter_low_across(qkv_ops)
    d_other = mm("fe,de->fd", d_qkv[half:], first_full[:, : 3 * wide]).astype(BF)
    mlp_other = mm("fh,dh->fd", hidden_act[half:], end_full).astype(BF)
    mlp_mine = mm("fh,dh->fd", hidden_act[:half], end_full)

    fc2_last = scatter_high_last(fc2_sum, 1, at)

    qkv_far, mid_near, d_other, mlp_other, mlp_mine, fc2_last = stage(
        qkv_far, mid_near, d_other, mlp_other, mlp_mine, fc2_last
    )
    qkv_near = scatter_low_near(near_operands(qkv_parts, qkv_far))
    mid_sum = scatter_high_step(high_operands(total_of(mid_near), 0, at), 0)
    d_other_got = swap_pieces(d_other, 2)
    input_grad, first_sums = first_norm_back(
        d_qkv, first_full, d_other_got, inputs, d_hidden, vectors
    )
    rows = jnp.concatenate([first_sums, mid_sums], axis=0)
    rows = rows + swap_core(rows)

    mid_sum, qkv_near, rows = stage(mid_sum, qkv_near, rows)
    width = rows.shape[1]
    flat = [rows, jnp.pad(d_sums[:, 0], ((0, 0), (0, width - 3 * PAIR)))]
    flat += [fc1_bias_grad[:, i : i + width] for i in range(0, fc1_bias_grad.shape[1], width)]
    flat = sum_over(jnp.concatenate(flat, axis=0), [1, 2])
    qkv_sum = scatter_high_step(high_operands(total_of(qkv_near), 0, at), 0)
    mlp_got = swap_core(mlp_other)
    mid_last = scatter_high_last(mid_sum, 1, at)

    qkv_sum, flat, mlp_got = stage(qkv_sum, flat, mlp_got)
    outputs = hidden_all[:half] + ((mlp_mine + mlp_got.astype(F32)) + vectors[5:6])
    flat = sum_over(flat, high[:0:-1])
    gains_out, shifts_out, qv_out, bias_out = finish_sums(
        flat,
        swap_dp(flat, high[0]),
        at["start"],
        [norm_gains.shape, shifts.shape, qv_bias.shape, (flat.shape[0] - 6 - pairs, width)],
    )
    (qkv_out,) = finish(
        finish_qkv_kernel, *scatter_high_last(qkv_sum, 1, at), [qkv_weight.shape], "finish_qkv"
    )
    (fc2_out,) = finish(finish_ff_kernel, *fc2_last, [(own, hidden_n)], "finish_fc2")
    fc1_out, out_out = finish(
        finish_ff_kernel, *mid_last, [(own, n) for n in (hidden_n, wide)], "finish_mid"
    )
    return (
        outputs[None],
        input_grad[None],
        qkv_out,
        out_out.T,
        fc1_out,
        fc2_out.T,
        gains_out,
        shifts_out,
        qv_out,
        bias_out.reshape(-1),
    )


def solution(mesh):
    specs = (
        P("dp", "tensor", None),
        P("dp", "tensor", None),
        P(None, "dp", "tensor"),
        P("tensor", "dp"),
        P("dp", "tensor"),
        P("tensor", "dp"),
        P(None, "dp"),
        P(None, "dp"),
        P(None, "tensor"),
        P("tensor"),
    )
    return jax.shard_map(body, mesh=mesh, in_specs=specs, out_specs=specs, check_vma=False)
```

```python
import functools

import jax
import jax.numpy as jnp
from jax import lax
from jax.experimental import pallas as pl
from jax.experimental.pallas import tpu as pltpu
from jax.sharding import PartitionSpec as P

HEAD = 64
PAIR = 2 * HEAD
ATTEND_VMEM = 20 * 2**20
BACK_VMEM = 24 * 2**20
ROWS_VMEM = 16 * 2**20
PIECES = 2
ROW_BLOCK = 256
COLUMN_BLOCK = 384
FREE = pl.CostEstimate(flops=0, bytes_accessed=0, transcendentals=0)
EPS = 1e-05
BF = jnp.bfloat16
F32 = jnp.float32


def after(x, *others):
    return lax.optimization_barrier((x, others))[0]


def stage(*values):
    return lax.optimization_barrier(values)


def digits_of(n):
    low = 4 if n % 4 == 0 else n
    found, stride = [(1, low)], low
    while stride < n:
        found.append((stride, 2))
        stride *= 2
    return found


def swap_dp(x, step):
    n = lax.axis_size("dp")
    return lax.ppermute(x, "dp", [(i, i ^ step) for i in range(n)])


def swap_core(x):
    return lax.ppermute(x, "tensor", [(0, 1), (1, 0)])


def position(own):
    n = lax.axis_size("dp")
    me = lax.axis_index("dp")
    bits = [(me >> i) & 1 for i in range(n.bit_length() - 1)]
    low = me & 3
    return {
        "bits": [(me & (1 << i)) != 0 for i in range(len(bits))],
        "low": [low ^ k for k in range(4)],
        "high": [[bit, 1 - bit] for bit in bits[2:]],
        "digit": low.reshape(1),
        "start": (me * own).reshape(1),
    }


def pick(options, bits):
    for bit in bits:
        options = [jnp.where(bit, b, a) for a, b in zip(options[0::2], options[1::2])]
    return options[0]


def place(got, stride, at):
    radix = len(got)
    first = stride.bit_length() - 1
    bits = at["bits"][first : first + radix.bit_length() - 1]
    placed = [pick([got[i ^ m] for m in range(radix)], bits) for i in range(radix)]
    return jnp.stack(placed, axis=1).reshape((-1,) + got[0].shape[1:])


def gather_high_at_once(x, at):
    n = lax.axis_size("dp")
    low = digits_of(n)[0][1]
    stride = n // 4
    cur = place([x[None]] + [swap_dp(x[None], stride * k) for k in range(1, 4)], stride, at)
    while stride > low:
        stride //= 2
        cur = place([cur, swap_dp(cur, stride)], stride, at)
    return cur


def gather_near(cur):
    return swap_dp(cur, 1), swap_dp(cur, 2)


def gather_far(near):
    half = near[0].shape[0] // 2
    return swap_dp(near[0][:half], 2), swap_dp(near[1][half:], 1)


def gather_low(cur):
    return [swap_dp(cur, k) for k in range(1, digits_of(lax.axis_size("dp"))[0][1])]


def rows_kernel(start, mine_ref, *refs):
    sources, out_ref = refs[:-1], refs[-1]
    high, _, _, columns = out_ref.shape
    mine = mine_ref[0]
    here = pl.ds(start, columns)
    for i in range(high):
        for k, source in enumerate(sources[:3]):
            out_ref[i, mine ^ k] = source[i, :, here]
        far = sources[3 + i * (len(sources) - 3) // high]
        out_ref[i, mine ^ 3] = far[i % far.shape[0]]


def all_rows(sources, start, columns, at):
    high, rows, _ = sources[0].shape
    full = pl.pallas_call(
        functools.partial(rows_kernel, start),
        in_specs=[pl.BlockSpec(memory_space=pltpu.SMEM)]
        + [pl.BlockSpec(memory_space=pltpu.VMEM)] * len(sources),
        out_specs=pl.BlockSpec(memory_space=pltpu.VMEM),
        out_shape=jax.ShapeDtypeStruct((high, 4, rows, columns), BF),
        cost_estimate=FREE,
        compiler_params=pltpu.CompilerParams(vmem_limit_bytes=ROWS_VMEM),
        name="all_rows",
    )(at["digit"], *sources)
    return full.reshape(-1, columns)


def part_of(view, index, first=0, count=0):
    sizes = (count or view.shape[0], 1) + view.shape[2:]
    starts = [jnp.int32(first), index] + [jnp.int32(0)] * (view.ndim - 2)
    piece = lax.dynamic_slice(view, starts, sizes, allow_negative_indices=False)
    return piece.reshape(sizes[:1] + sizes[2:])


def total_of(parts):
    total = parts[0].astype(F32)
    for part in parts[1:]:
        total = total + part.astype(F32)
    return total


def scatter_operands(x, at):
    n = lax.axis_size("dp")
    view = x.reshape(n // 4, 4, x.shape[0] // n, x.shape[1])
    half = view.shape[0] // 2
    one, two, across = (
        [part_of(view, index, first, half) for first in (0, half)] for index in at["low"][1:]
    )
    return (part_of(view, at["low"][0]), one, two), across


def scatter_low_across(operands):
    return swap_dp(operands[0], 1), swap_dp(operands[1], 2)


def near_operands(parts, across):
    mine, one, two = parts
    one = jnp.concatenate([one[0], total_of([one[1], across[1]]).astype(BF)], axis=0)
    two = jnp.concatenate([total_of([two[0], across[0]]).astype(BF), two[1]], axis=0)
    return mine, one, two


def scatter_low_near(operands):
    mine, one, two = operands
    return mine, swap_dp(one, 1), swap_dp(two, 2)


def high_operands(cur, index, at):
    view = cur.reshape((-1, 2) + cur.shape[1:])
    kept, sent = (part_of(view, i) for i in at["high"][index])
    return kept, sent.astype(BF)


def scatter_high_step(operands, index):
    stride, _ = digits_of(lax.axis_size("dp"))[1 + index]
    return operands[0] + swap_dp(operands[1], stride).astype(F32)


def scatter_high_last(cur, index, at):
    digits = digits_of(lax.axis_size("dp"))[1:]
    for i in range(index, len(digits) - 1):
        cur = scatter_high_step(high_operands(cur, i, at), i)
    kept, sent = high_operands(cur, len(digits) - 1, at)
    return kept[0], swap_dp(sent, digits[-1][0])[0]


def sum_over(x, steps):
    for step in steps:
        x = x + swap_dp(x, step)
    return x


def swap_pieces(x, count):
    rows = x.shape[0] // count
    return [swap_core(x[i * rows : (i + 1) * rows]) for i in range(count)]


def dot(a, b, ca, cb):
    return lax.dot_general(a, b, (((ca,), (cb,)), ((), ())), preferred_element_type=F32)


def attend_kernel(qkv_ref, *refs):
    out_ref, lse_ref = refs[-2:]
    queries = qkv_ref[:, :PAIR]
    keys_all = qkv_ref[:, PAIR : 2 * PAIR] * jnp.asarray(HEAD**-0.5, BF)
    values = qkv_ref[:, 2 * PAIR :]
    first = lax.broadcasted_iota(jnp.int32, (1, PAIR), 1) < HEAD
    outs, logs = [], []
    for own in (first, ~first):
        here = jnp.where(own, queries, jnp.zeros_like(queries))
        scores = dot(keys_all, here, 1, 1)
        row_max = jnp.max(scores, axis=0, keepdims=True)
        powers = jnp.exp(scores - row_max)
        summed = jnp.sum(powers, axis=0, keepdims=True)
        probs = (powers * (1.0 / summed)).astype(BF)
        outs.append(dot(values, probs, 0, 0))
        logs.append(row_max + jnp.log(summed))
    both = jnp.concatenate([outs[0][:HEAD], outs[1][HEAD:]], axis=0)
    out_ref[...] = both.T.astype(BF)
    lse_ref[...] = jnp.concatenate(logs, axis=0)[None]


def attend(qkv, start, count, kept=()):
    n, width = qkv.shape
    pairs = width // (3 * PAIR)
    return pl.pallas_call(
        attend_kernel,
        grid=(count,),
        in_specs=[pl.BlockSpec((n, 3 * PAIR), lambda p: (0, p + start))]
        + [pl.BlockSpec(memory_space=pl.ANY)] * len(kept),
        out_specs=[
            pl.BlockSpec((n, PAIR), lambda p: (0, p + start)),
            pl.BlockSpec((1, 2, n), lambda p: (p + start, 0, 0)),
        ],
        out_shape=[
            jax.ShapeDtypeStruct((n, pairs * PAIR), BF),
            jax.ShapeDtypeStruct((pairs, 2, n), F32),
        ],
        input_output_aliases={1 + i: i for i in range(len(kept))},
        compiler_params=pltpu.CompilerParams(vmem_limit_bytes=ATTEND_VMEM),
        cost_estimate=FREE,
        name="attend",
    )(qkv, *kept)


def attend_back_kernel(qkv_ref, lse_ref, grad_ref, *refs):
    out_ref, sum_ref = refs[-2:]
    factor = jnp.asarray(HEAD**-0.5, BF)
    queries = qkv_ref[:, :PAIR]
    keys_small = qkv_ref[:, PAIR : 2 * PAIR] * factor
    values = qkv_ref[:, 2 * PAIR :]
    grad = grad_ref[...]
    first = lax.broadcasted_iota(jnp.int32, (1, PAIR), 1) < HEAD
    parts = []
    for own in (first, ~first):
        q_here = jnp.where(own, queries, jnp.zeros_like(queries))
        g_here = jnp.where(own, grad, jnp.zeros_like(grad))
        parts.append((q_here, g_here, dot(keys_small, q_here, 1, 1), dot(values, g_here, 1, 1)))
    d_q, d_k, d_v = [], [], []
    for head, (q_here, g_here, scores, d_probs) in enumerate(parts):
        probs = jnp.exp(scores - lse_ref[0, head : head + 1, :])
        product = probs * d_probs
        row_sum = jnp.sum(product, axis=0, keepdims=True)
        d_scores = (product - probs * row_sum).astype(BF)
        d_v.append(dot(probs.astype(BF), g_here, 1, 0))
        d_k.append(dot(d_scores, q_here, 1, 0))
        d_q.append(dot(keys_small, d_scores, 0, 0))
    queries_t = jnp.concatenate([d_q[0][:HEAD], d_q[1][HEAD:]], axis=0)
    d_queries = queries_t.T.astype(BF)
    d_keys = ((d_k[0] + d_k[1]) * HEAD**-0.5).astype(BF)
    d_values = (d_v[0] + d_v[1]).astype(BF)
    for i, x in enumerate((d_queries, d_keys, d_values)):
        out_ref[:, i * PAIR : (i + 1) * PAIR] = x
        sum_ref[0, :, i * PAIR : (i + 1) * PAIR] = jnp.sum(x.astype(F32), axis=0, keepdims=True)


def attend_back(qkv, lse, grad, start, count, kept=()):
    n, width = qkv.shape
    pairs = width // (3 * PAIR)
    return pl.pallas_call(
        attend_back_kernel,
        grid=(count,),
        in_specs=[
            pl.BlockSpec((n, 3 * PAIR), lambda p: (0, p + start)),
            pl.BlockSpec((1, 2, n), lambda p: (p + start, 0, 0)),
            pl.BlockSpec((n, PAIR), lambda p: (0, p + start)),
        ]
        + [pl.BlockSpec(memory_space=pl.ANY)] * len(kept),
        out_specs=[
            pl.BlockSpec((n, 3 * PAIR), lambda p: (0, p + start)),
            pl.BlockSpec((1, 1, 3 * PAIR), lambda p: (p + start, 0, 0)),
        ],
        out_shape=[
            jax.ShapeDtypeStruct((n, width), BF),
            jax.ShapeDtypeStruct((pairs, 1, 3 * PAIR), F32),
        ],
        input_output_aliases={3 + i: i for i in range(len(kept))},
        compiler_params=pltpu.CompilerParams(vmem_limit_bytes=BACK_VMEM),
        cost_estimate=FREE,
        name="attend_back",
    )(qkv, lse, grad, *kept)


def rows_call(kernel, out_shape, name):
    return pl.pallas_call(
        kernel,
        out_shape=out_shape,
        cost_estimate=FREE,
        compiler_params=pltpu.CompilerParams(vmem_limit_bytes=ROWS_VMEM),
        name=name,
    )


def each_block(rows, step):
    @pl.loop(0, rows // ROW_BLOCK)
    def _(i):
        step(pl.ds(pl.multiple_of(i * ROW_BLOCK, ROW_BLOCK), ROW_BLOCK))


def pack_kernel(qkv_ref, out_ref, gains_ref, shifts_ref, packed_ref, small_ref):
    rows, wide = out_ref.shape
    for pair in range(wide // PAIR):
        for i in range(3):
            start = (3 * pair + i) * PAIR
            packed_ref[:, start : start + PAIR] = qkv_ref[i, :, pair * PAIR : (pair + 1) * PAIR]
    packed_ref[:, 3 * wide : 4 * wide] = out_ref[...]
    small_ref[...] = jnp.zeros_like(small_ref)
    small_ref[0:2, :rows] = gains_ref[...].astype(F32)
    small_ref[2:6, :rows] = shifts_ref[...].astype(F32)
    packed_ref[:, 4 * wide :] = jnp.zeros_like(packed_ref[:, 4 * wide :])
    packed_ref[:, 4 * wide : 4 * wide + 8] = small_ref[...].T[:rows].astype(BF)


def pack(qkv_weight, out_weight, gains, shifts):
    rows, wide = out_weight.shape
    args = (qkv_weight, out_weight, gains, shifts)
    shape = (rows, 4 * wide + PAIR)
    return pl.pallas_call(
        pack_kernel,
        out_shape=jax.ShapeDtypeStruct(shape, BF),
        scratch_shapes=[pltpu.VMEM((8, PAIR), F32)],
        cost_estimate=FREE,
        compiler_params=pltpu.CompilerParams(vmem_limit_bytes=4 * 2**20),
        name="pack",
    )(*args)


def finish_ff_kernel(kept_ref, got_ref, *out_refs):
    total = kept_ref[...] + got_ref[...].astype(F32)
    start = 0
    for out_ref in out_refs:
        columns = out_ref.shape[1]
        out_ref[...] = total[:, start : start + columns]
        start += columns


def finish_last_kernel(
    qkv_ref, qkv_got_ref, sums_ref, sums_got_ref, start_ref, *out_refs
):
    grad_ref, gains_ref, shifts_ref, qv_ref, bias_ref = out_refs
    pairs = qv_ref.shape[1] // PAIR
    grad = qkv_ref[...] + qkv_got_ref[...].astype(F32)
    for pair in range(pairs):
        for i in range(3):
            start = (3 * pair + i) * PAIR
            grad_ref[i, :, pair * PAIR : (pair + 1) * PAIR] = grad[:, start : start + PAIR]
    own = gains_ref.shape[1]
    total = sums_ref[...] + sums_got_ref[...]
    columns = total.shape[1]
    rows = pltpu.roll(total[:8], columns - start_ref[0], 1)[:, :own]
    gains_ref[...] = jnp.concatenate([rows[0:1], rows[2:3]], axis=0)
    shifts_ref[...] = jnp.concatenate([rows[1:2], rows[3:6]], axis=0)
    for pair in range(pairs):
        for i in range(2):
            here = slice(2 * i * PAIR, (2 * i + 1) * PAIR)
            qv_ref[i : i + 1, pair * PAIR : (pair + 1) * PAIR] = total[6 + pair : 7 + pair, here]
    for i in range(total.shape[0] - 6 - pairs):
        bias_ref[pl.ds(i * columns, columns)] = total[6 + pairs + i]


def finish_last(args, start, shapes):
    return pl.pallas_call(
        finish_last_kernel,
        in_specs=[pl.BlockSpec(memory_space=pltpu.VMEM)] * 4
        + [pl.BlockSpec(memory_space=pltpu.SMEM)],
        out_specs=[pl.BlockSpec(memory_space=pltpu.VMEM)] * 5,
        out_shape=[jax.ShapeDtypeStruct(x, F32) for x in shapes],
        cost_estimate=FREE,
        compiler_params=pltpu.CompilerParams(vmem_limit_bytes=4 * 2**20),
        name="finish_last",
    )(*args, start)


def finish(kernel, kept, got, shapes, name):
    return pl.pallas_call(
        kernel,
        out_shape=[jax.ShapeDtypeStruct(x, F32) for x in shapes],
        cost_estimate=FREE,
        compiler_params=pltpu.CompilerParams(vmem_limit_bytes=8 * 2**20),
        name=name,
    )(kept, got)


def join_kernel(mine_ref, other_ref, out_ref):
    half = mine_ref.shape[0]
    out_ref[:half] = mine_ref[...]
    out_ref[half:] = other_ref[...]


def join(mine, other):
    rows, columns = mine.shape
    shape = jax.ShapeDtypeStruct((2 * rows, columns), mine.dtype)
    return rows_call(join_kernel, shape, "join")(mine, other)


def standardized(x):
    center = x - jnp.mean(x, axis=-1, keepdims=True)
    inv_std = lax.rsqrt(jnp.mean(center * center, axis=-1, keepdims=True) + EPS)
    return center * inv_std, inv_std


def project_kernel(x_ref, weight_ref, bias_ref, normed_ref, qkv_ref, vectors_ref):
    width = qkv_ref.shape[1]
    small = weight_ref.shape[1] - PAIR
    vectors = weight_ref[:, small:].astype(F32).T[:8]
    vectors_ref[...] = vectors
    qv = bias_ref[...].astype(F32)
    none = jnp.zeros((1, PAIR), F32)
    bias = []
    for start in range(0, qv.shape[1], PAIR):
        bias += [qv[0:1, start : start + PAIR], none, qv[1:2, start : start + PAIR]]
    bias = jnp.concatenate(bias, axis=1)

    def step(here):
        unit, _ = standardized(x_ref[here].astype(F32))
        normed = (unit * vectors_ref[0:1] + vectors_ref[2:3]).astype(BF)
        normed_ref[here] = normed
        qkv_ref[here] = (dot(normed, weight_ref[:, :width], 1, 0) + bias).astype(BF)

    for i in range(0, x_ref.shape[0], ROW_BLOCK):
        step(pl.ds(i, ROW_BLOCK))


def project(x, first_full, bias, width):
    rows, columns = x.shape
    shapes = [
        jax.ShapeDtypeStruct((rows, columns), BF),
        jax.ShapeDtypeStruct((rows, width), BF),
        jax.ShapeDtypeStruct((8, columns), F32),
    ]
    return rows_call(project_kernel, shapes, "project")(x, first_full, bias)


def halves_of(refs, others):
    half = others[0].shape[0]
    return [
        ([ref.at[pl.ds(i * half, half)] for ref in refs], others[1 - i]) for i in range(PIECES)
    ]


def mid_norm_kernel(x_ref, mine_ref, vectors_ref, *refs):
    others, (hidden_ref, normed_ref) = refs[:PIECES], refs[PIECES:]
    for refs, other_ref in halves_of((x_ref, mine_ref, hidden_ref, normed_ref), others):
        frames, mine, hidden_half, normed_half = refs

        def step(here):
            branch = mine[here].astype(F32) + other_ref[here].astype(F32)
            hidden = frames[here].astype(F32) + (branch + vectors_ref[3:4])
            hidden_half[here] = hidden
            unit, _ = standardized(hidden)
            normed_half[here] = (unit * vectors_ref[1:2] + vectors_ref[4:5]).astype(BF)

        each_block(other_ref.shape[0], step)


def mid_norm(x, mine, others, vectors):
    shapes = [jax.ShapeDtypeStruct(x.shape, t) for t in (F32, BF)]
    return rows_call(mid_norm_kernel, shapes, "mid_norm")(x, mine, vectors, *others)


def act_back_kernel(d_out_ref, weight_ref, slope_ref, d_pre_ref, sums_ref):
    @pl.loop(0, d_pre_ref.shape[1] // COLUMN_BLOCK)
    def _(i):
        here = pl.ds(pl.multiple_of(i * COLUMN_BLOCK, COLUMN_BLOCK), COLUMN_BLOCK)
        d_act = dot(d_out_ref[...], weight_ref[:, here], 1, 0)
        d_pre = (d_act * slope_ref[:, here].astype(F32)).astype(BF)
        d_pre_ref[:, here] = d_pre
        sums_ref[:, here] = total_rows(d_pre.astype(F32))


def act_back(d_out, weight, slope):
    shapes = [jax.ShapeDtypeStruct(slope.shape, BF), jax.ShapeDtypeStruct((1, slope.shape[1]), F32)]
    return rows_call(act_back_kernel, shapes, "act_back")(d_out, weight, slope)


def norm_back(unit, inv_std, gain, grad):
    scaled = grad * gain
    return inv_std * (
        scaled
        - jnp.mean(scaled, axis=-1, keepdims=True)
        - unit * jnp.mean(scaled * unit, axis=-1, keepdims=True)
    )


def total_rows(x):
    return jnp.sum(x, axis=0, keepdims=True)


def mid_norm_back_kernel(mine_ref, hidden_ref, d_out_ref, vectors_ref, *refs):
    others, (branch_ref, d_hidden_ref, sums_ref) = refs[:PIECES], refs[PIECES:]
    sums_ref[...] = jnp.zeros_like(sums_ref)
    halves = halves_of((mine_ref, hidden_ref, d_out_ref, branch_ref), others)
    for i, (refs, other_ref) in enumerate(halves):
        mine, hidden, d_outs, branch = refs

        def step(here):
            grad = mine[here].astype(F32) + other_ref[here].astype(F32)
            unit, inv_std = standardized(hidden[here])
            d_out = d_outs[here].astype(F32)
            d_hidden = d_out + norm_back(unit, inv_std, vectors_ref[1:2], grad)
            d_branch = d_hidden.astype(BF)
            branch[here] = d_branch
            if i == 0:
                d_hidden_ref[here] = d_hidden
                terms = (grad * unit, d_branch.astype(F32), grad, d_out)
                sums_ref[...] += jnp.concatenate([total_rows(x) for x in terms], axis=0)

        each_block(other_ref.shape[0], step)


def mid_norm_back(mine, others, hidden, d_out, vectors):
    rows, columns = hidden.shape
    shapes = [
        jax.ShapeDtypeStruct((rows, columns), BF),
        jax.ShapeDtypeStruct((rows // 2, columns), F32),
        jax.ShapeDtypeStruct((4, columns), F32),
    ]
    return rows_call(mid_norm_back_kernel, shapes, "mid_norm_back")(
        mine, hidden, d_out, vectors, *others
    )


def first_norm_back_kernel(
    qkv_ref, weight_ref, x_ref, d_hidden_ref, vectors_ref, first_ref, second_ref, grad_ref, sums_ref
):
    sums = [jnp.zeros((1, x_ref.shape[1]), F32)] * 2
    width = qkv_ref.shape[1]
    rows = first_ref.shape[0]
    for i in range(x_ref.shape[0] // ROW_BLOCK):
        here = pl.ds(i * ROW_BLOCK, ROW_BLOCK)
        other_ref = (first_ref, second_ref)[i * ROW_BLOCK // rows]
        other = other_ref[pl.ds(i * ROW_BLOCK % rows, ROW_BLOCK)].astype(F32)
        grad = dot(qkv_ref[here], weight_ref[:, :width], 1, 1) + other
        unit, inv_std = standardized(x_ref[here].astype(F32))
        grad_ref[here] = d_hidden_ref[here] + norm_back(unit, inv_std, vectors_ref[0:1], grad)
        sums = [a + total_rows(b) for a, b in zip(sums, (grad * unit, grad))]
    sums_ref[...] = jnp.concatenate(sums, axis=0)


def first_norm_back(d_qkv, first_full, others, x, d_hidden, vectors):
    rows, columns = x.shape
    shapes = [jax.ShapeDtypeStruct((n, columns), F32) for n in (rows, 2)]
    return rows_call(first_norm_back_kernel, shapes, "first_norm_back")(
        d_qkv, first_full, x, d_hidden, vectors, *others
    )


def mm(spec, a, b):
    return jnp.einsum(spec, a, b, preferred_element_type=F32)


def body(
    inputs,
    cotangent,
    qkv_weight,
    out_weight,
    fc1_weight,
    fc2_weight,
    norm_gains,
    shifts,
    qv_bias,
    fc1_bias,
):
    inputs = inputs[0]
    cotangent = cotangent[0]
    own = norm_gains.shape[1]
    wide = qkv_weight.shape[2]
    pairs = wide // PAIR

    first_own = pack(qkv_weight, out_weight.T, norm_gains, shifts)
    at = position(own)
    half = inputs.shape[0]
    hidden_n = fc1_weight.shape[1]
    high = [stride for stride, _ in reversed(digits_of(lax.axis_size("dp"))[1:])]
    first_own, at = stage(first_own, at)
    first_part = gather_high_at_once(first_own, at)
    inputs_other = swap_core(inputs)

    ff_own = jnp.concatenate([fc1_weight, fc2_weight.T], axis=1)

    first_part, inputs_other, ff_part = stage(first_part, inputs_other, ff_own[None])
    first_near = gather_near(first_part)
    inputs_all = join(inputs, inputs_other)
    for stride in high:
        ff_part = place([ff_part, swap_dp(ff_part, stride)], stride, at)

    first_part, first_near, inputs_all = stage(first_part, first_near, inputs_all)
    first_far = gather_far(first_near)

    first_part, first_near, first_far, ff_part = stage(first_part, first_near, first_far, ff_part)
    ff_near = gather_near(ff_part)
    cotangent_other = swap_core(after(cotangent, first_part))
    first_full = all_rows([first_part, *first_near, *first_far], 0, first_part.shape[2], at)
    out_full = first_full[:, 3 * wide : 4 * wide]
    normed_all, qkv, vectors = project(inputs_all, first_full, qv_bias, 3 * wide)
    attended, log_sums = attend(qkv, 0, pairs)
    branch = mm("fe,de->fd", attended, out_full).astype(BF)
    branch_other = swap_pieces(branch, PIECES)
    hidden_all, normed_two_all = mid_norm(inputs_all, branch, branch_other, vectors)

    ff_part, ff_near, normed_two_all, cotangent_other = stage(
        ff_part, ff_near, normed_two_all, cotangent_other
    )
    mid_far = gather_far([x[:, :, :hidden_n] for x in ff_near])
    d_out_all = join(cotangent, cotangent_other)

    ff_part, ff_near, mid_far, d_out_all = stage(ff_part, ff_near, mid_far, d_out_all)
    end_far = gather_far([x[:, :, hidden_n:] for x in ff_near])
    mid_full = all_rows([ff_part, *ff_near, *mid_far], 0, hidden_n, at)
    hidden_pre = mm("fd,dh->fh", normed_two_all, mid_full) + fc1_bias.astype(F32)
    cdf = 0.5 * (1.0 + lax.erf(hidden_pre * 0.5**0.5))
    hidden_act = (hidden_pre * cdf).astype(BF)
    slope = cdf + hidden_pre * jnp.exp(-0.5 * hidden_pre * hidden_pre) * 0.3989422804014327
    hidden_act, slope, d_out_all, end_far = stage(hidden_act, slope.astype(BF), d_out_all, end_far)
    fc2_grad = mm("fd,fh->dh", d_out_all, hidden_act).astype(BF)
    fc2_parts, fc2_ops = scatter_operands(fc2_grad, at)

    ff_part, ff_near, end_far, d_out_all, fc2_ops = stage(
        ff_part, ff_near, end_far, d_out_all, fc2_ops
    )
    fc2_far = scatter_low_across(fc2_ops)
    end_full = all_rows([ff_part, *ff_near, *end_far], hidden_n, hidden_n, at)
    d_pre, fc1_bias_grad = act_back(d_out_all, end_full, slope)
    d_two = mm("fh,dh->fd", d_pre, mid_full).astype(BF)

    d_two, fc2_far, d_pre = stage(d_two, fc2_far, d_pre)
    fc2_near = scatter_low_near(near_operands(fc2_parts, fc2_far))
    d_two_other = swap_pieces(d_two, PIECES)
    fc1_grad = mm("fd,fh->dh", normed_two_all, d_pre).astype(BF)
    d_branch_all, d_hidden, mid_sums = mid_norm_back(
        d_two, d_two_other, hidden_all, d_out_all, vectors
    )
    d_attended = mm("fd,de->fe", d_branch_all, out_full).astype(BF)
    out_grad = mm("fd,fe->de", d_branch_all, attended).astype(BF)
    mid_parts, mid_ops = scatter_operands(jnp.concatenate([fc1_grad, out_grad], axis=1), at)

    d_attended, mid_ops = stage(d_attended, mid_ops)
    mid_far = scatter_low_across(mid_ops)
    d_proj = attend_back(qkv, log_sums, d_attended, 0, pairs - 1)

    d_proj, mid_far, fc2_near = stage(d_proj, mid_far, fc2_near)
    mid_near = scatter_low_near(near_operands(mid_parts, mid_far))
    fc2_sum = scatter_high_step(high_operands(total_of(fc2_near), 0, at), 0)
    d_qkv, d_sums = attend_back(qkv, log_sums, d_attended, pairs - 1, 1, d_proj)
    qkv_grad = mm("fd,fe->de", normed_all, d_qkv).astype(BF)
    qkv_parts, qkv_ops = scatter_operands(qkv_grad, at)

    qkv_ops, d_qkv, fc2_sum, hidden_act = stage(qkv_ops, d_qkv, fc2_sum, hidden_act)
    qkv_far = scatter_low_across(qkv_ops)
    d_other = mm("fe,de->fd", d_qkv[half:], first_full[:, : 3 * wide]).astype(BF)
    mlp_other = mm("fh,dh->fd", hidden_act[half:], end_full).astype(BF)
    mlp_mine = mm("fh,dh->fd", hidden_act[:half], end_full)

    fc2_last = scatter_high_last(fc2_sum, 1, at)

    qkv_far, mid_near, d_other, mlp_other, mlp_mine, fc2_last = stage(
        qkv_far, mid_near, d_other, mlp_other, mlp_mine, fc2_last
    )
    qkv_near = scatter_low_near(near_operands(qkv_parts, qkv_far))
    mid_sum = scatter_high_step(high_operands(total_of(mid_near), 0, at), 0)
    d_other_got = swap_pieces(d_other, 2)
    input_grad, first_sums = first_norm_back(
        d_qkv, first_full, d_other_got, inputs, d_hidden, vectors
    )
    rows = jnp.concatenate([first_sums, mid_sums], axis=0)
    rows = rows + swap_core(rows)

    mid_sum, qkv_near, rows = stage(mid_sum, qkv_near, rows)
    width = rows.shape[1]
    flat = [rows, jnp.pad(d_sums[:, 0], ((0, 0), (0, width - 3 * PAIR)))]
    flat += [fc1_bias_grad[:, i : i + width] for i in range(0, fc1_bias_grad.shape[1], width)]
    flat = sum_over(jnp.concatenate(flat, axis=0), [1, 2] + high[:0:-1])
    qkv_sum = scatter_high_step(high_operands(total_of(qkv_near), 0, at), 0)
    mlp_got = swap_core(mlp_other)
    mid_last = scatter_high_last(mid_sum, 1, at)

    qkv_sum, flat, mlp_got = stage(qkv_sum, flat, mlp_got)
    outputs = hidden_all[:half] + ((mlp_mine + mlp_got.astype(F32)) + vectors[5:6])
    qkv_out, gains_out, shifts_out, qv_out, bias_out = finish_last(
        (*scatter_high_last(qkv_sum, 1, at), flat, swap_dp(flat, high[0])),
        at["start"],
        [qkv_weight.shape, norm_gains.shape, shifts.shape, qv_bias.shape, fc1_bias.shape],
    )
    (fc2_out,) = finish(finish_ff_kernel, *fc2_last, [(own, hidden_n)], "finish_fc2")
    fc1_out, out_out = finish(
        finish_ff_kernel, *mid_last, [(own, n) for n in (hidden_n, wide)], "finish_mid"
    )
    return (
        outputs[None],
        input_grad[None],
        qkv_out,
        out_out.T,
        fc1_out,
        fc2_out.T,
        gains_out,
        shifts_out,
        qv_out,
        bias_out,
    )


def solution(mesh):
    specs = (
        P("dp", "tensor", None),
        P("dp", "tensor", None),
        P(None, "dp", "tensor"),
        P("tensor", "dp"),
        P("dp", "tensor"),
        P("tensor", "dp"),
        P(None, "dp"),
        P(None, "dp"),
        P(None, "tensor"),
        P("tensor"),
    )
    return jax.shard_map(body, mesh=mesh, in_specs=specs, out_specs=specs, check_vma=False)
```

```python
import functools

import jax
import jax.numpy as jnp
from jax import lax
from jax.experimental import pallas as pl
from jax.experimental.pallas import tpu as pltpu
from jax.sharding import PartitionSpec as P

HEAD = 64
PAIR = 2 * HEAD
ATTEND_VMEM = 20 * 2**20
BACK_VMEM = 24 * 2**20
ROWS_VMEM = 16 * 2**20
PIECES = 2
ROW_BLOCK = 256
COLUMN_BLOCK = 512
ACT_BLOCK = 256
FREE = pl.CostEstimate(flops=0, bytes_accessed=0, transcendentals=0)
EPS = 1e-05
BF = jnp.bfloat16
F32 = jnp.float32


def after(x, *others):
    return lax.optimization_barrier((x, others))[0]


def stage(*values):
    return lax.optimization_barrier(values)


def digits_of(n):
    low = 4 if n % 4 == 0 else n
    found, stride = [(1, low)], low
    while stride < n:
        found.append((stride, 2))
        stride *= 2
    return found


def swap_dp(x, step):
    n = lax.axis_size("dp")
    return lax.ppermute(x, "dp", [(i, i ^ step) for i in range(n)])


def swap_core(x):
    return lax.ppermute(x, "tensor", [(0, 1), (1, 0)])


def position(own):
    n = lax.axis_size("dp")
    me = lax.axis_index("dp")
    bits = [(me >> i) & 1 for i in range(n.bit_length() - 1)]
    low = me & 3
    return {
        "bits": [(me & (1 << i)) != 0 for i in range(len(bits))],
        "low": [low ^ k for k in range(4)],
        "high": [[bit, 1 - bit] for bit in bits[2:]],
        "digit": low.reshape(1),
        "start": (me * own).reshape(1),
    }


def pick(options, bits):
    for bit in bits:
        options = [jnp.where(bit, b, a) for a, b in zip(options[0::2], options[1::2])]
    return options[0]


def place(got, stride, at):
    radix = len(got)
    first = stride.bit_length() - 1
    bits = at["bits"][first : first + radix.bit_length() - 1]
    placed = [pick([got[i ^ m] for m in range(radix)], bits) for i in range(radix)]
    return jnp.stack(placed, axis=1).reshape((-1,) + got[0].shape[1:])


def gather_high_at_once(x, at):
    n = lax.axis_size("dp")
    low = digits_of(n)[0][1]
    stride = n // 4
    cur = place([x[None]] + [swap_dp(x[None], stride * k) for k in range(1, 4)], stride, at)
    while stride > low:
        stride //= 2
        cur = place([cur, swap_dp(cur, stride)], stride, at)
    return cur


def gather_near(cur):
    return swap_dp(cur, 1), swap_dp(cur, 2)


def gather_far(near):
    half = near[0].shape[0] // 2
    return swap_dp(near[0][:half], 2), swap_dp(near[1][half:], 1)


def gather_low(cur):
    return [swap_dp(cur, k) for k in range(1, digits_of(lax.axis_size("dp"))[0][1])]


def rows_kernel(start, mine_ref, *refs):
    sources, out_ref = refs[:-1], refs[-1]
    high, _, _, columns = out_ref.shape
    mine = mine_ref[0]
    here = pl.ds(start, columns)
    for i in range(high):
        for k, source in enumerate(sources[:3]):
            out_ref[i, mine ^ k] = source[i, :, here]
        far = sources[3 + i * (len(sources) - 3) // high]
        out_ref[i, mine ^ 3] = far[i % far.shape[0]]


def all_rows(sources, start, columns, at):
    high, rows, _ = sources[0].shape
    full = pl.pallas_call(
        functools.partial(rows_kernel, start),
        in_specs=[pl.BlockSpec(memory_space=pltpu.SMEM)]
        + [pl.BlockSpec(memory_space=pltpu.VMEM)] * len(sources),
        out_specs=pl.BlockSpec(memory_space=pltpu.VMEM),
        out_shape=jax.ShapeDtypeStruct((high, 4, rows, columns), BF),
        cost_estimate=FREE,
        compiler_params=pltpu.CompilerParams(vmem_limit_bytes=ROWS_VMEM),
        name="all_rows",
    )(at["digit"], *sources)
    return full.reshape(-1, columns)


def part_of(view, index, first=0, count=0):
    sizes = (count or view.shape[0], 1) + view.shape[2:]
    starts = [jnp.int32(first), index] + [jnp.int32(0)] * (view.ndim - 2)
    piece = lax.dynamic_slice(view, starts, sizes, allow_negative_indices=False)
    return piece.reshape(sizes[:1] + sizes[2:])


def total_of(parts):
    total = parts[0].astype(F32)
    for part in parts[1:]:
        total = total + part.astype(F32)
    return total


def scatter_operands(x, at):
    n = lax.axis_size("dp")
    view = x.reshape(n // 4, 4, x.shape[0] // n, x.shape[1])
    half = view.shape[0] // 2
    one, two, across = (
        [part_of(view, index, first, half) for first in (0, half)] for index in at["low"][1:]
    )
    return (part_of(view, at["low"][0]), one, two), across


def scatter_low_across(operands):
    return swap_dp(operands[0], 1), swap_dp(operands[1], 2)


def near_operands(parts, across):
    mine, one, two = parts
    one = jnp.concatenate([one[0], total_of([one[1], across[1]]).astype(BF)], axis=0)
    two = jnp.concatenate([total_of([two[0], across[0]]).astype(BF), two[1]], axis=0)
    return mine, one, two


def scatter_low_near(operands):
    mine, one, two = operands
    return mine, swap_dp(one, 1), swap_dp(two, 2)


def high_operands(cur, index, at):
    view = cur.reshape((-1, 2) + cur.shape[1:])
    kept, sent = (part_of(view, i) for i in at["high"][index])
    return kept, sent.astype(BF)


def scatter_high_step(operands, index):
    stride, _ = digits_of(lax.axis_size("dp"))[1 + index]
    return operands[0] + swap_dp(operands[1], stride).astype(F32)


def scatter_high_last(cur, index, at):
    digits = digits_of(lax.axis_size("dp"))[1:]
    for i in range(index, len(digits) - 1):
        cur = scatter_high_step(high_operands(cur, i, at), i)
    kept, sent = high_operands(cur, len(digits) - 1, at)
    return kept[0], swap_dp(sent, digits[-1][0])[0]


def sum_over(x, steps):
    for step in steps:
        x = x + swap_dp(x, step)
    return x


def swap_pieces(x, count):
    rows = x.shape[0] // count
    return [swap_core(x[i * rows : (i + 1) * rows]) for i in range(count)]


def dot(a, b, ca, cb):
    return lax.dot_general(a, b, (((ca,), (cb,)), ((), ())), preferred_element_type=F32)


def attend_kernel(qkv_ref, *refs):
    out_ref, lse_ref = refs[-2:]
    queries = qkv_ref[:, :PAIR]
    keys_all = qkv_ref[:, PAIR : 2 * PAIR] * jnp.asarray(HEAD**-0.5, BF)
    values = qkv_ref[:, 2 * PAIR :]
    first = lax.broadcasted_iota(jnp.int32, (1, PAIR), 1) < HEAD
    outs, logs = [], []
    for own in (first, ~first):
        here = jnp.where(own, queries, jnp.zeros_like(queries))
        scores = dot(keys_all, here, 1, 1)
        row_max = jnp.max(scores, axis=0, keepdims=True)
        powers = jnp.exp(scores - row_max)
        summed = jnp.sum(powers, axis=0, keepdims=True)
        probs = (powers * (1.0 / summed)).astype(BF)
        outs.append(dot(values, probs, 0, 0))
        logs.append(row_max + jnp.log(summed))
    both = jnp.concatenate([outs[0][:HEAD], outs[1][HEAD:]], axis=0)
    out_ref[...] = both.T.astype(BF)
    lse_ref[...] = jnp.concatenate(logs, axis=0)[None]


def attend(qkv, start, count, kept=()):
    n, width = qkv.shape
    pairs = width // (3 * PAIR)
    return pl.pallas_call(
        attend_kernel,
        grid=(count,),
        in_specs=[pl.BlockSpec((n, 3 * PAIR), lambda p: (0, p + start))]
        + [pl.BlockSpec(memory_space=pl.ANY)] * len(kept),
        out_specs=[
            pl.BlockSpec((n, PAIR), lambda p: (0, p + start)),
            pl.BlockSpec((1, 2, n), lambda p: (p + start, 0, 0)),
        ],
        out_shape=[
            jax.ShapeDtypeStruct((n, pairs * PAIR), BF),
            jax.ShapeDtypeStruct((pairs, 2, n), F32),
        ],
        input_output_aliases={1 + i: i for i in range(len(kept))},
        compiler_params=pltpu.CompilerParams(vmem_limit_bytes=ATTEND_VMEM),
        cost_estimate=FREE,
        name="attend",
    )(qkv, *kept)


def attend_back_kernel(qkv_ref, lse_ref, grad_ref, *refs):
    out_ref, sum_ref = refs[-2:]
    factor = jnp.asarray(HEAD**-0.5, BF)
    queries = qkv_ref[:, :PAIR]
    keys_small = qkv_ref[:, PAIR : 2 * PAIR] * factor
    values = qkv_ref[:, 2 * PAIR :]
    grad = grad_ref[...]
    first = lax.broadcasted_iota(jnp.int32, (1, PAIR), 1) < HEAD
    parts = []
    for own in (first, ~first):
        q_here = jnp.where(own, queries, jnp.zeros_like(queries))
        g_here = jnp.where(own, grad, jnp.zeros_like(grad))
        parts.append((q_here, g_here, dot(keys_small, q_here, 1, 1), dot(values, g_here, 1, 1)))
    d_q, d_k, d_v = [], [], []
    for head, (q_here, g_here, scores, d_probs) in enumerate(parts):
        probs = jnp.exp(scores - lse_ref[0, head : head + 1, :])
        product = probs * d_probs
        row_sum = jnp.sum(product, axis=0, keepdims=True)
        d_scores = (product - probs * row_sum).astype(BF)
        d_v.append(dot(probs.astype(BF), g_here, 1, 0))
        d_k.append(dot(d_scores, q_here, 1, 0))
        d_q.append(dot(keys_small, d_scores, 0, 0))
    queries_t = jnp.concatenate([d_q[0][:HEAD], d_q[1][HEAD:]], axis=0)
    d_queries = queries_t.T.astype(BF)
    d_keys = ((d_k[0] + d_k[1]) * HEAD**-0.5).astype(BF)
    d_values = (d_v[0] + d_v[1]).astype(BF)
    for i, x in enumerate((d_queries, d_keys, d_values)):
        out_ref[:, i * PAIR : (i + 1) * PAIR] = x
        sum_ref[0, :, i * PAIR : (i + 1) * PAIR] = jnp.sum(x.astype(F32), axis=0, keepdims=True)


def attend_back(qkv, lse, grad, start, count, kept=()):
    n, width = qkv.shape
    pairs = width // (3 * PAIR)
    return pl.pallas_call(
        attend_back_kernel,
        grid=(count,),
        in_specs=[
            pl.BlockSpec((n, 3 * PAIR), lambda p: (0, p + start)),
            pl.BlockSpec((1, 2, n), lambda p: (p + start, 0, 0)),
            pl.BlockSpec((n, PAIR), lambda p: (0, p + start)),
        ]
        + [pl.BlockSpec(memory_space=pl.ANY)] * len(kept),
        out_specs=[
            pl.BlockSpec((n, 3 * PAIR), lambda p: (0, p + start)),
            pl.BlockSpec((1, 1, 3 * PAIR), lambda p: (p + start, 0, 0)),
        ],
        out_shape=[
            jax.ShapeDtypeStruct((n, width), BF),
            jax.ShapeDtypeStruct((pairs, 1, 3 * PAIR), F32),
        ],
        input_output_aliases={3 + i: i for i in range(len(kept))},
        compiler_params=pltpu.CompilerParams(vmem_limit_bytes=BACK_VMEM),
        cost_estimate=FREE,
        name="attend_back",
    )(qkv, lse, grad, *kept)


def rows_call(kernel, out_shape, name):
    return pl.pallas_call(
        kernel,
        out_shape=out_shape,
        cost_estimate=FREE,
        compiler_params=pltpu.CompilerParams(vmem_limit_bytes=ROWS_VMEM),
        name=name,
    )


def each_block(rows, step):
    @pl.loop(0, rows // ROW_BLOCK)
    def _(i):
        step(pl.ds(pl.multiple_of(i * ROW_BLOCK, ROW_BLOCK), ROW_BLOCK))


def pack_kernel(qkv_ref, out_ref, gains_ref, shifts_ref, packed_ref, small_ref):
    rows, wide = out_ref.shape
    for pair in range(wide // PAIR):
        for i in range(3):
            start = (3 * pair + i) * PAIR
            packed_ref[:, start : start + PAIR] = qkv_ref[i, :, pair * PAIR : (pair + 1) * PAIR]
    packed_ref[:, 3 * wide : 4 * wide] = out_ref[...]
    small_ref[...] = jnp.zeros_like(small_ref)
    small_ref[0:2, :rows] = gains_ref[...].astype(F32)
    small_ref[2:6, :rows] = shifts_ref[...].astype(F32)
    packed_ref[:, 4 * wide :] = jnp.zeros_like(packed_ref[:, 4 * wide :])
    packed_ref[:, 4 * wide : 4 * wide + 8] = small_ref[...].T[:rows].astype(BF)


def pack(qkv_weight, out_weight, gains, shifts):
    rows, wide = out_weight.shape
    args = (qkv_weight, out_weight, gains, shifts)
    shape = (rows, 4 * wide + PAIR)
    return pl.pallas_call(
        pack_kernel,
        out_shape=jax.ShapeDtypeStruct(shape, BF),
        scratch_shapes=[pltpu.VMEM((8, PAIR), F32)],
        cost_estimate=FREE,
        compiler_params=pltpu.CompilerParams(vmem_limit_bytes=4 * 2**20),
        name="pack",
    )(*args)


def finish_ff_kernel(kept_ref, got_ref, *out_refs):
    total = kept_ref[...] + got_ref[...].astype(F32)
    start = 0
    for out_ref in out_refs:
        columns = out_ref.shape[1]
        out_ref[...] = total[:, start : start + columns]
        start += columns


def finish_last_kernel(
    qkv_ref, qkv_got_ref, sums_ref, sums_got_ref, start_ref, *out_refs
):
    grad_ref, gains_ref, shifts_ref, qv_ref, bias_ref = out_refs
    pairs = qv_ref.shape[1] // PAIR
    grad = qkv_ref[...] + qkv_got_ref[...].astype(F32)
    for pair in range(pairs):
        for i in range(3):
            start = (3 * pair + i) * PAIR
            grad_ref[i, :, pair * PAIR : (pair + 1) * PAIR] = grad[:, start : start + PAIR]
    own = gains_ref.shape[1]
    total = sums_ref[...] + sums_got_ref[...]
    columns = total.shape[1]
    rows = pltpu.roll(total[:8], columns - start_ref[0], 1)[:, :own]
    gains_ref[...] = jnp.concatenate([rows[0:1], rows[2:3]], axis=0)
    shifts_ref[...] = jnp.concatenate([rows[1:2], rows[3:6]], axis=0)
    for pair in range(pairs):
        for i in range(2):
            here = slice(2 * i * PAIR, (2 * i + 1) * PAIR)
            qv_ref[i : i + 1, pair * PAIR : (pair + 1) * PAIR] = total[6 + pair : 7 + pair, here]
    for i in range(total.shape[0] - 6 - pairs):
        bias_ref[pl.ds(i * columns, columns)] = total[6 + pairs + i]


def finish_last(args, start, shapes):
    return pl.pallas_call(
        finish_last_kernel,
        in_specs=[pl.BlockSpec(memory_space=pltpu.VMEM)] * 4
        + [pl.BlockSpec(memory_space=pltpu.SMEM)],
        out_specs=[pl.BlockSpec(memory_space=pltpu.VMEM)] * 5,
        out_shape=[jax.ShapeDtypeStruct(x, F32) for x in shapes],
        cost_estimate=FREE,
        compiler_params=pltpu.CompilerParams(vmem_limit_bytes=4 * 2**20),
        name="finish_last",
    )(*args, start)


def finish(kernel, kept, got, shapes, name):
    return pl.pallas_call(
        kernel,
        out_shape=[jax.ShapeDtypeStruct(x, F32) for x in shapes],
        cost_estimate=FREE,
        compiler_params=pltpu.CompilerParams(vmem_limit_bytes=8 * 2**20),
        name=name,
    )(kept, got)


def join_kernel(mine_ref, other_ref, out_ref):
    half = mine_ref.shape[0]
    out_ref[:half] = mine_ref[...]
    out_ref[half:] = other_ref[...]


def join(mine, other):
    rows, columns = mine.shape
    shape = jax.ShapeDtypeStruct((2 * rows, columns), mine.dtype)
    return rows_call(join_kernel, shape, "join")(mine, other)


def standardized(x):
    center = x - jnp.mean(x, axis=-1, keepdims=True)
    inv_std = lax.rsqrt(jnp.mean(center * center, axis=-1, keepdims=True) + EPS)
    return center * inv_std, inv_std


def project_kernel(x_ref, weight_ref, bias_ref, normed_ref, qkv_ref, vectors_ref):
    width = qkv_ref.shape[1]
    small = weight_ref.shape[1] - PAIR
    vectors = weight_ref[:, small:].astype(F32).T[:8]
    vectors_ref[...] = vectors
    qv = bias_ref[...].astype(F32)
    none = jnp.zeros((1, PAIR), F32)
    bias = []
    for start in range(0, qv.shape[1], PAIR):
        bias += [qv[0:1, start : start + PAIR], none, qv[1:2, start : start + PAIR]]
    bias = jnp.concatenate(bias, axis=1)

    def step(here):
        unit, _ = standardized(x_ref[here].astype(F32))
        normed = (unit * vectors_ref[0:1] + vectors_ref[2:3]).astype(BF)
        normed_ref[here] = normed
        qkv_ref[here] = (dot(normed, weight_ref[:, :width], 1, 0) + bias).astype(BF)

    for i in range(0, x_ref.shape[0], ROW_BLOCK):
        step(pl.ds(i, ROW_BLOCK))


def project(x, first_full, bias, width):
    rows, columns = x.shape
    shapes = [
        jax.ShapeDtypeStruct((rows, columns), BF),
        jax.ShapeDtypeStruct((rows, width), BF),
        jax.ShapeDtypeStruct((8, columns), F32),
    ]
    return rows_call(project_kernel, shapes, "project")(x, first_full, bias)


def halves_of(refs, others):
    half = others[0].shape[0]
    return [
        ([ref.at[pl.ds(i * half, half)] for ref in refs], others[1 - i]) for i in range(PIECES)
    ]


def mid_norm_kernel(x_ref, mine_ref, vectors_ref, *refs):
    others, (hidden_ref, normed_ref) = refs[:PIECES], refs[PIECES:]
    for refs, other_ref in halves_of((x_ref, mine_ref, hidden_ref, normed_ref), others):
        frames, mine, hidden_half, normed_half = refs

        def step(here):
            branch = mine[here].astype(F32) + other_ref[here].astype(F32)
            hidden = frames[here].astype(F32) + (branch + vectors_ref[3:4])
            hidden_half[here] = hidden
            unit, _ = standardized(hidden)
            normed_half[here] = (unit * vectors_ref[1:2] + vectors_ref[4:5]).astype(BF)

        each_block(other_ref.shape[0], step)


def mid_norm(x, mine, others, vectors):
    shapes = [jax.ShapeDtypeStruct(x.shape, t) for t in (F32, BF)]
    return rows_call(mid_norm_kernel, shapes, "mid_norm")(x, mine, vectors, *others)


def act_kernel(x_ref, weight_ref, bias_ref, act_ref, slope_ref):
    bias = bias_ref[...].astype(F32).reshape(1, bias_ref.shape[0])
    for start in range(0, act_ref.shape[1], ACT_BLOCK):
        here = slice(start, start + ACT_BLOCK)
        pre = dot(x_ref[...], weight_ref[:, here], 1, 0) + bias[:, here]
        cdf = 0.5 * (1.0 + lax.erf(pre * 0.5**0.5))
        act_ref[:, here] = (pre * cdf).astype(BF)
        slope = cdf + pre * jnp.exp(-0.5 * pre * pre) * 0.3989422804014327
        slope_ref[:, here] = slope.astype(BF)


def act(x, weight, bias):
    shape = jax.ShapeDtypeStruct((x.shape[0], weight.shape[1]), BF)
    return rows_call(act_kernel, [shape, shape], "act")(x, weight, bias)


def act_back_kernel(d_out_ref, weight_ref, slope_ref, d_pre_ref, sums_ref):
    @pl.loop(0, d_pre_ref.shape[1] // COLUMN_BLOCK)
    def _(i):
        here = pl.ds(pl.multiple_of(i * COLUMN_BLOCK, COLUMN_BLOCK), COLUMN_BLOCK)
        d_act = dot(d_out_ref[...], weight_ref[:, here], 1, 0)
        d_pre = (d_act * slope_ref[:, here].astype(F32)).astype(BF)
        d_pre_ref[:, here] = d_pre
        sums_ref[:, here] = total_rows(d_pre.astype(F32))


def act_back(d_out, weight, slope):
    shapes = [jax.ShapeDtypeStruct(slope.shape, BF), jax.ShapeDtypeStruct((1, slope.shape[1]), F32)]
    return rows_call(act_back_kernel, shapes, "act_back")(d_out, weight, slope)


def norm_back(unit, inv_std, gain, grad):
    scaled = grad * gain
    return inv_std * (
        scaled
        - jnp.mean(scaled, axis=-1, keepdims=True)
        - unit * jnp.mean(scaled * unit, axis=-1, keepdims=True)
    )


def total_rows(x):
    return jnp.sum(x, axis=0, keepdims=True)


def mid_norm_back_kernel(mine_ref, hidden_ref, d_out_ref, vectors_ref, *refs):
    others, (branch_ref, d_hidden_ref, sums_ref) = refs[:PIECES], refs[PIECES:]
    sums_ref[...] = jnp.zeros_like(sums_ref)
    halves = halves_of((mine_ref, hidden_ref, d_out_ref, branch_ref), others)
    for i, (refs, other_ref) in enumerate(halves):
        mine, hidden, d_outs, branch = refs

        def step(here):
            grad = mine[here].astype(F32) + other_ref[here].astype(F32)
            unit, inv_std = standardized(hidden[here])
            d_out = d_outs[here].astype(F32)
            d_hidden = d_out + norm_back(unit, inv_std, vectors_ref[1:2], grad)
            d_branch = d_hidden.astype(BF)
            branch[here] = d_branch
            if i == 0:
                d_hidden_ref[here] = d_hidden
                terms = (grad * unit, d_branch.astype(F32), grad, d_out)
                sums_ref[...] += jnp.concatenate([total_rows(x) for x in terms], axis=0)

        each_block(other_ref.shape[0], step)


def mid_norm_back(mine, others, hidden, d_out, vectors):
    rows, columns = hidden.shape
    shapes = [
        jax.ShapeDtypeStruct((rows, columns), BF),
        jax.ShapeDtypeStruct((rows // 2, columns), F32),
        jax.ShapeDtypeStruct((4, columns), F32),
    ]
    return rows_call(mid_norm_back_kernel, shapes, "mid_norm_back")(
        mine, hidden, d_out, vectors, *others
    )


def first_norm_back_kernel(
    qkv_ref, weight_ref, x_ref, d_hidden_ref, vectors_ref, first_ref, second_ref, grad_ref, sums_ref
):
    sums = [jnp.zeros((1, x_ref.shape[1]), F32)] * 2
    width = qkv_ref.shape[1]
    rows = first_ref.shape[0]
    for i in range(x_ref.shape[0] // ROW_BLOCK):
        here = pl.ds(i * ROW_BLOCK, ROW_BLOCK)
        other_ref = (first_ref, second_ref)[i * ROW_BLOCK // rows]
        other = other_ref[pl.ds(i * ROW_BLOCK % rows, ROW_BLOCK)].astype(F32)
        grad = dot(qkv_ref[here], weight_ref[:, :width], 1, 1) + other
        unit, inv_std = standardized(x_ref[here].astype(F32))
        grad_ref[here] = d_hidden_ref[here] + norm_back(unit, inv_std, vectors_ref[0:1], grad)
        sums = [a + total_rows(b) for a, b in zip(sums, (grad * unit, grad))]
    sums_ref[...] = jnp.concatenate(sums, axis=0)


def first_norm_back(d_qkv, first_full, others, x, d_hidden, vectors):
    rows, columns = x.shape
    shapes = [jax.ShapeDtypeStruct((n, columns), F32) for n in (rows, 2)]
    return rows_call(first_norm_back_kernel, shapes, "first_norm_back")(
        d_qkv, first_full, x, d_hidden, vectors, *others
    )


def last_terms_kernel(d_qkv_ref, first_ref, act_ref, end_ref, d_other_ref, other_ref, mine_ref):
    half, columns = mine_ref.shape
    width = d_qkv_ref.shape[1]
    there = pl.ds(half, half)
    d_other = dot(d_qkv_ref[there], first_ref[:, :width], 1, 1)
    d_other_ref[...] = d_other.astype(BF)
    other_ref[...] = dot(act_ref[there], end_ref[...], 1, 1).astype(BF)
    mine_ref[...] = dot(act_ref[pl.ds(0, half)], end_ref[...], 1, 1)


def last_terms(d_qkv, first_full, hidden_act, end_full):
    shape = (d_qkv.shape[0] // 2, end_full.shape[0])
    shapes = [jax.ShapeDtypeStruct(shape, t) for t in (BF, BF, F32)]
    return rows_call(last_terms_kernel, shapes, "last_terms")(
        d_qkv, first_full, hidden_act, end_full
    )


def mm(spec, a, b):
    return jnp.einsum(spec, a, b, preferred_element_type=F32)


def body(
    inputs,
    cotangent,
    qkv_weight,
    out_weight,
    fc1_weight,
    fc2_weight,
    norm_gains,
    shifts,
    qv_bias,
    fc1_bias,
):
    inputs = inputs[0]
    cotangent = cotangent[0]
    own = norm_gains.shape[1]
    wide = qkv_weight.shape[2]
    pairs = wide // PAIR

    first_own = pack(qkv_weight, out_weight.T, norm_gains, shifts)
    at = position(own)
    half = inputs.shape[0]
    hidden_n = fc1_weight.shape[1]
    high = [stride for stride, _ in reversed(digits_of(lax.axis_size("dp"))[1:])]
    first_own, at = stage(first_own, at)
    first_part = gather_high_at_once(first_own, at)
    inputs_other = swap_core(inputs)

    ff_own = jnp.concatenate([fc1_weight, fc2_weight.T], axis=1)

    first_part, inputs_other, ff_part = stage(first_part, inputs_other, ff_own[None])
    first_near = gather_near(first_part)
    inputs_all = join(inputs, inputs_other)
    for stride in high:
        ff_part = place([ff_part, swap_dp(ff_part, stride)], stride, at)

    first_part, first_near, inputs_all = stage(first_part, first_near, inputs_all)
    first_far = gather_far(first_near)

    first_part, first_near, first_far, ff_part = stage(first_part, first_near, first_far, ff_part)
    ff_near = gather_near(ff_part)
    cotangent_other = swap_core(after(cotangent, first_part))
    first_full = all_rows([first_part, *first_near, *first_far], 0, first_part.shape[2], at)
    out_full = first_full[:, 3 * wide : 4 * wide]
    normed_all, qkv, vectors = project(inputs_all, first_full, qv_bias, 3 * wide)
    attended, log_sums = attend(qkv, 0, pairs)
    branch = mm("fe,de->fd", attended, out_full).astype(BF)
    branch_other = swap_pieces(branch, PIECES)
    hidden_all, normed_two_all = mid_norm(inputs_all, branch, branch_other, vectors)

    ff_part, ff_near, normed_two_all, cotangent_other = stage(
        ff_part, ff_near, normed_two_all, cotangent_other
    )
    mid_far = gather_far([x[:, :, :hidden_n] for x in ff_near])
    d_out_all = join(cotangent, cotangent_other)

    ff_part, ff_near, mid_far, d_out_all = stage(ff_part, ff_near, mid_far, d_out_all)
    end_far = gather_far([x[:, :, hidden_n:] for x in ff_near])
    mid_full = all_rows([ff_part, *ff_near, *mid_far], 0, hidden_n, at)
    hidden_act, slope = act(normed_two_all, mid_full, fc1_bias)
    hidden_act, slope, d_out_all = stage(hidden_act, slope, d_out_all)
    fc2_grad = mm("fd,fh->dh", d_out_all, hidden_act).astype(BF)
    fc2_parts, fc2_ops = scatter_operands(fc2_grad, at)

    ff_part, ff_near, end_far, d_out_all, fc2_ops = stage(
        ff_part, ff_near, end_far, d_out_all, fc2_ops
    )
    fc2_far = scatter_low_across(fc2_ops)
    end_full = all_rows([ff_part, *ff_near, *end_far], hidden_n, hidden_n, at)
    d_pre, fc1_bias_grad = act_back(d_out_all, end_full, slope)
    d_two = mm("fh,dh->fd", d_pre, mid_full).astype(BF)

    d_two, fc2_far, d_pre = stage(d_two, fc2_far, d_pre)
    fc2_near = scatter_low_near(near_operands(fc2_parts, fc2_far))
    d_two_other = swap_pieces(d_two, PIECES)
    fc1_grad = mm("fd,fh->dh", normed_two_all, d_pre).astype(BF)
    d_branch_all, d_hidden, mid_sums = mid_norm_back(
        d_two, d_two_other, hidden_all, d_out_all, vectors
    )
    d_attended = mm("fd,de->fe", d_branch_all, out_full).astype(BF)
    out_grad = mm("fd,fe->de", d_branch_all, attended).astype(BF)
    mid_parts, mid_ops = scatter_operands(jnp.concatenate([fc1_grad, out_grad], axis=1), at)

    d_attended, mid_ops = stage(d_attended, mid_ops)
    mid_far = scatter_low_across(mid_ops)
    d_proj = attend_back(qkv, log_sums, d_attended, 0, pairs - 1)

    d_proj, mid_far, fc2_near = stage(d_proj, mid_far, fc2_near)
    mid_near = scatter_low_near(near_operands(mid_parts, mid_far))
    fc2_sum = scatter_high_step(high_operands(total_of(fc2_near), 0, at), 0)
    d_qkv, d_sums = attend_back(qkv, log_sums, d_attended, pairs - 1, 1, d_proj)
    qkv_grad = mm("fd,fe->de", normed_all, d_qkv).astype(BF)
    qkv_parts, qkv_ops = scatter_operands(qkv_grad, at)

    qkv_ops, d_qkv, fc2_sum, hidden_act = stage(qkv_ops, d_qkv, fc2_sum, hidden_act)
    qkv_far = scatter_low_across(qkv_ops)
    d_other, mlp_other, mlp_mine = last_terms(d_qkv, first_full, hidden_act, end_full)
    fc2_last = scatter_high_last(fc2_sum, 1, at)

    qkv_far, mid_near, d_other, mlp_other, mlp_mine, fc2_last = stage(
        qkv_far, mid_near, d_other, mlp_other, mlp_mine, fc2_last
    )
    qkv_ops = near_operands(qkv_parts, qkv_far)
    mid_near = after(mid_near, qkv_ops)
    qkv_near = scatter_low_near(qkv_ops)
    mid_sum = scatter_high_step(high_operands(total_of(mid_near), 0, at), 0)
    d_other_got = swap_pieces(d_other, 2)
    input_grad, first_sums = first_norm_back(
        d_qkv, first_full, d_other_got, inputs, d_hidden, vectors
    )
    rows = jnp.concatenate([first_sums, mid_sums], axis=0)
    rows = rows + swap_core(rows)

    mid_sum, qkv_near, rows = stage(mid_sum, qkv_near, rows)
    width = rows.shape[1]
    flat = [rows, jnp.pad(d_sums[:, 0], ((0, 0), (0, width - 3 * PAIR)))]
    flat += [fc1_bias_grad[:, i : i + width] for i in range(0, fc1_bias_grad.shape[1], width)]
    flat = sum_over(jnp.concatenate(flat, axis=0), [1, 2])
    qkv_sum = scatter_high_step(high_operands(total_of(qkv_near), 0, at), 0)
    mlp_got = swap_core(mlp_other)
    mid_last = scatter_high_last(mid_sum, 1, at)

    qkv_sum, flat, mlp_got = stage(qkv_sum, flat, mlp_got)
    outputs = hidden_all[:half] + ((mlp_mine + mlp_got.astype(F32)) + vectors[5:6])
    flat = sum_over(flat, high[:0:-1])
    qkv_out, gains_out, shifts_out, qv_out, bias_out = finish_last(
        (*scatter_high_last(qkv_sum, 1, at), flat, swap_dp(flat, high[0])),
        at["start"],
        [qkv_weight.shape, norm_gains.shape, shifts.shape, qv_bias.shape, fc1_bias.shape],
    )
    mid_last = after(mid_last[0], qkv_sum), mid_last[1]
    (fc2_out,) = finish(finish_ff_kernel, *fc2_last, [(own, hidden_n)], "finish_fc2")
    fc1_out, out_out = finish(
        finish_ff_kernel, *mid_last, [(own, n) for n in (hidden_n, wide)], "finish_mid"
    )
    return (
        outputs[None],
        input_grad[None],
        qkv_out,
        out_out.T,
        fc1_out,
        fc2_out.T,
        gains_out,
        shifts_out,
        qv_out,
        bias_out,
    )


def solution(mesh):
    specs = (
        P("dp", "tensor", None),
        P("dp", "tensor", None),
        P(None, "dp", "tensor"),
        P("tensor", "dp"),
        P("dp", "tensor"),
        P("tensor", "dp"),
        P(None, "dp"),
        P(None, "dp"),
        P(None, "tensor"),
        P("tensor"),
    )
    return jax.shard_map(body, mesh=mesh, in_specs=specs, out_specs=specs, check_vma=False)
```

```python
import functools

import jax
import jax.numpy as jnp
from jax import lax
from jax.experimental import pallas as pl
from jax.experimental.pallas import tpu as pltpu
from jax.sharding import PartitionSpec as P

HEAD = 64
PAIR = 2 * HEAD
ATTEND_VMEM = 20 * 2**20
BACK_VMEM = 24 * 2**20
ROWS_VMEM = 16 * 2**20
PIECES = 2
ROW_BLOCK = 256
COLUMN_BLOCK = 512
ACT_BLOCK = 256
FREE = pl.CostEstimate(flops=0, bytes_accessed=0, transcendentals=0)
EPS = 1e-05
BF = jnp.bfloat16
F32 = jnp.float32


def after(x, *others):
    return lax.optimization_barrier((x, others))[0]


def stage(*values):
    return lax.optimization_barrier(values)


def digits_of(n):
    low = 4 if n % 4 == 0 else n
    found, stride = [(1, low)], low
    while stride < n:
        found.append((stride, 2))
        stride *= 2
    return found


def swap_dp(x, step):
    n = lax.axis_size("dp")
    return lax.ppermute(x, "dp", [(i, i ^ step) for i in range(n)])


def swap_core(x):
    return lax.ppermute(x, "tensor", [(0, 1), (1, 0)])


def position(own):
    n = lax.axis_size("dp")
    me = lax.axis_index("dp")
    bits = [(me >> i) & 1 for i in range(n.bit_length() - 1)]
    low = me & 3
    return {
        "bits": [(me & (1 << i)) != 0 for i in range(len(bits))],
        "low": [low ^ k for k in range(4)],
        "high": [[bit, 1 - bit] for bit in bits[2:]],
        "digit": low.reshape(1),
        "start": (me * own).reshape(1),
    }


def pick(options, bits):
    for bit in bits:
        options = [jnp.where(bit, b, a) for a, b in zip(options[0::2], options[1::2])]
    return options[0]


def place(got, stride, at):
    radix = len(got)
    first = stride.bit_length() - 1
    bits = at["bits"][first : first + radix.bit_length() - 1]
    placed = [pick([got[i ^ m] for m in range(radix)], bits) for i in range(radix)]
    return jnp.stack(placed, axis=1).reshape((-1,) + got[0].shape[1:])


def gather_high_at_once(x, at):
    n = lax.axis_size("dp")
    low = digits_of(n)[0][1]
    stride = n // 4
    cur = place([x[None]] + [swap_dp(x[None], stride * k) for k in range(1, 4)], stride, at)
    while stride > low:
        stride //= 2
        cur = place([cur, swap_dp(cur, stride)], stride, at)
    return cur


def gather_near(cur):
    return swap_dp(cur, 1), swap_dp(cur, 2)


def gather_far(near):
    half = near[0].shape[0] // 2
    return swap_dp(near[0][:half], 2), swap_dp(near[1][half:], 1)


def gather_low(cur):
    return [swap_dp(cur, k) for k in range(1, digits_of(lax.axis_size("dp"))[0][1])]


def rows_kernel(start, mine_ref, *refs):
    sources, out_ref = refs[:-1], refs[-1]
    high, _, _, columns = out_ref.shape
    mine = mine_ref[0]
    here = pl.ds(start, columns)
    for i in range(high):
        for k, source in enumerate(sources[:3]):
            out_ref[i, mine ^ k] = source[i, :, here]
        far = sources[3 + i * (len(sources) - 3) // high]
        out_ref[i, mine ^ 3] = far[i % far.shape[0]]


def all_rows(sources, start, columns, at):
    high, rows, _ = sources[0].shape
    full = pl.pallas_call(
        functools.partial(rows_kernel, start),
        in_specs=[pl.BlockSpec(memory_space=pltpu.SMEM)]
        + [pl.BlockSpec(memory_space=pltpu.VMEM)] * len(sources),
        out_specs=pl.BlockSpec(memory_space=pltpu.VMEM),
        out_shape=jax.ShapeDtypeStruct((high, 4, rows, columns), BF),
        cost_estimate=FREE,
        compiler_params=pltpu.CompilerParams(vmem_limit_bytes=ROWS_VMEM),
        name="all_rows",
    )(at["digit"], *sources)
    return full.reshape(-1, columns)


def part_of(view, index, first=0, count=0):
    sizes = (count or view.shape[0], 1) + view.shape[2:]
    starts = [jnp.int32(first), index] + [jnp.int32(0)] * (view.ndim - 2)
    piece = lax.dynamic_slice(view, starts, sizes, allow_negative_indices=False)
    return piece.reshape(sizes[:1] + sizes[2:])


def total_of(parts):
    total = parts[0].astype(F32)
    for part in parts[1:]:
        total = total + part.astype(F32)
    return total


def scatter_operands(x, at):
    n = lax.axis_size("dp")
    view = x.reshape(n // 4, 4, x.shape[0] // n, x.shape[1])
    half = view.shape[0] // 2
    one, two, across = (
        [part_of(view, index, first, half) for first in (0, half)] for index in at["low"][1:]
    )
    return (part_of(view, at["low"][0]), one, two), across


def scatter_low_across(operands):
    return swap_dp(operands[0], 1), swap_dp(operands[1], 2)


def near_operands(parts, across):
    mine, one, two = parts
    one = jnp.concatenate([one[0], total_of([one[1], across[1]]).astype(BF)], axis=0)
    two = jnp.concatenate([total_of([two[0], across[0]]).astype(BF), two[1]], axis=0)
    return mine, one, two


def scatter_low_near(operands):
    mine, one, two = operands
    return mine, swap_dp(one, 1), swap_dp(two, 2)


def high_operands(cur, index, at):
    view = cur.reshape((-1, 2) + cur.shape[1:])
    kept, sent = (part_of(view, i) for i in at["high"][index])
    return kept, sent.astype(BF)


def scatter_high_step(operands, index):
    stride, _ = digits_of(lax.axis_size("dp"))[1 + index]
    return operands[0] + swap_dp(operands[1], stride).astype(F32)


def scatter_high_last(cur, index, at):
    digits = digits_of(lax.axis_size("dp"))[1:]
    for i in range(index, len(digits) - 1):
        cur = scatter_high_step(high_operands(cur, i, at), i)
    kept, sent = high_operands(cur, len(digits) - 1, at)
    return kept[0], swap_dp(sent, digits[-1][0])[0]


def sum_over(x, steps):
    for step in steps:
        x = x + swap_dp(x, step)
    return x


def swap_pieces(x, count):
    rows = x.shape[0] // count
    return [swap_core(x[i * rows : (i + 1) * rows]) for i in range(count)]


def dot(a, b, ca, cb):
    return lax.dot_general(a, b, (((ca,), (cb,)), ((), ())), preferred_element_type=F32)


def attend_kernel(qkv_ref, *refs):
    out_ref, lse_ref = refs[-2:]
    keys_all = qkv_ref[:, PAIR : 2 * PAIR] * jnp.asarray(HEAD**-0.5, BF)
    values = qkv_ref[:, 2 * PAIR :]
    first = lax.broadcasted_iota(jnp.int32, (1, PAIR), 1) < HEAD
    block = qkv_ref.shape[0] // 2

    @pl.loop(0, 2)
    def _(i):
        rows = pl.ds(pl.multiple_of(i * block, block), block)
        queries = qkv_ref[rows, :PAIR]
        outs, logs = [], []
        for own in (first, ~first):
            here = jnp.where(own, queries, jnp.zeros_like(queries))
            scores = dot(keys_all, here, 1, 1)
            row_max = jnp.max(scores, axis=0, keepdims=True)
            powers = jnp.exp(scores - row_max)
            summed = jnp.sum(powers, axis=0, keepdims=True)
            probs = (powers * (1.0 / summed)).astype(BF)
            outs.append(dot(values, probs, 0, 0))
            logs.append(row_max + jnp.log(summed))
        both = jnp.concatenate([outs[0][:HEAD], outs[1][HEAD:]], axis=0)
        out_ref[rows] = both.T.astype(BF)
        lse_ref[0, :, rows] = jnp.concatenate(logs, axis=0)


def attend(qkv, start, count, kept=()):
    n, width = qkv.shape
    pairs = width // (3 * PAIR)
    return pl.pallas_call(
        attend_kernel,
        grid=(count,),
        in_specs=[pl.BlockSpec((n, 3 * PAIR), lambda p: (0, p + start))]
        + [pl.BlockSpec(memory_space=pl.ANY)] * len(kept),
        out_specs=[
            pl.BlockSpec((n, PAIR), lambda p: (0, p + start)),
            pl.BlockSpec((1, 2, n), lambda p: (p + start, 0, 0)),
        ],
        out_shape=[
            jax.ShapeDtypeStruct((n, pairs * PAIR), BF),
            jax.ShapeDtypeStruct((pairs, 2, n), F32),
        ],
        input_output_aliases={1 + i: i for i in range(len(kept))},
        compiler_params=pltpu.CompilerParams(vmem_limit_bytes=ATTEND_VMEM),
        cost_estimate=FREE,
        name="attend",
    )(qkv, *kept)


def attend_back_kernel(block, qkv_ref, lse_ref, grad_ref, *refs):
    out_ref, sum_ref, d_keys_ref, d_values_ref = refs[-4:]
    n = qkv_ref.shape[0]
    keys_small = qkv_ref[:, PAIR : 2 * PAIR] * jnp.asarray(HEAD**-0.5, BF)
    values = qkv_ref[:, 2 * PAIR :]
    first = lax.broadcasted_iota(jnp.int32, (1, PAIR), 1) < HEAD

    def chunk(here):
        queries = qkv_ref[here, :PAIR]
        grad = grad_ref[here]
        parts = []
        for own in (first, ~first):
            q_here = jnp.where(own, queries, jnp.zeros_like(queries))
            g_here = jnp.where(own, grad, jnp.zeros_like(grad))
            parts.append(
                (q_here, g_here, dot(keys_small, q_here, 1, 1), dot(values, g_here, 1, 1))
            )
        d_q, d_k, d_v = [], [], []
        for head, (q_here, g_here, scores, d_probs) in enumerate(parts):
            probs = jnp.exp(scores - lse_ref[0, head : head + 1, here])
            product = probs * d_probs
            row_sum = jnp.sum(product, axis=0, keepdims=True)
            d_scores = (product - probs * row_sum).astype(BF)
            d_v.append(dot(probs.astype(BF), g_here, 1, 0))
            d_k.append(dot(d_scores, q_here, 1, 0))
            d_q.append(dot(keys_small, d_scores, 0, 0))
        queries_t = jnp.concatenate([d_q[0][:HEAD], d_q[1][HEAD:]], axis=0)
        out_ref[here, :PAIR] = queries_t.T.astype(BF)
        return d_k[0] + d_k[1], d_v[0] + d_v[1]

    def finish(d_keys, d_values):
        out_ref[:, PAIR : 2 * PAIR] = (d_keys * HEAD**-0.5).astype(BF)
        out_ref[:, 2 * PAIR :] = d_values.astype(BF)
        for i in range(0, 3 * PAIR, PAIR):
            here = slice(i, i + PAIR)
            sum_ref[0, :, here] = total_rows(out_ref[:, here].astype(F32))

    if block == n:
        finish(*chunk(slice(None)))
        return

    d_keys_ref[...] = jnp.zeros_like(d_keys_ref)
    d_values_ref[...] = jnp.zeros_like(d_values_ref)

    @pl.loop(0, n // block)
    def _(i):
        d_keys, d_values = chunk(pl.ds(pl.multiple_of(i * block, block), block))
        d_keys_ref[...] += d_keys
        d_values_ref[...] += d_values

    finish(d_keys_ref[...], d_values_ref[...])


def attend_back(qkv, lse, grad, start, count, block, kept=()):
    n, width = qkv.shape
    pairs = width // (3 * PAIR)
    return pl.pallas_call(
        functools.partial(attend_back_kernel, block),
        grid=(count,),
        in_specs=[
            pl.BlockSpec((n, 3 * PAIR), lambda p: (0, p + start)),
            pl.BlockSpec((1, 2, n), lambda p: (p + start, 0, 0)),
            pl.BlockSpec((n, PAIR), lambda p: (0, p + start)),
        ]
        + [pl.BlockSpec(memory_space=pl.ANY)] * len(kept),
        out_specs=[
            pl.BlockSpec((n, 3 * PAIR), lambda p: (0, p + start)),
            pl.BlockSpec((1, 1, 3 * PAIR), lambda p: (p + start, 0, 0)),
        ],
        out_shape=[
            jax.ShapeDtypeStruct((n, width), BF),
            jax.ShapeDtypeStruct((pairs, 1, 3 * PAIR), F32),
        ],
        scratch_shapes=[pltpu.VMEM((n, PAIR), F32)] * 2,
        input_output_aliases={3 + i: i for i in range(len(kept))},
        compiler_params=pltpu.CompilerParams(vmem_limit_bytes=BACK_VMEM),
        cost_estimate=FREE,
        name="attend_back",
    )(qkv, lse, grad, *kept)


def rows_call(kernel, out_shape, name, scratch=()):
    return pl.pallas_call(
        kernel,
        out_shape=out_shape,
        scratch_shapes=scratch,
        cost_estimate=FREE,
        compiler_params=pltpu.CompilerParams(vmem_limit_bytes=ROWS_VMEM),
        name=name,
    )


def each_block(rows, step):
    @pl.loop(0, rows // ROW_BLOCK)
    def _(i):
        step(pl.ds(pl.multiple_of(i * ROW_BLOCK, ROW_BLOCK), ROW_BLOCK))


def pack_kernel(qkv_ref, out_ref, gains_ref, shifts_ref, packed_ref, small_ref):
    rows, wide = out_ref.shape
    for pair in range(wide // PAIR):
        for i in range(3):
            start = (3 * pair + i) * PAIR
            packed_ref[:, start : start + PAIR] = qkv_ref[i, :, pair * PAIR : (pair + 1) * PAIR]
    packed_ref[:, 3 * wide : 4 * wide] = out_ref[...]
    small_ref[...] = jnp.zeros_like(small_ref)
    small_ref[0:2, :rows] = gains_ref[...].astype(F32)
    small_ref[2:6, :rows] = shifts_ref[...].astype(F32)
    packed_ref[:, 4 * wide :] = jnp.zeros_like(packed_ref[:, 4 * wide :])
    packed_ref[:, 4 * wide : 4 * wide + 8] = small_ref[...].T[:rows].astype(BF)


def pack(qkv_weight, out_weight, gains, shifts):
    rows, wide = out_weight.shape
    args = (qkv_weight, out_weight, gains, shifts)
    shape = (rows, 4 * wide + PAIR)
    return pl.pallas_call(
        pack_kernel,
        out_shape=jax.ShapeDtypeStruct(shape, BF),
        scratch_shapes=[pltpu.VMEM((8, PAIR), F32)],
        cost_estimate=FREE,
        compiler_params=pltpu.CompilerParams(vmem_limit_bytes=4 * 2**20),
        name="pack",
    )(*args)


def finish_ff_kernel(kept_ref, got_ref, *out_refs):
    total = kept_ref[...] + got_ref[...].astype(F32)
    start = 0
    for out_ref in out_refs:
        columns = out_ref.shape[1]
        out_ref[...] = total[:, start : start + columns]
        start += columns


def finish_last_kernel(
    qkv_ref, qkv_got_ref, sums_ref, sums_got_ref, start_ref, *out_refs
):
    grad_ref, gains_ref, shifts_ref, qv_ref, bias_ref = out_refs
    pairs = qv_ref.shape[1] // PAIR
    grad = qkv_ref[...] + qkv_got_ref[...].astype(F32)
    for pair in range(pairs):
        for i in range(3):
            start = (3 * pair + i) * PAIR
            grad_ref[i, :, pair * PAIR : (pair + 1) * PAIR] = grad[:, start : start + PAIR]
    own = gains_ref.shape[1]
    total = sums_ref[...] + sums_got_ref[...]
    columns = total.shape[1]
    rows = pltpu.roll(total[:8], columns - start_ref[0], 1)[:, :own]
    gains_ref[...] = jnp.concatenate([rows[0:1], rows[2:3]], axis=0)
    shifts_ref[...] = jnp.concatenate([rows[1:2], rows[3:6]], axis=0)
    for pair in range(pairs):
        for i in range(2):
            here = slice(2 * i * PAIR, (2 * i + 1) * PAIR)
            qv_ref[i : i + 1, pair * PAIR : (pair + 1) * PAIR] = total[6 + pair : 7 + pair, here]
    for i in range(total.shape[0] - 6 - pairs):
        bias_ref[pl.ds(i * columns, columns)] = total[6 + pairs + i]


def finish_last(args, start, shapes):
    return pl.pallas_call(
        finish_last_kernel,
        in_specs=[pl.BlockSpec(memory_space=pltpu.VMEM)] * 4
        + [pl.BlockSpec(memory_space=pltpu.SMEM)],
        out_specs=[pl.BlockSpec(memory_space=pltpu.VMEM)] * 5,
        out_shape=[jax.ShapeDtypeStruct(x, F32) for x in shapes],
        cost_estimate=FREE,
        compiler_params=pltpu.CompilerParams(vmem_limit_bytes=4 * 2**20),
        name="finish_last",
    )(*args, start)


def finish(kernel, kept, got, shapes, name):
    return pl.pallas_call(
        kernel,
        out_shape=[jax.ShapeDtypeStruct(x, F32) for x in shapes],
        cost_estimate=FREE,
        compiler_params=pltpu.CompilerParams(vmem_limit_bytes=8 * 2**20),
        name=name,
    )(kept, got)


def join_kernel(mine_ref, other_ref, out_ref):
    half = mine_ref.shape[0]
    out_ref[:half] = mine_ref[...]
    out_ref[half:] = other_ref[...]


def join(mine, other):
    rows, columns = mine.shape
    shape = jax.ShapeDtypeStruct((2 * rows, columns), mine.dtype)
    return rows_call(join_kernel, shape, "join")(mine, other)


def standardized(x):
    center = x - jnp.mean(x, axis=-1, keepdims=True)
    inv_std = lax.rsqrt(jnp.mean(center * center, axis=-1, keepdims=True) + EPS)
    return center * inv_std, inv_std


def project_kernel(x_ref, weight_ref, bias_ref, normed_ref, qkv_ref, vectors_ref):
    width = qkv_ref.shape[1]
    small = weight_ref.shape[1] - PAIR
    vectors = weight_ref[:, small:].astype(F32).T[:8]
    vectors_ref[...] = vectors
    qv = bias_ref[...].astype(F32)
    none = jnp.zeros((1, PAIR), F32)
    bias = []
    for start in range(0, qv.shape[1], PAIR):
        bias += [qv[0:1, start : start + PAIR], none, qv[1:2, start : start + PAIR]]
    bias = jnp.concatenate(bias, axis=1)

    def step(here):
        unit, _ = standardized(x_ref[here].astype(F32))
        normed = (unit * vectors_ref[0:1] + vectors_ref[2:3]).astype(BF)
        normed_ref[here] = normed
        qkv_ref[here] = (dot(normed, weight_ref[:, :width], 1, 0) + bias).astype(BF)

    each_block(x_ref.shape[0], step)


def project(x, first_full, bias, width):
    rows, columns = x.shape
    shapes = [
        jax.ShapeDtypeStruct((rows, columns), BF),
        jax.ShapeDtypeStruct((rows, width), BF),
        jax.ShapeDtypeStruct((8, columns), F32),
    ]
    return rows_call(project_kernel, shapes, "project")(x, first_full, bias)


def halves_of(refs, others):
    half = others[0].shape[0]
    return [
        ([ref.at[pl.ds(i * half, half)] for ref in refs], others[1 - i]) for i in range(PIECES)
    ]


def mid_norm_kernel(x_ref, mine_ref, vectors_ref, *refs):
    others, (hidden_ref, normed_ref) = refs[:PIECES], refs[PIECES:]
    for refs, other_ref in halves_of((x_ref, mine_ref, hidden_ref, normed_ref), others):
        frames, mine, hidden_half, normed_half = refs

        def step(here):
            branch = mine[here].astype(F32) + other_ref[here].astype(F32)
            hidden = frames[here].astype(F32) + (branch + vectors_ref[3:4])
            hidden_half[here] = hidden
            unit, _ = standardized(hidden)
            normed_half[here] = (unit * vectors_ref[1:2] + vectors_ref[4:5]).astype(BF)

        each_block(other_ref.shape[0], step)


def mid_norm(x, mine, others, vectors):
    shapes = [jax.ShapeDtypeStruct(x.shape, t) for t in (F32, BF)]
    return rows_call(mid_norm_kernel, shapes, "mid_norm")(x, mine, vectors, *others)


def act_kernel(x_ref, weight_ref, bias_ref, act_ref, slope_ref, row_ref):
    row_ref[...] = bias_ref[...].astype(F32).reshape(1, bias_ref.shape[0])

    @pl.loop(0, act_ref.shape[1] // ACT_BLOCK)
    def _(i):
        here = pl.ds(pl.multiple_of(i * ACT_BLOCK, ACT_BLOCK), ACT_BLOCK)
        pre = dot(x_ref[...], weight_ref[:, here], 1, 0) + row_ref[:, here]
        cdf = 0.5 * (1.0 + lax.erf(pre * 0.5**0.5))
        act_ref[:, here] = (pre * cdf).astype(BF)
        slope = cdf + pre * jnp.exp(-0.5 * pre * pre) * 0.3989422804014327
        slope_ref[:, here] = slope.astype(BF)


def act(x, weight, bias):
    shape = jax.ShapeDtypeStruct((x.shape[0], weight.shape[1]), BF)
    scratch = [pltpu.VMEM((1, bias.shape[0]), F32)]
    return rows_call(act_kernel, [shape, shape], "act", scratch)(x, weight, bias)


def act_back_kernel(d_out_ref, weight_ref, slope_ref, d_pre_ref, sums_ref):
    @pl.loop(0, d_pre_ref.shape[1] // COLUMN_BLOCK)
    def _(i):
        here = pl.ds(pl.multiple_of(i * COLUMN_BLOCK, COLUMN_BLOCK), COLUMN_BLOCK)
        d_act = dot(d_out_ref[...], weight_ref[:, here], 1, 0)
        d_pre = (d_act * slope_ref[:, here].astype(F32)).astype(BF)
        d_pre_ref[:, here] = d_pre
        sums_ref[:, here] = total_rows(d_pre.astype(F32))


def act_back(d_out, weight, slope):
    shapes = [jax.ShapeDtypeStruct(slope.shape, BF), jax.ShapeDtypeStruct((1, slope.shape[1]), F32)]
    return rows_call(act_back_kernel, shapes, "act_back")(d_out, weight, slope)


def norm_back(unit, inv_std, gain, grad):
    scaled = grad * gain
    return inv_std * (
        scaled
        - jnp.mean(scaled, axis=-1, keepdims=True)
        - unit * jnp.mean(scaled * unit, axis=-1, keepdims=True)
    )


def total_rows(x):
    return jnp.sum(x, axis=0, keepdims=True)


def mid_norm_back_kernel(mine_ref, hidden_ref, d_out_ref, vectors_ref, *refs):
    others, (branch_ref, d_hidden_ref, sums_ref) = refs[:PIECES], refs[PIECES:]
    sums_ref[...] = jnp.zeros_like(sums_ref)
    halves = halves_of((mine_ref, hidden_ref, d_out_ref, branch_ref), others)
    for i, (refs, other_ref) in enumerate(halves):
        mine, hidden, d_outs, branch = refs

        def step(here):
            grad = mine[here].astype(F32) + other_ref[here].astype(F32)
            unit, inv_std = standardized(hidden[here])
            d_out = d_outs[here].astype(F32)
            d_hidden = d_out + norm_back(unit, inv_std, vectors_ref[1:2], grad)
            d_branch = d_hidden.astype(BF)
            branch[here] = d_branch
            if i == 0:
                d_hidden_ref[here] = d_hidden
                terms = (grad * unit, d_branch.astype(F32), grad, d_out)
                sums_ref[...] += jnp.concatenate([total_rows(x) for x in terms], axis=0)

        each_block(other_ref.shape[0], step)


def mid_norm_back(mine, others, hidden, d_out, vectors):
    rows, columns = hidden.shape
    shapes = [
        jax.ShapeDtypeStruct((rows, columns), BF),
        jax.ShapeDtypeStruct((rows // 2, columns), F32),
        jax.ShapeDtypeStruct((4, columns), F32),
    ]
    return rows_call(mid_norm_back_kernel, shapes, "mid_norm_back")(
        mine, hidden, d_out, vectors, *others
    )


def first_norm_back_kernel(
    qkv_ref, weight_ref, x_ref, d_hidden_ref, vectors_ref, first_ref, second_ref, grad_ref, sums_ref
):
    width = qkv_ref.shape[1]
    sums_ref[...] = jnp.zeros_like(sums_ref)

    @pl.loop(0, x_ref.shape[0] // ROW_BLOCK)
    def _(i):
        here = pl.ds(pl.multiple_of(i * ROW_BLOCK, ROW_BLOCK), ROW_BLOCK)
        other = jnp.where(i == 0, first_ref[...], second_ref[...]).astype(F32)
        grad = dot(qkv_ref[here], weight_ref[:, :width], 1, 1) + other
        unit, inv_std = standardized(x_ref[here].astype(F32))
        grad_ref[here] = d_hidden_ref[here] + norm_back(unit, inv_std, vectors_ref[0:1], grad)
        sums_ref[0:1] += total_rows(grad * unit)
        sums_ref[1:2] += total_rows(grad)


def first_norm_back(d_qkv, first_full, others, x, d_hidden, vectors):
    rows, columns = x.shape
    shapes = [jax.ShapeDtypeStruct((n, columns), F32) for n in (rows, 2)]
    return rows_call(first_norm_back_kernel, shapes, "first_norm_back")(
        d_qkv, first_full, x, d_hidden, vectors, *others
    )


def last_terms_kernel(d_qkv_ref, first_ref, act_ref, end_ref, d_other_ref, other_ref, mine_ref):
    half, columns = mine_ref.shape
    width = d_qkv_ref.shape[1]
    others = pl.ds(half, half)
    d_qkv, act_other = d_qkv_ref.at[others], act_ref.at[others]

    def step(here):
        d_other = dot(d_qkv[here], first_ref[:, :width], 1, 1)
        d_other_ref[here] = d_other.astype(BF)
        other_ref[here] = dot(act_other[here], end_ref[...], 1, 1).astype(BF)
        mine_ref[here] = dot(act_ref[here], end_ref[...], 1, 1)

    each_block(half, step)


def last_terms(d_qkv, first_full, hidden_act, end_full):
    shape = (d_qkv.shape[0] // 2, end_full.shape[0])
    shapes = [jax.ShapeDtypeStruct(shape, t) for t in (BF, BF, F32)]
    return rows_call(last_terms_kernel, shapes, "last_terms")(
        d_qkv, first_full, hidden_act, end_full
    )


def mm(spec, a, b):
    return jnp.einsum(spec, a, b, preferred_element_type=F32)


def body(
    inputs,
    cotangent,
    qkv_weight,
    out_weight,
    fc1_weight,
    fc2_weight,
    norm_gains,
    shifts,
    qv_bias,
    fc1_bias,
):
    inputs = inputs[0]
    cotangent = cotangent[0]
    own = norm_gains.shape[1]
    wide = qkv_weight.shape[2]
    pairs = wide // PAIR

    first_own = pack(qkv_weight, out_weight.T, norm_gains, shifts)
    at = position(own)
    half = inputs.shape[0]
    hidden_n = fc1_weight.shape[1]
    high = [stride for stride, _ in reversed(digits_of(lax.axis_size("dp"))[1:])]
    first_own, at = stage(first_own, at)
    first_part = gather_high_at_once(first_own, at)
    inputs_other = swap_core(inputs)

    ff_own = jnp.concatenate([fc1_weight, fc2_weight.T], axis=1)

    first_part, inputs_other, ff_part = stage(first_part, inputs_other, ff_own[None])
    first_near = gather_near(first_part)
    inputs_all = join(inputs, inputs_other)
    for stride in high:
        ff_part = place([ff_part, swap_dp(ff_part, stride)], stride, at)

    first_part, first_near, inputs_all = stage(first_part, first_near, inputs_all)
    first_far = gather_far(first_near)

    first_part, first_near, first_far, ff_part = stage(first_part, first_near, first_far, ff_part)
    ff_near = gather_near(ff_part)
    cotangent_other = swap_core(after(cotangent, first_part))
    first_full = all_rows([first_part, *first_near, *first_far], 0, first_part.shape[2], at)
    out_full = first_full[:, 3 * wide : 4 * wide]
    normed_all, qkv, vectors = project(inputs_all, first_full, qv_bias, 3 * wide)
    attended, log_sums = attend(qkv, 0, pairs)
    branch = mm("fe,de->fd", attended, out_full).astype(BF)
    branch_other = swap_pieces(branch, PIECES)
    hidden_all, normed_two_all = mid_norm(inputs_all, branch, branch_other, vectors)

    ff_part, ff_near, normed_two_all, cotangent_other = stage(
        ff_part, ff_near, normed_two_all, cotangent_other
    )
    mid_far = gather_far([x[:, :, :hidden_n] for x in ff_near])
    d_out_all = join(cotangent, cotangent_other)

    ff_part, ff_near, mid_far, d_out_all = stage(ff_part, ff_near, mid_far, d_out_all)
    end_far = gather_far([x[:, :, hidden_n:] for x in ff_near])
    mid_full = all_rows([ff_part, *ff_near, *mid_far], 0, hidden_n, at)
    hidden_act, slope = act(normed_two_all, mid_full, fc1_bias)
    hidden_act, slope, d_out_all = stage(hidden_act, slope, d_out_all)
    fc2_grad = mm("fd,fh->dh", d_out_all, hidden_act).astype(BF)
    fc2_parts, fc2_ops = scatter_operands(fc2_grad, at)

    ff_part, ff_near, end_far, d_out_all, fc2_ops = stage(
        ff_part, ff_near, end_far, d_out_all, fc2_ops
    )
    fc2_far = scatter_low_across(fc2_ops)
    end_full = all_rows([ff_part, *ff_near, *end_far], hidden_n, hidden_n, at)
    d_pre, fc1_bias_grad = act_back(d_out_all, end_full, slope)
    d_two = mm("fh,dh->fd", d_pre, mid_full).astype(BF)

    d_two, fc2_far, d_pre = stage(d_two, fc2_far, d_pre)
    fc2_near = scatter_low_near(near_operands(fc2_parts, fc2_far))
    d_two_other = swap_pieces(d_two, PIECES)
    fc1_grad = mm("fd,fh->dh", normed_two_all, d_pre).astype(BF)
    d_branch_all, d_hidden, mid_sums = mid_norm_back(
        d_two, d_two_other, hidden_all, d_out_all, vectors
    )
    d_attended = mm("fd,de->fe", d_branch_all, out_full).astype(BF)
    out_grad = mm("fd,fe->de", d_branch_all, attended).astype(BF)
    mid_parts, mid_ops = scatter_operands(jnp.concatenate([fc1_grad, out_grad], axis=1), at)

    d_attended, mid_ops = stage(d_attended, mid_ops)
    mid_far = scatter_low_across(mid_ops)
    d_proj = attend_back(qkv, log_sums, d_attended, 0, pairs - 1, 2 * half)

    d_proj, mid_far, fc2_near = stage(d_proj, mid_far, fc2_near)
    mid_near = scatter_low_near(near_operands(mid_parts, mid_far))
    fc2_sum = scatter_high_step(high_operands(total_of(fc2_near), 0, at), 0)
    d_qkv, d_sums = attend_back(qkv, log_sums, d_attended, pairs - 1, 1, half, d_proj)
    qkv_grad = mm("fd,fe->de", normed_all, d_qkv).astype(BF)
    qkv_parts, qkv_ops = scatter_operands(qkv_grad, at)

    qkv_ops, d_qkv, fc2_sum, hidden_act = stage(qkv_ops, d_qkv, fc2_sum, hidden_act)
    qkv_far = scatter_low_across(qkv_ops)
    d_other, mlp_other, mlp_mine = last_terms(d_qkv, first_full, hidden_act, end_full)
    fc2_last = scatter_high_last(fc2_sum, 1, at)

    qkv_far, mid_near, d_other, mlp_other, mlp_mine, fc2_last = stage(
        qkv_far, mid_near, d_other, mlp_other, mlp_mine, fc2_last
    )
    qkv_ops = near_operands(qkv_parts, qkv_far)
    mid_near = after(mid_near, qkv_ops)
    qkv_near = scatter_low_near(qkv_ops)
    mid_sum = scatter_high_step(high_operands(total_of(mid_near), 0, at), 0)
    d_other_got = swap_pieces(d_other, 2)
    input_grad, first_sums = first_norm_back(
        d_qkv, first_full, d_other_got, inputs, d_hidden, vectors
    )
    rows = jnp.concatenate([first_sums, mid_sums], axis=0)
    rows = rows + swap_core(rows)

    mid_sum, qkv_near, rows = stage(mid_sum, qkv_near, rows)
    width = rows.shape[1]
    flat = [rows, jnp.pad(d_sums[:, 0], ((0, 0), (0, width - 3 * PAIR)))]
    flat += [fc1_bias_grad[:, i : i + width] for i in range(0, fc1_bias_grad.shape[1], width)]
    flat = sum_over(jnp.concatenate(flat, axis=0), [1, 2])
    qkv_sum = scatter_high_step(high_operands(total_of(qkv_near), 0, at), 0)
    mlp_got = swap_core(mlp_other)
    mid_last = scatter_high_last(mid_sum, 1, at)

    qkv_sum, flat, mlp_got = stage(qkv_sum, flat, mlp_got)
    outputs = hidden_all[:half] + ((mlp_mine + mlp_got.astype(F32)) + vectors[5:6])
    flat = sum_over(flat, high[:0:-1])
    qkv_out, gains_out, shifts_out, qv_out, bias_out = finish_last(
        (*scatter_high_last(qkv_sum, 1, at), flat, swap_dp(flat, high[0])),
        at["start"],
        [qkv_weight.shape, norm_gains.shape, shifts.shape, qv_bias.shape, fc1_bias.shape],
    )
    mid_last = after(mid_last[0], qkv_sum), mid_last[1]
    (fc2_out,) = finish(finish_ff_kernel, *fc2_last, [(own, hidden_n)], "finish_fc2")
    fc1_out, out_out = finish(
        finish_ff_kernel, *mid_last, [(own, n) for n in (hidden_n, wide)], "finish_mid"
    )
    return (
        outputs[None],
        input_grad[None],
        qkv_out,
        out_out.T,
        fc1_out,
        fc2_out.T,
        gains_out,
        shifts_out,
        qv_out,
        bias_out,
    )


def solution(mesh):
    specs = (
        P("dp", "tensor", None),
        P("dp", "tensor", None),
        P(None, "dp", "tensor"),
        P("tensor", "dp"),
        P("dp", "tensor"),
        P("tensor", "dp"),
        P(None, "dp"),
        P(None, "dp"),
        P(None, "tensor"),
        P("tensor"),
    )
    return jax.shard_map(body, mesh=mesh, in_specs=specs, out_specs=specs, check_vma=False)
```

```python
import functools

import jax
import jax.numpy as jnp
from jax import lax
from jax.experimental import pallas as pl
from jax.experimental.pallas import tpu as pltpu
from jax.sharding import PartitionSpec as P

HEAD = 64
PAIR = 2 * HEAD
ATTEND_VMEM = 20 * 2**20
BACK_VMEM = 24 * 2**20
ROWS_VMEM = 16 * 2**20
PIECES = 2
ROW_BLOCK = 256
COLUMN_BLOCK = 512
ACT_BLOCK = 256
FREE = pl.CostEstimate(flops=0, bytes_accessed=0, transcendentals=0)
EPS = 1e-05
BF = jnp.bfloat16
F32 = jnp.float32


def after(x, *others):
    return lax.optimization_barrier((x, others))[0]


def stage(*values):
    return lax.optimization_barrier(values)


def digits_of(n):
    low = 4 if n % 4 == 0 else n
    found, stride = [(1, low)], low
    while stride < n:
        found.append((stride, 2))
        stride *= 2
    return found


def swap_dp(x, step):
    n = lax.axis_size("dp")
    return lax.ppermute(x, "dp", [(i, i ^ step) for i in range(n)])


def swap_core(x):
    return lax.ppermute(x, "tensor", [(0, 1), (1, 0)])


def position(own):
    n = lax.axis_size("dp")
    me = lax.axis_index("dp")
    bits = [(me >> i) & 1 for i in range(n.bit_length() - 1)]
    low = me & 3
    return {
        "bits": [(me & (1 << i)) != 0 for i in range(len(bits))],
        "low": [low ^ k for k in range(4)],
        "high": [[bit, 1 - bit] for bit in bits[2:]],
        "digit": low.reshape(1),
        "start": (me * own).reshape(1),
    }


def pick(options, bits):
    for bit in bits:
        options = [jnp.where(bit, b, a) for a, b in zip(options[0::2], options[1::2])]
    return options[0]


def place(got, stride, at):
    radix = len(got)
    first = stride.bit_length() - 1
    bits = at["bits"][first : first + radix.bit_length() - 1]
    placed = [pick([got[i ^ m] for m in range(radix)], bits) for i in range(radix)]
    return jnp.stack(placed, axis=1).reshape((-1,) + got[0].shape[1:])


def gather_high_at_once(x, at):
    n = lax.axis_size("dp")
    low = digits_of(n)[0][1]
    stride = n // 4
    cur = place([x[None]] + [swap_dp(x[None], stride * k) for k in range(1, 4)], stride, at)
    while stride > low:
        stride //= 2
        cur = place([cur, swap_dp(cur, stride)], stride, at)
    return cur


def gather_near(cur):
    return swap_dp(cur, 1), swap_dp(cur, 2)


def gather_far(near):
    half = near[0].shape[0] // 2
    return swap_dp(near[0][:half], 2), swap_dp(near[1][half:], 1)


def gather_low(cur):
    return [swap_dp(cur, k) for k in range(1, digits_of(lax.axis_size("dp"))[0][1])]


def rows_kernel(start, mine_ref, *refs):
    sources, out_ref = refs[:-1], refs[-1]
    high, _, _, columns = out_ref.shape
    mine = mine_ref[0]
    here = pl.ds(start, columns)
    for i in range(high):
        for k, source in enumerate(sources[:3]):
            out_ref[i, mine ^ k] = source[i, :, here]
        far = sources[3 + i * (len(sources) - 3) // high]
        out_ref[i, mine ^ 3] = far[i % far.shape[0]]


def all_rows(sources, start, columns, at):
    high, rows, _ = sources[0].shape
    full = pl.pallas_call(
        functools.partial(rows_kernel, start),
        in_specs=[pl.BlockSpec(memory_space=pltpu.SMEM)]
        + [pl.BlockSpec(memory_space=pltpu.VMEM)] * len(sources),
        out_specs=pl.BlockSpec(memory_space=pltpu.VMEM),
        out_shape=jax.ShapeDtypeStruct((high, 4, rows, columns), BF),
        cost_estimate=FREE,
        compiler_params=pltpu.CompilerParams(vmem_limit_bytes=ROWS_VMEM),
        name="all_rows",
    )(at["digit"], *sources)
    return full.reshape(-1, columns)


def part_of(view, index, first=0, count=0):
    sizes = (count or view.shape[0], 1) + view.shape[2:]
    starts = [jnp.int32(first), index] + [jnp.int32(0)] * (view.ndim - 2)
    piece = lax.dynamic_slice(view, starts, sizes, allow_negative_indices=False)
    return piece.reshape(sizes[:1] + sizes[2:])


def total_of(parts):
    total = parts[0].astype(F32)
    for part in parts[1:]:
        total = total + part.astype(F32)
    return total


def scatter_operands(x, at):
    n = lax.axis_size("dp")
    view = x.reshape(n // 4, 4, x.shape[0] // n, x.shape[1])
    half = view.shape[0] // 2
    one, two, across = (
        [part_of(view, index, first, half) for first in (0, half)] for index in at["low"][1:]
    )
    return (part_of(view, at["low"][0]), one, two), across


def scatter_low_across(operands):
    return swap_dp(operands[0], 1), swap_dp(operands[1], 2)


def near_operands(parts, across):
    mine, one, two = parts
    one = jnp.concatenate([one[0], total_of([one[1], across[1]]).astype(BF)], axis=0)
    two = jnp.concatenate([total_of([two[0], across[0]]).astype(BF), two[1]], axis=0)
    return mine, one, two


def scatter_low_near(operands):
    mine, one, two = operands
    return mine, swap_dp(one, 1), swap_dp(two, 2)


def high_operands(cur, index, at):
    view = cur.reshape((-1, 2) + cur.shape[1:])
    kept, sent = (part_of(view, i) for i in at["high"][index])
    return kept, sent.astype(BF)


def scatter_high_step(operands, index):
    stride, _ = digits_of(lax.axis_size("dp"))[1 + index]
    return operands[0] + swap_dp(operands[1], stride).astype(F32)


def scatter_high_last(cur, index, at):
    digits = digits_of(lax.axis_size("dp"))[1:]
    for i in range(index, len(digits) - 1):
        cur = scatter_high_step(high_operands(cur, i, at), i)
    kept, sent = high_operands(cur, len(digits) - 1, at)
    return kept[0], swap_dp(sent, digits[-1][0])[0]


def sum_over(x, steps):
    for step in steps:
        x = x + swap_dp(x, step)
    return x


def swap_pieces(x, count):
    rows = x.shape[0] // count
    return [swap_core(x[i * rows : (i + 1) * rows]) for i in range(count)]


def dot(a, b, ca, cb):
    return lax.dot_general(a, b, (((ca,), (cb,)), ((), ())), preferred_element_type=F32)


def attend_kernel(qkv_ref, *refs):
    out_ref, lse_ref = refs[-2:]
    keys_all = qkv_ref[:, PAIR : 2 * PAIR] * jnp.asarray(HEAD**-0.5, BF)
    values = qkv_ref[:, 2 * PAIR :]
    first = lax.broadcasted_iota(jnp.int32, (1, PAIR), 1) < HEAD
    block = qkv_ref.shape[0] // 2

    @pl.loop(0, 2)
    def _(i):
        rows = pl.ds(pl.multiple_of(i * block, block), block)
        queries = qkv_ref[rows, :PAIR]
        outs, logs = [], []
        for own in (first, ~first):
            here = jnp.where(own, queries, jnp.zeros_like(queries))
            scores = dot(keys_all, here, 1, 1)
            row_max = jnp.max(scores, axis=0, keepdims=True)
            powers = jnp.exp(scores - row_max)
            summed = jnp.sum(powers, axis=0, keepdims=True)
            probs = (powers * (1.0 / summed)).astype(BF)
            outs.append(dot(values, probs, 0, 0))
            logs.append(row_max + jnp.log(summed))
        both = jnp.concatenate([outs[0][:HEAD], outs[1][HEAD:]], axis=0)
        out_ref[rows] = both.T.astype(BF)
        lse_ref[0, :, rows] = jnp.concatenate(logs, axis=0)


def attend(qkv, start, count, kept=()):
    n, width = qkv.shape
    pairs = width // (3 * PAIR)
    return pl.pallas_call(
        attend_kernel,
        grid=(count,),
        in_specs=[pl.BlockSpec((n, 3 * PAIR), lambda p: (0, p + start))]
        + [pl.BlockSpec(memory_space=pl.ANY)] * len(kept),
        out_specs=[
            pl.BlockSpec((n, PAIR), lambda p: (0, p + start)),
            pl.BlockSpec((1, 2, n), lambda p: (p + start, 0, 0)),
        ],
        out_shape=[
            jax.ShapeDtypeStruct((n, pairs * PAIR), BF),
            jax.ShapeDtypeStruct((pairs, 2, n), F32),
        ],
        input_output_aliases={1 + i: i for i in range(len(kept))},
        compiler_params=pltpu.CompilerParams(vmem_limit_bytes=ATTEND_VMEM),
        cost_estimate=FREE,
        name="attend",
    )(qkv, *kept)


def attend_back_kernel(block, qkv_ref, lse_ref, grad_ref, *refs):
    out_ref, sum_ref, d_keys_ref, d_values_ref = refs[-4:]
    n = qkv_ref.shape[0]
    keys_small = qkv_ref[:, PAIR : 2 * PAIR] * jnp.asarray(HEAD**-0.5, BF)
    values = qkv_ref[:, 2 * PAIR :]
    first = lax.broadcasted_iota(jnp.int32, (1, PAIR), 1) < HEAD

    def chunk(here):
        queries = qkv_ref[here, :PAIR]
        grad = grad_ref[here]
        parts = []
        for own in (first, ~first):
            q_here = jnp.where(own, queries, jnp.zeros_like(queries))
            g_here = jnp.where(own, grad, jnp.zeros_like(grad))
            parts.append(
                (q_here, g_here, dot(keys_small, q_here, 1, 1), dot(values, g_here, 1, 1))
            )
        d_q, d_k, d_v = [], [], []
        for head, (q_here, g_here, scores, d_probs) in enumerate(parts):
            probs = jnp.exp(scores - lse_ref[0, head : head + 1, here])
            product = probs * d_probs
            row_sum = jnp.sum(product, axis=0, keepdims=True)
            d_scores = (product - probs * row_sum).astype(BF)
            d_v.append(dot(probs.astype(BF), g_here, 1, 0))
            d_k.append(dot(d_scores, q_here, 1, 0))
            d_q.append(dot(keys_small, d_scores, 0, 0))
        queries_t = jnp.concatenate([d_q[0][:HEAD], d_q[1][HEAD:]], axis=0)
        out_ref[here, :PAIR] = queries_t.T.astype(BF)
        return d_k[0] + d_k[1], d_v[0] + d_v[1]

    def finish(d_keys, d_values):
        out_ref[:, PAIR : 2 * PAIR] = (d_keys * HEAD**-0.5).astype(BF)
        out_ref[:, 2 * PAIR :] = d_values.astype(BF)
        for i in range(0, 3 * PAIR, PAIR):
            here = slice(i, i + PAIR)
            sum_ref[0, :, here] = total_rows(out_ref[:, here].astype(F32))

    if block == n:
        finish(*chunk(slice(None)))
        return

    d_keys_ref[...] = jnp.zeros_like(d_keys_ref)
    d_values_ref[...] = jnp.zeros_like(d_values_ref)

    @pl.loop(0, n // block)
    def _(i):
        d_keys, d_values = chunk(pl.ds(pl.multiple_of(i * block, block), block))
        d_keys_ref[...] += d_keys
        d_values_ref[...] += d_values

    finish(d_keys_ref[...], d_values_ref[...])


def attend_back(qkv, lse, grad, start, count, block, kept=()):
    n, width = qkv.shape
    pairs = width // (3 * PAIR)
    return pl.pallas_call(
        functools.partial(attend_back_kernel, block),
        grid=(count,),
        in_specs=[
            pl.BlockSpec((n, 3 * PAIR), lambda p: (0, p + start)),
            pl.BlockSpec((1, 2, n), lambda p: (p + start, 0, 0)),
            pl.BlockSpec((n, PAIR), lambda p: (0, p + start)),
        ]
        + [pl.BlockSpec(memory_space=pl.ANY)] * len(kept),
        out_specs=[
            pl.BlockSpec((n, 3 * PAIR), lambda p: (0, p + start)),
            pl.BlockSpec((1, 1, 3 * PAIR), lambda p: (p + start, 0, 0)),
        ],
        out_shape=[
            jax.ShapeDtypeStruct((n, width), BF),
            jax.ShapeDtypeStruct((pairs, 1, 3 * PAIR), F32),
        ],
        scratch_shapes=[pltpu.VMEM((n, PAIR), F32)] * 2,
        input_output_aliases={3 + i: i for i in range(len(kept))},
        compiler_params=pltpu.CompilerParams(vmem_limit_bytes=BACK_VMEM),
        cost_estimate=FREE,
        name="attend_back",
    )(qkv, lse, grad, *kept)


def rows_call(kernel, out_shape, name, scratch=()):
    return pl.pallas_call(
        kernel,
        out_shape=out_shape,
        scratch_shapes=scratch,
        cost_estimate=FREE,
        compiler_params=pltpu.CompilerParams(vmem_limit_bytes=ROWS_VMEM),
        name=name,
    )


def each_block(rows, step):
    @pl.loop(0, rows // ROW_BLOCK)
    def _(i):
        step(pl.ds(pl.multiple_of(i * ROW_BLOCK, ROW_BLOCK), ROW_BLOCK))


def pack_kernel(qkv_ref, out_ref, vectors_ref, packed_ref, small_ref):
    rows, wide = out_ref.shape
    for pair in range(wide // PAIR):
        for i in range(3):
            start = (3 * pair + i) * PAIR
            packed_ref[:, start : start + PAIR] = qkv_ref[i, :, pair * PAIR : (pair + 1) * PAIR]
    packed_ref[:, 3 * wide : 4 * wide] = out_ref[...]
    small_ref[...] = jnp.zeros_like(small_ref)
    small_ref[0:6, :rows] = vectors_ref[...].astype(F32)
    packed_ref[:, 4 * wide :] = jnp.zeros_like(packed_ref[:, 4 * wide :])
    packed_ref[:, 4 * wide : 4 * wide + 8] = small_ref[...].T[:rows].astype(BF)


def pack(qkv_weight, out_weight, gains, shifts):
    rows, wide = out_weight.shape
    args = (qkv_weight, out_weight, jnp.concatenate([gains, shifts], axis=0))
    shape = (rows, 4 * wide + PAIR)
    return pl.pallas_call(
        pack_kernel,
        out_shape=jax.ShapeDtypeStruct(shape, BF),
        scratch_shapes=[pltpu.VMEM((8, PAIR), F32)],
        cost_estimate=FREE,
        compiler_params=pltpu.CompilerParams(vmem_limit_bytes=4 * 2**20),
        name="pack",
    )(*args)


def finish_ff_kernel(kept_ref, got_ref, *out_refs):
    total = kept_ref[...] + got_ref[...].astype(F32)
    start = 0
    for out_ref in out_refs:
        columns = out_ref.shape[1]
        out_ref[...] = total[:, start : start + columns]
        start += columns


def finish_last_kernel(
    qkv_ref, qkv_got_ref, sums_ref, sums_got_ref, start_ref, *out_refs
):
    grad_ref, gains_ref, shifts_ref, qv_ref, bias_ref = out_refs
    pairs = qv_ref.shape[1] // PAIR
    grad = qkv_ref[...] + qkv_got_ref[...].astype(F32)
    for pair in range(pairs):
        for i in range(3):
            start = (3 * pair + i) * PAIR
            grad_ref[i, :, pair * PAIR : (pair + 1) * PAIR] = grad[:, start : start + PAIR]
    own = gains_ref.shape[1]
    total = sums_ref[...] + sums_got_ref[...]
    columns = total.shape[1]
    rows = pltpu.roll(total[:8], columns - start_ref[0], 1)[:, :own]
    gains_ref[...] = jnp.concatenate([rows[0:1], rows[2:3]], axis=0)
    shifts_ref[...] = jnp.concatenate([rows[1:2], rows[3:6]], axis=0)
    for pair in range(pairs):
        for i in range(2):
            here = slice(2 * i * PAIR, (2 * i + 1) * PAIR)
            qv_ref[i : i + 1, pair * PAIR : (pair + 1) * PAIR] = total[6 + pair : 7 + pair, here]
    for i in range(total.shape[0] - 6 - pairs):
        bias_ref[pl.ds(i * columns, columns)] = total[6 + pairs + i]


def finish_last(args, start, shapes):
    return pl.pallas_call(
        finish_last_kernel,
        in_specs=[pl.BlockSpec(memory_space=pltpu.VMEM)] * 4
        + [pl.BlockSpec(memory_space=pltpu.SMEM)],
        out_specs=[pl.BlockSpec(memory_space=pltpu.VMEM)] * 5,
        out_shape=[jax.ShapeDtypeStruct(x, F32) for x in shapes],
        cost_estimate=FREE,
        compiler_params=pltpu.CompilerParams(vmem_limit_bytes=4 * 2**20),
        name="finish_last",
    )(*args, start)


def finish(kernel, kept, got, shapes, name):
    return pl.pallas_call(
        kernel,
        out_shape=[jax.ShapeDtypeStruct(x, F32) for x in shapes],
        cost_estimate=FREE,
        compiler_params=pltpu.CompilerParams(vmem_limit_bytes=8 * 2**20),
        name=name,
    )(kept, got)


def join_kernel(mine_ref, other_ref, out_ref):
    half = mine_ref.shape[0]
    out_ref[:half] = mine_ref[...]
    out_ref[half:] = other_ref[...]


def join(mine, other):
    rows, columns = mine.shape
    shape = jax.ShapeDtypeStruct((2 * rows, columns), mine.dtype)
    return rows_call(join_kernel, shape, "join")(mine, other)


def standardized(x):
    center = x - jnp.mean(x, axis=-1, keepdims=True)
    inv_std = lax.rsqrt(jnp.mean(center * center, axis=-1, keepdims=True) + EPS)
    return center * inv_std, inv_std


def project_kernel(x_ref, weight_ref, bias_ref, normed_ref, qkv_ref, vectors_ref):
    width = qkv_ref.shape[1]
    small = weight_ref.shape[1] - PAIR
    vectors = weight_ref[:, small:].astype(F32).T[:8]
    vectors_ref[...] = vectors
    qv = bias_ref[...].astype(F32)
    none = jnp.zeros((1, PAIR), F32)
    bias = []
    for start in range(0, qv.shape[1], PAIR):
        bias += [qv[0:1, start : start + PAIR], none, qv[1:2, start : start + PAIR]]
    bias = jnp.concatenate(bias, axis=1)

    def step(here):
        unit, _ = standardized(x_ref[here].astype(F32))
        normed = (unit * vectors_ref[0:1] + vectors_ref[2:3]).astype(BF)
        normed_ref[here] = normed
        qkv_ref[here] = (dot(normed, weight_ref[:, :width], 1, 0) + bias).astype(BF)

    each_block(x_ref.shape[0], step)


def project(x, first_full, bias, width):
    rows, columns = x.shape
    shapes = [
        jax.ShapeDtypeStruct((rows, columns), BF),
        jax.ShapeDtypeStruct((rows, width), BF),
        jax.ShapeDtypeStruct((8, columns), F32),
    ]
    return rows_call(project_kernel, shapes, "project")(x, first_full, bias)


def halves_of(refs, others):
    half = others[0].shape[0]
    return [
        ([ref.at[pl.ds(i * half, half)] for ref in refs], others[1 - i]) for i in range(PIECES)
    ]


def mid_norm_kernel(x_ref, mine_ref, vectors_ref, *refs):
    others, (hidden_ref, normed_ref) = refs[:PIECES], refs[PIECES:]
    for refs, other_ref in halves_of((x_ref, mine_ref, hidden_ref, normed_ref), others):
        frames, mine, hidden_half, normed_half = refs

        def step(here):
            branch = mine[here].astype(F32) + other_ref[here].astype(F32)
            hidden = frames[here].astype(F32) + (branch + vectors_ref[3:4])
            hidden_half[here] = hidden
            unit, _ = standardized(hidden)
            normed_half[here] = (unit * vectors_ref[1:2] + vectors_ref[4:5]).astype(BF)

        each_block(other_ref.shape[0], step)


def mid_norm(x, mine, others, vectors):
    shapes = [jax.ShapeDtypeStruct(x.shape, t) for t in (F32, BF)]
    return rows_call(mid_norm_kernel, shapes, "mid_norm")(x, mine, vectors, *others)


def act_kernel(x_ref, weight_ref, bias_ref, act_ref, slope_ref, row_ref):
    row_ref[...] = bias_ref[...].astype(F32).reshape(1, bias_ref.shape[0])

    @pl.loop(0, act_ref.shape[1] // ACT_BLOCK)
    def _(i):
        here = pl.ds(pl.multiple_of(i * ACT_BLOCK, ACT_BLOCK), ACT_BLOCK)
        pre = dot(x_ref[...], weight_ref[:, here], 1, 0) + row_ref[:, here]
        cdf = 0.5 * (1.0 + lax.erf(pre * 0.5**0.5))
        act_ref[:, here] = (pre * cdf).astype(BF)
        slope = cdf + pre * jnp.exp(-0.5 * pre * pre) * 0.3989422804014327
        slope_ref[:, here] = slope.astype(BF)


def act(x, weight, bias):
    shape = jax.ShapeDtypeStruct((x.shape[0], weight.shape[1]), BF)
    scratch = [pltpu.VMEM((1, bias.shape[0]), F32)]
    return rows_call(act_kernel, [shape, shape], "act", scratch)(x, weight, bias)


def act_back_kernel(d_out_ref, weight_ref, slope_ref, d_pre_ref, sums_ref):
    @pl.loop(0, d_pre_ref.shape[1] // COLUMN_BLOCK)
    def _(i):
        here = pl.ds(pl.multiple_of(i * COLUMN_BLOCK, COLUMN_BLOCK), COLUMN_BLOCK)
        d_act = dot(d_out_ref[...], weight_ref[:, here], 1, 0)
        d_pre = (d_act * slope_ref[:, here].astype(F32)).astype(BF)
        d_pre_ref[:, here] = d_pre
        sums_ref[:, here] = total_rows(d_pre.astype(F32))


def act_back(d_out, weight, slope):
    shapes = [jax.ShapeDtypeStruct(slope.shape, BF), jax.ShapeDtypeStruct((1, slope.shape[1]), F32)]
    return rows_call(act_back_kernel, shapes, "act_back")(d_out, weight, slope)


def norm_back(unit, inv_std, gain, grad):
    scaled = grad * gain
    return inv_std * (
        scaled
        - jnp.mean(scaled, axis=-1, keepdims=True)
        - unit * jnp.mean(scaled * unit, axis=-1, keepdims=True)
    )


def total_rows(x):
    return jnp.sum(x, axis=0, keepdims=True)


def mid_norm_back_kernel(mine_ref, hidden_ref, d_out_ref, vectors_ref, *refs):
    others, (branch_ref, d_hidden_ref, sums_ref) = refs[:PIECES], refs[PIECES:]
    sums_ref[...] = jnp.zeros_like(sums_ref)
    halves = halves_of((mine_ref, hidden_ref, d_out_ref, branch_ref), others)
    for i, (refs, other_ref) in enumerate(halves):
        mine, hidden, d_outs, branch = refs

        def step(here):
            grad = mine[here].astype(F32) + other_ref[here].astype(F32)
            unit, inv_std = standardized(hidden[here])
            d_out = d_outs[here].astype(F32)
            d_hidden = d_out + norm_back(unit, inv_std, vectors_ref[1:2], grad)
            d_branch = d_hidden.astype(BF)
            branch[here] = d_branch
            if i == 0:
                d_hidden_ref[here] = d_hidden
                terms = (grad * unit, d_branch.astype(F32), grad, d_out)
                sums_ref[...] += jnp.concatenate([total_rows(x) for x in terms], axis=0)

        each_block(other_ref.shape[0], step)


def mid_norm_back(mine, others, hidden, d_out, vectors):
    rows, columns = hidden.shape
    shapes = [
        jax.ShapeDtypeStruct((rows, columns), BF),
        jax.ShapeDtypeStruct((rows // 2, columns), F32),
        jax.ShapeDtypeStruct((4, columns), F32),
    ]
    return rows_call(mid_norm_back_kernel, shapes, "mid_norm_back")(
        mine, hidden, d_out, vectors, *others
    )


def first_norm_back_kernel(
    qkv_ref, weight_ref, x_ref, d_hidden_ref, vectors_ref, first_ref, second_ref, grad_ref, sums_ref
):
    width = qkv_ref.shape[1]
    sums_ref[...] = jnp.zeros_like(sums_ref)

    @pl.loop(0, x_ref.shape[0] // ROW_BLOCK)
    def _(i):
        here = pl.ds(pl.multiple_of(i * ROW_BLOCK, ROW_BLOCK), ROW_BLOCK)
        other = jnp.where(i == 0, first_ref[...], second_ref[...]).astype(F32)
        grad = dot(qkv_ref[here], weight_ref[:, :width], 1, 1) + other
        unit, inv_std = standardized(x_ref[here].astype(F32))
        grad_ref[here] = d_hidden_ref[here] + norm_back(unit, inv_std, vectors_ref[0:1], grad)
        sums_ref[0:1] += total_rows(grad * unit)
        sums_ref[1:2] += total_rows(grad)


def first_norm_back(d_qkv, first_full, others, x, d_hidden, vectors):
    rows, columns = x.shape
    shapes = [jax.ShapeDtypeStruct((n, columns), F32) for n in (rows, 2)]
    return rows_call(first_norm_back_kernel, shapes, "first_norm_back")(
        d_qkv, first_full, x, d_hidden, vectors, *others
    )


def last_terms_kernel(d_qkv_ref, first_ref, act_ref, end_ref, d_other_ref, other_ref, mine_ref):
    half, columns = mine_ref.shape
    width = d_qkv_ref.shape[1]
    others = pl.ds(half, half)
    d_qkv, act_other = d_qkv_ref.at[others], act_ref.at[others]

    def step(here):
        d_other = dot(d_qkv[here], first_ref[:, :width], 1, 1)
        d_other_ref[here] = d_other.astype(BF)
        other_ref[here] = dot(act_other[here], end_ref[...], 1, 1).astype(BF)
        mine_ref[here] = dot(act_ref[here], end_ref[...], 1, 1)

    each_block(half, step)


def last_terms(d_qkv, first_full, hidden_act, end_full):
    shape = (d_qkv.shape[0] // 2, end_full.shape[0])
    shapes = [jax.ShapeDtypeStruct(shape, t) for t in (BF, BF, F32)]
    return rows_call(last_terms_kernel, shapes, "last_terms")(
        d_qkv, first_full, hidden_act, end_full
    )


def mm(spec, a, b):
    return jnp.einsum(spec, a, b, preferred_element_type=F32)


def body(
    inputs,
    cotangent,
    qkv_weight,
    out_weight,
    fc1_weight,
    fc2_weight,
    norm_gains,
    shifts,
    qv_bias,
    fc1_bias,
):
    inputs = inputs[0]
    cotangent = cotangent[0]
    own = norm_gains.shape[1]
    wide = qkv_weight.shape[2]
    pairs = wide // PAIR

    first_own = pack(qkv_weight, out_weight.T, norm_gains, shifts)
    at = position(own)
    half = inputs.shape[0]
    hidden_n = fc1_weight.shape[1]
    high = [stride for stride, _ in reversed(digits_of(lax.axis_size("dp"))[1:])]
    first_own, at = stage(first_own, at)
    first_part = gather_high_at_once(first_own, at)
    inputs_other = swap_core(inputs)

    ff_own = jnp.concatenate([fc1_weight, fc2_weight.T], axis=1)

    first_part, inputs_other, ff_part = stage(first_part, inputs_other, ff_own[None])
    first_near = gather_near(first_part)
    inputs_all = join(inputs, inputs_other)
    for stride in high:
        ff_part = place([ff_part, swap_dp(ff_part, stride)], stride, at)

    first_part, first_near, inputs_all = stage(first_part, first_near, inputs_all)
    first_far = gather_far(first_near)

    first_part, first_near, first_far, ff_part = stage(first_part, first_near, first_far, ff_part)
    ff_near = gather_near(ff_part)
    cotangent_other = swap_core(after(cotangent, first_part))
    first_full = all_rows([first_part, *first_near, *first_far], 0, first_part.shape[2], at)
    out_full = first_full[:, 3 * wide : 4 * wide]
    normed_all, qkv, vectors = project(inputs_all, first_full, qv_bias, 3 * wide)
    attended, log_sums = attend(qkv, 0, pairs)
    branch = mm("fe,de->fd", attended, out_full).astype(BF)
    branch_other = swap_pieces(branch, PIECES)
    hidden_all, normed_two_all = mid_norm(inputs_all, branch, branch_other, vectors)

    ff_part, ff_near, normed_two_all, cotangent_other = stage(
        ff_part, ff_near, normed_two_all, cotangent_other
    )
    mid_far = gather_far([x[:, :, :hidden_n] for x in ff_near])
    d_out_all = join(cotangent, cotangent_other)

    ff_part, ff_near, mid_far, d_out_all = stage(ff_part, ff_near, mid_far, d_out_all)
    end_far = gather_far([x[:, :, hidden_n:] for x in ff_near])
    mid_full = all_rows([ff_part, *ff_near, *mid_far], 0, hidden_n, at)
    hidden_act, slope = act(normed_two_all, mid_full, fc1_bias)
    hidden_act, slope, d_out_all = stage(hidden_act, slope, d_out_all)
    fc2_grad = mm("fd,fh->dh", d_out_all, hidden_act).astype(BF)
    fc2_parts, fc2_ops = scatter_operands(fc2_grad, at)

    ff_part, ff_near, end_far, d_out_all, fc2_ops = stage(
        ff_part, ff_near, end_far, d_out_all, fc2_ops
    )
    fc2_far = scatter_low_across(fc2_ops)
    end_full = all_rows([ff_part, *ff_near, *end_far], hidden_n, hidden_n, at)
    d_pre, fc1_bias_grad = act_back(d_out_all, end_full, slope)
    d_two = mm("fh,dh->fd", d_pre, mid_full).astype(BF)

    d_two, fc2_far, d_pre = stage(d_two, fc2_far, d_pre)
    fc2_ops = near_operands(fc2_parts, fc2_far)
    fc2_near = scatter_low_near(fc2_ops)
    d_two_other = swap_pieces(after(d_two, fc2_ops), PIECES)
    fc1_grad = mm("fd,fh->dh", normed_two_all, d_pre).astype(BF)
    d_branch_all, d_hidden, mid_sums = mid_norm_back(
        d_two, d_two_other, hidden_all, d_out_all, vectors
    )
    d_attended = mm("fd,de->fe", d_branch_all, out_full).astype(BF)
    out_grad = mm("fd,fe->de", d_branch_all, attended).astype(BF)
    mid_parts, mid_ops = scatter_operands(jnp.concatenate([fc1_grad, out_grad], axis=1), at)

    d_attended, mid_ops = stage(d_attended, mid_ops)
    mid_far = scatter_low_across(mid_ops)
    d_proj = attend_back(qkv, log_sums, d_attended, 0, pairs - 1, 2 * half)

    d_proj, mid_far, fc2_near = stage(d_proj, mid_far, fc2_near)
    mid_ops = near_operands(mid_parts, mid_far)
    mid_near = scatter_low_near(mid_ops)
    fc2_near = after(fc2_near, mid_ops)
    fc2_sum = scatter_high_step(high_operands(total_of(fc2_near), 0, at), 0)
    d_qkv, d_sums = attend_back(qkv, log_sums, d_attended, pairs - 1, 1, half, d_proj)
    qkv_grad = mm("fd,fe->de", normed_all, d_qkv).astype(BF)
    qkv_parts, qkv_ops = scatter_operands(qkv_grad, at)

    qkv_ops, d_qkv, fc2_sum, hidden_act = stage(qkv_ops, d_qkv, fc2_sum, hidden_act)
    qkv_far = scatter_low_across(qkv_ops)
    d_other, mlp_other, mlp_mine = last_terms(d_qkv, first_full, hidden_act, end_full)
    fc2_last = scatter_high_last(fc2_sum, 1, at)

    qkv_far, mid_near, d_other, mlp_other, mlp_mine, fc2_last = stage(
        qkv_far, mid_near, d_other, mlp_other, mlp_mine, fc2_last
    )
    qkv_ops = near_operands(qkv_parts, qkv_far)
    mid_near = after(mid_near, qkv_ops)
    qkv_near = scatter_low_near(qkv_ops)
    mid_sum = scatter_high_step(high_operands(total_of(mid_near), 0, at), 0)
    d_other_got = swap_pieces(d_other, 2)
    input_grad, first_sums = first_norm_back(
        d_qkv, first_full, d_other_got, inputs, d_hidden, vectors
    )
    rows = jnp.concatenate([first_sums, mid_sums], axis=0)
    rows = rows + swap_core(rows)

    mid_sum, qkv_near, rows = stage(mid_sum, qkv_near, rows)
    width = rows.shape[1]
    flat = [rows, jnp.pad(d_sums[:, 0], ((0, 0), (0, width - 3 * PAIR)))]
    flat += [fc1_bias_grad[:, i : i + width] for i in range(0, fc1_bias_grad.shape[1], width)]
    flat = sum_over(jnp.concatenate(flat, axis=0), [1, 2])
    qkv_sum = scatter_high_step(high_operands(total_of(qkv_near), 0, at), 0)
    mlp_got = swap_core(mlp_other)
    mid_last = scatter_high_last(mid_sum, 1, at)

    qkv_sum, flat, mlp_got = stage(qkv_sum, flat, mlp_got)
    outputs = hidden_all[:half] + ((mlp_mine + mlp_got.astype(F32)) + vectors[5:6])
    flat = sum_over(flat, high[:0:-1])
    qkv_out, gains_out, shifts_out, qv_out, bias_out = finish_last(
        (*scatter_high_last(qkv_sum, 1, at), flat, swap_dp(flat, high[0])),
        at["start"],
        [qkv_weight.shape, norm_gains.shape, shifts.shape, qv_bias.shape, fc1_bias.shape],
    )
    mid_last = after(mid_last[0], qkv_sum), mid_last[1]
    (fc2_out,) = finish(finish_ff_kernel, *fc2_last, [(own, hidden_n)], "finish_fc2")
    fc1_out, out_out = finish(
        finish_ff_kernel, *mid_last, [(own, n) for n in (hidden_n, wide)], "finish_mid"
    )
    return (
        outputs[None],
        input_grad[None],
        qkv_out,
        out_out.T,
        fc1_out,
        fc2_out.T,
        gains_out,
        shifts_out,
        qv_out,
        bias_out,
    )


def solution(mesh):
    specs = (
        P("dp", "tensor", None),
        P("dp", "tensor", None),
        P(None, "dp", "tensor"),
        P("tensor", "dp"),
        P("dp", "tensor"),
        P("tensor", "dp"),
        P(None, "dp"),
        P(None, "dp"),
        P(None, "tensor"),
        P("tensor"),
    )
    return jax.shard_map(body, mesh=mesh, in_specs=specs, out_specs=specs, check_vma=False)
```

```python
import functools

import jax
import jax.numpy as jnp
from jax import lax
from jax.experimental import pallas as pl
from jax.experimental.pallas import tpu as pltpu
from jax.sharding import PartitionSpec as P

HEAD = 64
PAIR = 2 * HEAD
ATTEND_VMEM = 20 * 2**20
BACK_VMEM = 24 * 2**20
ROWS_VMEM = 16 * 2**20
PIECES = 2
ROW_BLOCK = 256
COLUMN_BLOCK = 768
ACT_BLOCK = 768
FREE = pl.CostEstimate(flops=0, bytes_accessed=0, transcendentals=0)
EPS = 1e-05
BF = jnp.bfloat16
F32 = jnp.float32


def after(x, *others):
    return lax.optimization_barrier((x, others))[0]


def stage(*values):
    return lax.optimization_barrier(values)


def digits_of(n):
    low = 4 if n % 4 == 0 else n
    found, stride = [(1, low)], low
    while stride < n:
        found.append((stride, 2))
        stride *= 2
    return found


def swap_dp(x, step):
    n = lax.axis_size("dp")
    return lax.ppermute(x, "dp", [(i, i ^ step) for i in range(n)])


def swap_core(x):
    return lax.ppermute(x, "tensor", [(0, 1), (1, 0)])


def position(own):
    n = lax.axis_size("dp")
    me = lax.axis_index("dp")
    bits = [(me >> i) & 1 for i in range(n.bit_length() - 1)]
    low = me & 3
    return {
        "bits": [(me & (1 << i)) != 0 for i in range(len(bits))],
        "low": [low ^ k for k in range(4)],
        "high": [[bit, 1 - bit] for bit in bits[2:]],
        "digit": low.reshape(1),
        "start": (me * own).reshape(1),
    }


def pick(options, bits):
    for bit in bits:
        options = [jnp.where(bit, b, a) for a, b in zip(options[0::2], options[1::2])]
    return options[0]


def place(got, stride, at):
    radix = len(got)
    first = stride.bit_length() - 1
    bits = at["bits"][first : first + radix.bit_length() - 1]
    placed = [pick([got[i ^ m] for m in range(radix)], bits) for i in range(radix)]
    return jnp.stack(placed, axis=1).reshape((-1,) + got[0].shape[1:])


def gather_high_at_once(x, at):
    n = lax.axis_size("dp")
    low = digits_of(n)[0][1]
    stride = n // 4
    cur = place([x[None]] + [swap_dp(x[None], stride * k) for k in range(1, 4)], stride, at)
    while stride > low:
        stride //= 2
        cur = place([cur, swap_dp(cur, stride)], stride, at)
    return cur


def gather_near(cur):
    return swap_dp(cur, 1), swap_dp(cur, 2)


def gather_far(near):
    half = near[0].shape[0] // 2
    return swap_dp(near[0][:half], 2), swap_dp(near[1][half:], 1)


def gather_low(cur):
    return [swap_dp(cur, k) for k in range(1, digits_of(lax.axis_size("dp"))[0][1])]


def rows_kernel(start, mine_ref, *refs):
    sources, out_ref = refs[:-1], refs[-1]
    high, _, _, columns = out_ref.shape
    mine = mine_ref[0]
    here = pl.ds(start, columns)
    for i in range(high):
        for k, source in enumerate(sources[:3]):
            out_ref[i, mine ^ k] = source[i, :, here]
        far = sources[3 + i * (len(sources) - 3) // high]
        out_ref[i, mine ^ 3] = far[i % far.shape[0]]


def all_rows(sources, start, columns, at):
    high, rows, _ = sources[0].shape
    full = pl.pallas_call(
        functools.partial(rows_kernel, start),
        in_specs=[pl.BlockSpec(memory_space=pltpu.SMEM)]
        + [pl.BlockSpec(memory_space=pltpu.VMEM)] * len(sources),
        out_specs=pl.BlockSpec(memory_space=pltpu.VMEM),
        out_shape=jax.ShapeDtypeStruct((high, 4, rows, columns), BF),
        cost_estimate=FREE,
        compiler_params=pltpu.CompilerParams(vmem_limit_bytes=ROWS_VMEM),
        name="all_rows",
    )(at["digit"], *sources)
    return full.reshape(-1, columns)


def part_of(view, index, first=0, count=0):
    sizes = (count or view.shape[0], 1) + view.shape[2:]
    starts = [jnp.int32(first), index] + [jnp.int32(0)] * (view.ndim - 2)
    piece = lax.dynamic_slice(view, starts, sizes, allow_negative_indices=False)
    return piece.reshape(sizes[:1] + sizes[2:])


def total_of(parts):
    total = parts[0].astype(F32)
    for part in parts[1:]:
        total = total + part.astype(F32)
    return total


def scatter_operands(x, at):
    n = lax.axis_size("dp")
    view = x.reshape(n // 4, 4, x.shape[0] // n, x.shape[1])
    half = view.shape[0] // 2
    one, two, across = (
        [part_of(view, index, first, half) for first in (0, half)] for index in at["low"][1:]
    )
    return (part_of(view, at["low"][0]), one, two), across


def scatter_low_across(operands):
    return swap_dp(operands[0], 1), swap_dp(operands[1], 2)


def near_operands(parts, across):
    mine, one, two = parts
    one = jnp.concatenate([one[0], total_of([one[1], across[1]]).astype(BF)], axis=0)
    two = jnp.concatenate([total_of([two[0], across[0]]).astype(BF), two[1]], axis=0)
    return mine, one, two


def scatter_low_near(operands):
    mine, one, two = operands
    return mine, swap_dp(one, 1), swap_dp(two, 2)


def high_operands(cur, index, at):
    view = cur.reshape((-1, 2) + cur.shape[1:])
    kept, sent = (part_of(view, i) for i in at["high"][index])
    return kept, sent.astype(BF)


def scatter_high_step(operands, index):
    stride, _ = digits_of(lax.axis_size("dp"))[1 + index]
    return operands[0] + swap_dp(operands[1], stride).astype(F32)


def scatter_high_last(cur, index, at):
    digits = digits_of(lax.axis_size("dp"))[1:]
    for i in range(index, len(digits) - 1):
        cur = scatter_high_step(high_operands(cur, i, at), i)
    kept, sent = high_operands(cur, len(digits) - 1, at)
    return kept[0], swap_dp(sent, digits[-1][0])[0]


def sum_over(x, steps):
    for step in steps:
        x = x + swap_dp(x, step)
    return x


def swap_pieces(x, count):
    rows = x.shape[0] // count
    return [swap_core(x[i * rows : (i + 1) * rows]) for i in range(count)]


def dot(a, b, ca, cb):
    return lax.dot_general(a, b, (((ca,), (cb,)), ((), ())), preferred_element_type=F32)


def attend_kernel(qkv_ref, *refs):
    out_ref, lse_ref = refs[-2:]
    keys_all = qkv_ref[:, PAIR : 2 * PAIR] * jnp.asarray(HEAD**-0.5, BF)
    values = qkv_ref[:, 2 * PAIR :]
    first = lax.broadcasted_iota(jnp.int32, (1, PAIR), 1) < HEAD
    block = qkv_ref.shape[0] // 2

    @pl.loop(0, 2)
    def _(i):
        rows = pl.ds(pl.multiple_of(i * block, block), block)
        queries = qkv_ref[rows, :PAIR]
        outs, logs = [], []
        for own in (first, ~first):
            here = jnp.where(own, queries, jnp.zeros_like(queries))
            scores = dot(keys_all, here, 1, 1)
            row_max = jnp.max(scores, axis=0, keepdims=True)
            powers = jnp.exp(scores - row_max)
            summed = jnp.sum(powers, axis=0, keepdims=True)
            probs = (powers * (1.0 / summed)).astype(BF)
            outs.append(dot(values, probs, 0, 0))
            logs.append(row_max + jnp.log(summed))
        both = jnp.concatenate([outs[0][:HEAD], outs[1][HEAD:]], axis=0)
        out_ref[rows] = both.T.astype(BF)
        lse_ref[0, :, rows] = jnp.concatenate(logs, axis=0)


def attend(qkv, start, count, kept=()):
    n, width = qkv.shape
    pairs = width // (3 * PAIR)
    return pl.pallas_call(
        attend_kernel,
        grid=(count,),
        in_specs=[pl.BlockSpec((n, 3 * PAIR), lambda p: (0, p + start))]
        + [pl.BlockSpec(memory_space=pl.ANY)] * len(kept),
        out_specs=[
            pl.BlockSpec((n, PAIR), lambda p: (0, p + start)),
            pl.BlockSpec((1, 2, n), lambda p: (p + start, 0, 0)),
        ],
        out_shape=[
            jax.ShapeDtypeStruct((n, pairs * PAIR), BF),
            jax.ShapeDtypeStruct((pairs, 2, n), F32),
        ],
        input_output_aliases={1 + i: i for i in range(len(kept))},
        compiler_params=pltpu.CompilerParams(vmem_limit_bytes=ATTEND_VMEM),
        cost_estimate=FREE,
        name="attend",
    )(qkv, *kept)


def attend_back_kernel(block, qkv_ref, lse_ref, grad_ref, *refs):
    out_ref, sum_ref, d_keys_ref, d_values_ref = refs[-4:]
    n = qkv_ref.shape[0]
    keys_small = qkv_ref[:, PAIR : 2 * PAIR] * jnp.asarray(HEAD**-0.5, BF)
    values = qkv_ref[:, 2 * PAIR :]
    first = lax.broadcasted_iota(jnp.int32, (1, PAIR), 1) < HEAD

    def chunk(here):
        queries = qkv_ref[here, :PAIR]
        grad = grad_ref[here]
        parts = []
        for own in (first, ~first):
            q_here = jnp.where(own, queries, jnp.zeros_like(queries))
            g_here = jnp.where(own, grad, jnp.zeros_like(grad))
            parts.append(
                (q_here, g_here, dot(keys_small, q_here, 1, 1), dot(values, g_here, 1, 1))
            )
        d_q, d_k, d_v = [], [], []
        for head, (q_here, g_here, scores, d_probs) in enumerate(parts):
            probs = jnp.exp(scores - lse_ref[0, head : head + 1, here])
            product = probs * d_probs
            row_sum = jnp.sum(product, axis=0, keepdims=True)
            d_scores = (product - probs * row_sum).astype(BF)
            d_v.append(dot(probs.astype(BF), g_here, 1, 0))
            d_k.append(dot(d_scores, q_here, 1, 0))
            d_q.append(dot(keys_small, d_scores, 0, 0))
        queries_t = jnp.concatenate([d_q[0][:HEAD], d_q[1][HEAD:]], axis=0)
        out_ref[here, :PAIR] = queries_t.T.astype(BF)
        return d_k[0] + d_k[1], d_v[0] + d_v[1]

    def finish(d_keys, d_values):
        out_ref[:, PAIR : 2 * PAIR] = (d_keys * HEAD**-0.5).astype(BF)
        out_ref[:, 2 * PAIR :] = d_values.astype(BF)
        for i in range(0, 3 * PAIR, PAIR):
            here = slice(i, i + PAIR)
            sum_ref[0, :, here] = total_rows(out_ref[:, here].astype(F32))

    if block == n:
        finish(*chunk(slice(None)))
        return

    d_keys_ref[...] = jnp.zeros_like(d_keys_ref)
    d_values_ref[...] = jnp.zeros_like(d_values_ref)

    @pl.loop(0, n // block)
    def _(i):
        d_keys, d_values = chunk(pl.ds(pl.multiple_of(i * block, block), block))
        d_keys_ref[...] += d_keys
        d_values_ref[...] += d_values

    finish(d_keys_ref[...], d_values_ref[...])


def attend_back(qkv, lse, grad, start, count, block, kept=()):
    n, width = qkv.shape
    pairs = width // (3 * PAIR)
    return pl.pallas_call(
        functools.partial(attend_back_kernel, block),
        grid=(count,),
        in_specs=[
            pl.BlockSpec((n, 3 * PAIR), lambda p: (0, p + start)),
            pl.BlockSpec((1, 2, n), lambda p: (p + start, 0, 0)),
            pl.BlockSpec((n, PAIR), lambda p: (0, p + start)),
        ]
        + [pl.BlockSpec(memory_space=pl.ANY)] * len(kept),
        out_specs=[
            pl.BlockSpec((n, 3 * PAIR), lambda p: (0, p + start)),
            pl.BlockSpec((1, 1, 3 * PAIR), lambda p: (p + start, 0, 0)),
        ],
        out_shape=[
            jax.ShapeDtypeStruct((n, width), BF),
            jax.ShapeDtypeStruct((pairs, 1, 3 * PAIR), F32),
        ],
        scratch_shapes=[pltpu.VMEM((n, PAIR), F32)] * 2,
        input_output_aliases={3 + i: i for i in range(len(kept))},
        compiler_params=pltpu.CompilerParams(vmem_limit_bytes=BACK_VMEM),
        cost_estimate=FREE,
        name="attend_back",
    )(qkv, lse, grad, *kept)


def rows_call(kernel, out_shape, name, scratch=()):
    return pl.pallas_call(
        kernel,
        out_shape=out_shape,
        scratch_shapes=scratch,
        cost_estimate=FREE,
        compiler_params=pltpu.CompilerParams(vmem_limit_bytes=ROWS_VMEM),
        name=name,
    )


def each_block(rows, step):
    @pl.loop(0, rows // ROW_BLOCK)
    def _(i):
        step(pl.ds(pl.multiple_of(i * ROW_BLOCK, ROW_BLOCK), ROW_BLOCK))


def pack_kernel(qkv_ref, out_ref, vectors_ref, packed_ref, small_ref):
    rows, wide = out_ref.shape
    for pair in range(wide // PAIR):
        for i in range(3):
            start = (3 * pair + i) * PAIR
            packed_ref[:, start : start + PAIR] = qkv_ref[i, :, pair * PAIR : (pair + 1) * PAIR]
    packed_ref[:, 3 * wide : 4 * wide] = out_ref[...]
    small_ref[...] = jnp.zeros_like(small_ref)
    small_ref[0:6, :rows] = vectors_ref[...].astype(F32)
    packed_ref[:, 4 * wide :] = jnp.zeros_like(packed_ref[:, 4 * wide :])
    packed_ref[:, 4 * wide : 4 * wide + 8] = small_ref[...].T[:rows].astype(BF)


def pack(qkv_weight, out_weight, gains, shifts):
    rows, wide = out_weight.shape
    args = (qkv_weight, out_weight, jnp.concatenate([gains, shifts], axis=0))
    shape = (rows, 4 * wide + PAIR)
    return pl.pallas_call(
        pack_kernel,
        out_shape=jax.ShapeDtypeStruct(shape, BF),
        scratch_shapes=[pltpu.VMEM((8, PAIR), F32)],
        cost_estimate=FREE,
        compiler_params=pltpu.CompilerParams(vmem_limit_bytes=4 * 2**20),
        name="pack",
    )(*args)


def finish_ff_kernel(kept_ref, got_ref, *out_refs):
    total = kept_ref[...] + got_ref[...].astype(F32)
    start = 0
    for out_ref in out_refs:
        columns = out_ref.shape[1]
        out_ref[...] = total[:, start : start + columns]
        start += columns


def finish_last_kernel(
    qkv_ref, qkv_got_ref, sums_ref, sums_got_ref, start_ref, *out_refs
):
    grad_ref, gains_ref, shifts_ref, qv_ref, bias_ref = out_refs
    pairs = qv_ref.shape[1] // PAIR
    grad = qkv_ref[...] + qkv_got_ref[...].astype(F32)
    for pair in range(pairs):
        for i in range(3):
            start = (3 * pair + i) * PAIR
            grad_ref[i, :, pair * PAIR : (pair + 1) * PAIR] = grad[:, start : start + PAIR]
    own = gains_ref.shape[1]
    total = sums_ref[...] + sums_got_ref[...]
    columns = total.shape[1]
    rows = pltpu.roll(total[:8], columns - start_ref[0], 1)[:, :own]
    gains_ref[...] = jnp.concatenate([rows[0:1], rows[2:3]], axis=0)
    shifts_ref[...] = jnp.concatenate([rows[1:2], rows[3:6]], axis=0)
    for pair in range(pairs):
        for i in range(2):
            here = slice(2 * i * PAIR, (2 * i + 1) * PAIR)
            qv_ref[i : i + 1, pair * PAIR : (pair + 1) * PAIR] = total[6 + pair : 7 + pair, here]
    for i in range(total.shape[0] - 6 - pairs):
        bias_ref[pl.ds(i * columns, columns)] = total[6 + pairs + i]


def finish_last(args, start, shapes):
    return pl.pallas_call(
        finish_last_kernel,
        in_specs=[pl.BlockSpec(memory_space=pltpu.VMEM)] * 4
        + [pl.BlockSpec(memory_space=pltpu.SMEM)],
        out_specs=[pl.BlockSpec(memory_space=pltpu.VMEM)] * 5,
        out_shape=[jax.ShapeDtypeStruct(x, F32) for x in shapes],
        cost_estimate=FREE,
        compiler_params=pltpu.CompilerParams(vmem_limit_bytes=4 * 2**20),
        name="finish_last",
    )(*args, start)


def finish(kernel, kept, got, shapes, name):
    return pl.pallas_call(
        kernel,
        out_shape=[jax.ShapeDtypeStruct(x, F32) for x in shapes],
        cost_estimate=FREE,
        compiler_params=pltpu.CompilerParams(vmem_limit_bytes=8 * 2**20),
        name=name,
    )(kept, got)


def join_kernel(mine_ref, other_ref, out_ref):
    half = mine_ref.shape[0]
    out_ref[:half] = mine_ref[...]
    out_ref[half:] = other_ref[...]


def join(mine, other):
    rows, columns = mine.shape
    shape = jax.ShapeDtypeStruct((2 * rows, columns), mine.dtype)
    return rows_call(join_kernel, shape, "join")(mine, other)


def standardized(x):
    center = x - jnp.mean(x, axis=-1, keepdims=True)
    inv_std = lax.rsqrt(jnp.mean(center * center, axis=-1, keepdims=True) + EPS)
    return center * inv_std, inv_std


def project_kernel(x_ref, weight_ref, bias_ref, normed_ref, qkv_ref, vectors_ref):
    width = qkv_ref.shape[1]
    small = weight_ref.shape[1] - PAIR
    vectors = weight_ref[:, small:].astype(F32).T[:8]
    vectors_ref[...] = vectors
    qv = bias_ref[...].astype(F32)
    none = jnp.zeros((1, PAIR), F32)
    bias = []
    for start in range(0, qv.shape[1], PAIR):
        bias += [qv[0:1, start : start + PAIR], none, qv[1:2, start : start + PAIR]]
    bias = jnp.concatenate(bias, axis=1)

    def step(here):
        unit, _ = standardized(x_ref[here].astype(F32))
        normed = (unit * vectors_ref[0:1] + vectors_ref[2:3]).astype(BF)
        normed_ref[here] = normed
        qkv_ref[here] = (dot(normed, weight_ref[:, :width], 1, 0) + bias).astype(BF)

    each_block(x_ref.shape[0], step)


def project(x, first_full, bias, width):
    rows, columns = x.shape
    shapes = [
        jax.ShapeDtypeStruct((rows, columns), BF),
        jax.ShapeDtypeStruct((rows, width), BF),
        jax.ShapeDtypeStruct((8, columns), F32),
    ]
    return rows_call(project_kernel, shapes, "project")(x, first_full, bias)


def halves_of(refs, others):
    half = others[0].shape[0]
    return [
        ([ref.at[pl.ds(i * half, half)] for ref in refs], others[1 - i]) for i in range(PIECES)
    ]


def mid_norm_kernel(x_ref, mine_ref, vectors_ref, *refs):
    others, (hidden_ref, normed_ref) = refs[:PIECES], refs[PIECES:]
    for refs, other_ref in halves_of((x_ref, mine_ref, hidden_ref, normed_ref), others):
        frames, mine, hidden_half, normed_half = refs

        def step(here):
            branch = mine[here].astype(F32) + other_ref[here].astype(F32)
            hidden = frames[here].astype(F32) + (branch + vectors_ref[3:4])
            hidden_half[here] = hidden
            unit, _ = standardized(hidden)
            normed_half[here] = (unit * vectors_ref[1:2] + vectors_ref[4:5]).astype(BF)

        each_block(other_ref.shape[0], step)


def mid_norm(x, mine, others, vectors):
    shapes = [jax.ShapeDtypeStruct(x.shape, t) for t in (F32, BF)]
    return rows_call(mid_norm_kernel, shapes, "mid_norm")(x, mine, vectors, *others)


def act_kernel(x_ref, weight_ref, bias_ref, act_ref, slope_ref, row_ref):
    row_ref[...] = bias_ref[...].astype(F32).reshape(1, bias_ref.shape[0])

    @pl.loop(0, act_ref.shape[1] // ACT_BLOCK)
    def _(i):
        here = pl.ds(pl.multiple_of(i * ACT_BLOCK, ACT_BLOCK), ACT_BLOCK)
        pre = dot(x_ref[...], weight_ref[:, here], 1, 0) + row_ref[:, here]
        cdf = 0.5 * (1.0 + lax.erf(pre * 0.5**0.5))
        act_ref[:, here] = (pre * cdf).astype(BF)
        slope = cdf + pre * jnp.exp(-0.5 * pre * pre) * 0.3989422804014327
        slope_ref[:, here] = slope.astype(BF)


def act(x, weight, bias):
    shape = jax.ShapeDtypeStruct((x.shape[0], weight.shape[1]), BF)
    scratch = [pltpu.VMEM((1, bias.shape[0]), F32)]
    return rows_call(act_kernel, [shape, shape], "act", scratch)(x, weight, bias)


def act_back_kernel(d_out_ref, weight_ref, slope_ref, d_pre_ref, sums_ref):
    @pl.loop(0, d_pre_ref.shape[1] // COLUMN_BLOCK)
    def _(i):
        here = pl.ds(pl.multiple_of(i * COLUMN_BLOCK, COLUMN_BLOCK), COLUMN_BLOCK)
        d_act = dot(d_out_ref[...], weight_ref[:, here], 1, 0)
        d_pre = (d_act * slope_ref[:, here].astype(F32)).astype(BF)
        d_pre_ref[:, here] = d_pre
        sums_ref[:, here] = total_rows(d_pre.astype(F32))


def act_back(d_out, weight, slope):
    shapes = [jax.ShapeDtypeStruct(slope.shape, BF), jax.ShapeDtypeStruct((1, slope.shape[1]), F32)]
    return rows_call(act_back_kernel, shapes, "act_back")(d_out, weight, slope)


def norm_back(unit, inv_std, gain, grad):
    scaled = grad * gain
    return inv_std * (
        scaled
        - jnp.mean(scaled, axis=-1, keepdims=True)
        - unit * jnp.mean(scaled * unit, axis=-1, keepdims=True)
    )


def total_rows(x):
    return jnp.sum(x, axis=0, keepdims=True)


def mid_norm_back_kernel(mine_ref, hidden_ref, d_out_ref, vectors_ref, *refs):
    others, (branch_ref, d_hidden_ref, sums_ref) = refs[:PIECES], refs[PIECES:]
    sums_ref[...] = jnp.zeros_like(sums_ref)
    halves = halves_of((mine_ref, hidden_ref, d_out_ref, branch_ref), others)
    for i, (refs, other_ref) in enumerate(halves):
        mine, hidden, d_outs, branch = refs

        def step(here):
            grad = mine[here].astype(F32) + other_ref[here].astype(F32)
            unit, inv_std = standardized(hidden[here])
            d_out = d_outs[here].astype(F32)
            d_hidden = d_out + norm_back(unit, inv_std, vectors_ref[1:2], grad)
            d_branch = d_hidden.astype(BF)
            branch[here] = d_branch
            if i == 0:
                d_hidden_ref[here] = d_hidden
                terms = (grad * unit, d_branch.astype(F32), grad, d_out)
                sums_ref[...] += jnp.concatenate([total_rows(x) for x in terms], axis=0)

        each_block(other_ref.shape[0], step)


def mid_norm_back(mine, others, hidden, d_out, vectors):
    rows, columns = hidden.shape
    shapes = [
        jax.ShapeDtypeStruct((rows, columns), BF),
        jax.ShapeDtypeStruct((rows // 2, columns), F32),
        jax.ShapeDtypeStruct((4, columns), F32),
    ]
    return rows_call(mid_norm_back_kernel, shapes, "mid_norm_back")(
        mine, hidden, d_out, vectors, *others
    )


def first_norm_back_kernel(
    qkv_ref, weight_ref, x_ref, d_hidden_ref, vectors_ref, first_ref, second_ref, grad_ref, sums_ref
):
    width = qkv_ref.shape[1]
    sums_ref[...] = jnp.zeros_like(sums_ref)

    @pl.loop(0, x_ref.shape[0] // ROW_BLOCK)
    def _(i):
        here = pl.ds(pl.multiple_of(i * ROW_BLOCK, ROW_BLOCK), ROW_BLOCK)
        other = jnp.where(i == 0, first_ref[...], second_ref[...]).astype(F32)
        grad = dot(qkv_ref[here], weight_ref[:, :width], 1, 1) + other
        unit, inv_std = standardized(x_ref[here].astype(F32))
        grad_ref[here] = d_hidden_ref[here] + norm_back(unit, inv_std, vectors_ref[0:1], grad)
        sums_ref[0:1] += total_rows(grad * unit)
        sums_ref[1:2] += total_rows(grad)


def first_norm_back(d_qkv, first_full, others, x, d_hidden, vectors):
    rows, columns = x.shape
    shapes = [jax.ShapeDtypeStruct((n, columns), F32) for n in (rows, 2)]
    return rows_call(first_norm_back_kernel, shapes, "first_norm_back")(
        d_qkv, first_full, x, d_hidden, vectors, *others
    )


def last_terms_kernel(d_qkv_ref, first_ref, act_ref, end_ref, d_other_ref, other_ref, mine_ref):
    half, columns = mine_ref.shape
    width = d_qkv_ref.shape[1]
    others = pl.ds(half, half)
    d_qkv, act_other = d_qkv_ref.at[others], act_ref.at[others]

    def step(here):
        d_other = dot(d_qkv[here], first_ref[:, :width], 1, 1)
        d_other_ref[here] = d_other.astype(BF)
        other_ref[here] = dot(act_other[here], end_ref[...], 1, 1).astype(BF)
        mine_ref[here] = dot(act_ref[here], end_ref[...], 1, 1)

    each_block(half, step)


def last_terms(d_qkv, first_full, hidden_act, end_full):
    shape = (d_qkv.shape[0] // 2, end_full.shape[0])
    shapes = [jax.ShapeDtypeStruct(shape, t) for t in (BF, BF, F32)]
    return rows_call(last_terms_kernel, shapes, "last_terms")(
        d_qkv, first_full, hidden_act, end_full
    )


def mm(spec, a, b):
    return jnp.einsum(spec, a, b, preferred_element_type=F32)


def body(
    inputs,
    cotangent,
    qkv_weight,
    out_weight,
    fc1_weight,
    fc2_weight,
    norm_gains,
    shifts,
    qv_bias,
    fc1_bias,
):
    inputs = inputs[0]
    cotangent = cotangent[0]
    own = norm_gains.shape[1]
    wide = qkv_weight.shape[2]
    pairs = wide // PAIR

    first_own = pack(qkv_weight, out_weight.T, norm_gains, shifts)
    at = position(own)
    half = inputs.shape[0]
    hidden_n = fc1_weight.shape[1]
    high = [stride for stride, _ in reversed(digits_of(lax.axis_size("dp"))[1:])]
    first_own, at = stage(first_own, at)
    first_part = gather_high_at_once(first_own, at)
    inputs_other = swap_core(inputs)

    ff_own = jnp.concatenate([fc1_weight, fc2_weight.T], axis=1)

    first_part, inputs_other, ff_part = stage(first_part, inputs_other, ff_own[None])
    first_near = gather_near(first_part)
    inputs_all = join(inputs, inputs_other)
    for stride in high:
        ff_part = place([ff_part, swap_dp(ff_part, stride)], stride, at)

    first_part, first_near, inputs_all = stage(first_part, first_near, inputs_all)
    first_far = gather_far(first_near)

    first_part, first_near, first_far, ff_part = stage(first_part, first_near, first_far, ff_part)
    ff_near = gather_near(ff_part)
    cotangent_other = swap_core(after(cotangent, first_part))
    first_full = all_rows([first_part, *first_near, *first_far], 0, first_part.shape[2], at)
    out_full = first_full[:, 3 * wide : 4 * wide]
    normed_all, qkv, vectors = project(inputs_all, first_full, qv_bias, 3 * wide)
    attended, log_sums = attend(qkv, 0, pairs)
    branch = mm("fe,de->fd", attended, out_full).astype(BF)
    branch_other = swap_pieces(branch, PIECES)
    hidden_all, normed_two_all = mid_norm(inputs_all, branch, branch_other, vectors)

    ff_part, ff_near, normed_two_all, cotangent_other = stage(
        ff_part, ff_near, normed_two_all, cotangent_other
    )
    mid_far = gather_far([x[:, :, :hidden_n] for x in ff_near])
    d_out_all = join(cotangent, cotangent_other)

    ff_part, ff_near, mid_far, d_out_all = stage(ff_part, ff_near, mid_far, d_out_all)
    end_far = gather_far([x[:, :, hidden_n:] for x in ff_near])
    mid_full = all_rows([ff_part, *ff_near, *mid_far], 0, hidden_n, at)
    hidden_act, slope = act(normed_two_all, mid_full, fc1_bias)
    hidden_act, slope, d_out_all = stage(hidden_act, slope, d_out_all)
    fc2_grad = mm("fd,fh->dh", d_out_all, hidden_act).astype(BF)
    fc2_parts, fc2_ops = scatter_operands(fc2_grad, at)

    ff_part, ff_near, end_far, d_out_all, fc2_ops = stage(
        ff_part, ff_near, end_far, d_out_all, fc2_ops
    )
    fc2_far = scatter_low_across(fc2_ops)
    end_full = all_rows([ff_part, *ff_near, *end_far], hidden_n, hidden_n, at)
    d_pre, fc1_bias_grad = act_back(d_out_all, end_full, slope)
    d_two = mm("fh,dh->fd", d_pre, mid_full).astype(BF)

    d_two, fc2_far, d_pre = stage(d_two, fc2_far, d_pre)
    fc2_ops = near_operands(fc2_parts, fc2_far)
    fc2_near = scatter_low_near(fc2_ops)
    d_two_other = swap_pieces(after(d_two, fc2_ops), PIECES)
    fc1_grad = mm("fd,fh->dh", normed_two_all, d_pre).astype(BF)
    d_branch_all, d_hidden, mid_sums = mid_norm_back(
        d_two, d_two_other, hidden_all, d_out_all, vectors
    )
    d_attended = mm("fd,de->fe", d_branch_all, out_full).astype(BF)
    out_grad = mm("fd,fe->de", d_branch_all, attended).astype(BF)
    mid_parts, mid_ops = scatter_operands(jnp.concatenate([fc1_grad, out_grad], axis=1), at)

    d_attended, mid_ops = stage(d_attended, mid_ops)
    mid_far = scatter_low_across(mid_ops)
    d_proj = attend_back(qkv, log_sums, d_attended, 0, pairs - 1, 2 * half)

    d_proj, mid_far, fc2_near = stage(d_proj, mid_far, fc2_near)
    mid_ops = near_operands(mid_parts, mid_far)
    mid_near = scatter_low_near(mid_ops)
    fc2_near = after(fc2_near, mid_ops)
    fc2_sum = scatter_high_step(high_operands(total_of(fc2_near), 0, at), 0)
    d_qkv, d_sums = attend_back(qkv, log_sums, d_attended, pairs - 1, 1, half, d_proj)
    qkv_grad = mm("fd,fe->de", normed_all, d_qkv).astype(BF)
    qkv_parts, qkv_ops = scatter_operands(qkv_grad, at)

    qkv_ops, d_qkv, fc2_sum, hidden_act = stage(qkv_ops, d_qkv, fc2_sum, hidden_act)
    qkv_far = scatter_low_across(qkv_ops)
    d_other, mlp_other, mlp_mine = last_terms(d_qkv, first_full, hidden_act, end_full)
    fc2_last = scatter_high_last(fc2_sum, 1, at)

    qkv_far, mid_near, d_other, mlp_other, mlp_mine, fc2_last = stage(
        qkv_far, mid_near, d_other, mlp_other, mlp_mine, fc2_last
    )
    qkv_ops = near_operands(qkv_parts, qkv_far)
    mid_near = after(mid_near, qkv_ops)
    qkv_near = scatter_low_near(qkv_ops)
    mid_kept, mid_sent = high_operands(total_of(mid_near), 0, at)
    mid_got = swap_dp(mid_sent, digits_of(lax.axis_size("dp"))[1][0])
    d_other_got = swap_pieces(d_other, 2)
    input_grad, first_sums = first_norm_back(
        d_qkv, first_full, d_other_got, inputs, d_hidden, vectors
    )
    rows = jnp.concatenate([first_sums, mid_sums], axis=0)
    rows = rows + swap_core(rows)

    mid_kept, mid_got, qkv_near, rows = stage(mid_kept, mid_got, qkv_near, rows)
    mid_sum = mid_kept + mid_got.astype(F32)
    width = rows.shape[1]
    flat = [rows, jnp.pad(d_sums[:, 0], ((0, 0), (0, width - 3 * PAIR)))]
    flat += [fc1_bias_grad[:, i : i + width] for i in range(0, fc1_bias_grad.shape[1], width)]
    flat = sum_over(jnp.concatenate(flat, axis=0), [1, 2])
    qkv_sum = scatter_high_step(high_operands(total_of(qkv_near), 0, at), 0)
    mlp_got = swap_core(mlp_other)
    mid_last = scatter_high_last(mid_sum, 1, at)

    qkv_sum, flat, mlp_got = stage(qkv_sum, flat, mlp_got)
    outputs = hidden_all[:half] + ((mlp_mine + mlp_got.astype(F32)) + vectors[5:6])
    flat = sum_over(flat, high[:0:-1])
    qkv_out, gains_out, shifts_out, qv_out, bias_out = finish_last(
        (*scatter_high_last(qkv_sum, 1, at), flat, swap_dp(flat, high[0])),
        at["start"],
        [qkv_weight.shape, norm_gains.shape, shifts.shape, qv_bias.shape, fc1_bias.shape],
    )
    mid_last = after(mid_last[0], qkv_sum), mid_last[1]
    (fc2_out,) = finish(finish_ff_kernel, *fc2_last, [(own, hidden_n)], "finish_fc2")
    fc1_out, out_out = finish(
        finish_ff_kernel, *mid_last, [(own, n) for n in (hidden_n, wide)], "finish_mid"
    )
    return (
        outputs[None],
        input_grad[None],
        qkv_out,
        out_out.T,
        fc1_out,
        fc2_out.T,
        gains_out,
        shifts_out,
        qv_out,
        bias_out,
    )


def solution(mesh):
    specs = (
        P("dp", "tensor", None),
        P("dp", "tensor", None),
        P(None, "dp", "tensor"),
        P("tensor", "dp"),
        P("dp", "tensor"),
        P("tensor", "dp"),
        P(None, "dp"),
        P(None, "dp"),
        P(None, "tensor"),
        P("tensor"),
    )
    return jax.shard_map(body, mesh=mesh, in_specs=specs, out_specs=specs, check_vma=False)
```

```python
import functools

import jax
import jax.numpy as jnp
from jax import lax
from jax.experimental import pallas as pl
from jax.experimental.pallas import tpu as pltpu
from jax.sharding import PartitionSpec as P

HEAD = 64
PAIR = 2 * HEAD
ATTEND_VMEM = 20 * 2**20
BACK_VMEM = 24 * 2**20
ROWS_VMEM = 16 * 2**20
PIECES = 2
ROW_BLOCK = 256
COLUMN_BLOCK = 512
ACT_BLOCK = 256
FREE = pl.CostEstimate(flops=0, bytes_accessed=0, transcendentals=0)
EPS = 1e-05
BF = jnp.bfloat16
F32 = jnp.float32


def after(x, *others):
    return lax.optimization_barrier((x, others))[0]


def stage(*values):
    return lax.optimization_barrier(values)


def digits_of(n):
    low = 4 if n % 4 == 0 else n
    found, stride = [(1, low)], low
    while stride < n:
        found.append((stride, 2))
        stride *= 2
    return found


def swap_dp(x, step):
    n = lax.axis_size("dp")
    return lax.ppermute(x, "dp", [(i, i ^ step) for i in range(n)])


def swap_core(x):
    return lax.ppermute(x, "tensor", [(0, 1), (1, 0)])


def position(own):
    n = lax.axis_size("dp")
    me = lax.axis_index("dp")
    bits = [(me >> i) & 1 for i in range(n.bit_length() - 1)]
    low = me & 3
    return {
        "bits": [(me & (1 << i)) != 0 for i in range(len(bits))],
        "low": [low ^ k for k in range(4)],
        "high": [[bit, 1 - bit] for bit in bits[2:]],
        "digit": low.reshape(1),
        "start": (me * own).reshape(1),
    }


def pick(options, bits):
    for bit in bits:
        options = [jnp.where(bit, b, a) for a, b in zip(options[0::2], options[1::2])]
    return options[0]


def place(got, stride, at):
    radix = len(got)
    first = stride.bit_length() - 1
    bits = at["bits"][first : first + radix.bit_length() - 1]
    placed = [pick([got[i ^ m] for m in range(radix)], bits) for i in range(radix)]
    return jnp.stack(placed, axis=1).reshape((-1,) + got[0].shape[1:])


def gather_high_at_once(x, at):
    n = lax.axis_size("dp")
    low = digits_of(n)[0][1]
    stride = n // 4
    cur = place([x[None]] + [swap_dp(x[None], stride * k) for k in range(1, 4)], stride, at)
    while stride > low:
        stride //= 2
        cur = place([cur, swap_dp(cur, stride)], stride, at)
    return cur


def gather_near(cur):
    return swap_dp(cur, 1), swap_dp(cur, 2)


def gather_far(near):
    half = near[0].shape[0] // 2
    return swap_dp(near[0][:half], 2), swap_dp(near[1][half:], 1)


def gather_low(cur):
    return [swap_dp(cur, k) for k in range(1, digits_of(lax.axis_size("dp"))[0][1])]


def rows_kernel(start, mine_ref, *refs):
    sources, out_ref = refs[:-1], refs[-1]
    high, _, _, columns = out_ref.shape
    mine = mine_ref[0]
    here = pl.ds(start, columns)
    for i in range(high):
        for k, source in enumerate(sources[:3]):
            out_ref[i, mine ^ k] = source[i, :, here]
        far = sources[3 + i * (len(sources) - 3) // high]
        out_ref[i, mine ^ 3] = far[i % far.shape[0]]


def all_rows(sources, start, columns, at):
    high, rows, _ = sources[0].shape
    full = pl.pallas_call(
        functools.partial(rows_kernel, start),
        in_specs=[pl.BlockSpec(memory_space=pltpu.SMEM)]
        + [pl.BlockSpec(memory_space=pltpu.VMEM)] * len(sources),
        out_specs=pl.BlockSpec(memory_space=pltpu.VMEM),
        out_shape=jax.ShapeDtypeStruct((high, 4, rows, columns), BF),
        cost_estimate=FREE,
        compiler_params=pltpu.CompilerParams(vmem_limit_bytes=ROWS_VMEM),
        name="all_rows",
    )(at["digit"], *sources)
    return full.reshape(-1, columns)


def part_of(view, index, first=0, count=0):
    sizes = (count or view.shape[0], 1) + view.shape[2:]
    starts = [jnp.int32(first), index] + [jnp.int32(0)] * (view.ndim - 2)
    piece = lax.dynamic_slice(view, starts, sizes, allow_negative_indices=False)
    return piece.reshape(sizes[:1] + sizes[2:])


def total_of(parts):
    total = parts[0].astype(F32)
    for part in parts[1:]:
        total = total + part.astype(F32)
    return total


def scatter_operands(x, at):
    n = lax.axis_size("dp")
    view = x.reshape(n // 4, 4, x.shape[0] // n, x.shape[1])
    half = view.shape[0] // 2
    one, two, across = (
        [part_of(view, index, first, half) for first in (0, half)] for index in at["low"][1:]
    )
    return (part_of(view, at["low"][0]), one, two), across


def scatter_low_across(operands):
    return swap_dp(operands[0], 1), swap_dp(operands[1], 2)


def near_operands(parts, across):
    mine, one, two = parts
    one = jnp.concatenate([one[0], total_of([one[1], across[1]]).astype(BF)], axis=0)
    two = jnp.concatenate([total_of([two[0], across[0]]).astype(BF), two[1]], axis=0)
    return mine, one, two


def scatter_low_near(operands):
    mine, one, two = operands
    return mine, swap_dp(one, 1), swap_dp(two, 2)


def high_operands(cur, index, at):
    view = cur.reshape((-1, 2) + cur.shape[1:])
    kept, sent = (part_of(view, i) for i in at["high"][index])
    return kept, sent.astype(BF)


def scatter_high_step(operands, index):
    stride, _ = digits_of(lax.axis_size("dp"))[1 + index]
    return operands[0] + swap_dp(operands[1], stride).astype(F32)


def scatter_high_last(cur, index, at):
    digits = digits_of(lax.axis_size("dp"))[1:]
    for i in range(index, len(digits) - 1):
        cur = scatter_high_step(high_operands(cur, i, at), i)
    kept, sent = high_operands(cur, len(digits) - 1, at)
    return kept[0], swap_dp(sent, digits[-1][0])[0]


def sum_over(x, steps):
    for step in steps:
        x = x + swap_dp(x, step)
    return x


def swap_pieces(x, count):
    rows = x.shape[0] // count
    return [swap_core(x[i * rows : (i + 1) * rows]) for i in range(count)]


def dot(a, b, ca, cb):
    return lax.dot_general(a, b, (((ca,), (cb,)), ((), ())), preferred_element_type=F32)


def attend_kernel(qkv_ref, *refs):
    out_ref, lse_ref = refs[-2:]
    keys_all = qkv_ref[:, PAIR : 2 * PAIR] * jnp.asarray(HEAD**-0.5, BF)
    values = qkv_ref[:, 2 * PAIR :]
    first = lax.broadcasted_iota(jnp.int32, (1, PAIR), 1) < HEAD
    block = qkv_ref.shape[0] // 2

    @pl.loop(0, 2)
    def _(i):
        rows = pl.ds(pl.multiple_of(i * block, block), block)
        queries = qkv_ref[rows, :PAIR]
        outs, logs = [], []
        for own in (first, ~first):
            here = jnp.where(own, queries, jnp.zeros_like(queries))
            scores = dot(keys_all, here, 1, 1)
            row_max = jnp.max(scores, axis=0, keepdims=True)
            powers = jnp.exp(scores - row_max)
            summed = jnp.sum(powers, axis=0, keepdims=True)
            probs = (powers * (1.0 / summed)).astype(BF)
            outs.append(dot(values, probs, 0, 0))
            logs.append(row_max + jnp.log(summed))
        both = jnp.concatenate([outs[0][:HEAD], outs[1][HEAD:]], axis=0)
        out_ref[rows] = both.T.astype(BF)
        lse_ref[0, :, rows] = jnp.concatenate(logs, axis=0)


def attend(qkv, start, count, kept=()):
    n, width = qkv.shape
    pairs = width // (3 * PAIR)
    return pl.pallas_call(
        attend_kernel,
        grid=(count,),
        in_specs=[pl.BlockSpec((n, 3 * PAIR), lambda p: (0, p + start))]
        + [pl.BlockSpec(memory_space=pl.ANY)] * len(kept),
        out_specs=[
            pl.BlockSpec((n, PAIR), lambda p: (0, p + start)),
            pl.BlockSpec((1, 2, n), lambda p: (p + start, 0, 0)),
        ],
        out_shape=[
            jax.ShapeDtypeStruct((n, pairs * PAIR), BF),
            jax.ShapeDtypeStruct((pairs, 2, n), F32),
        ],
        input_output_aliases={1 + i: i for i in range(len(kept))},
        compiler_params=pltpu.CompilerParams(vmem_limit_bytes=ATTEND_VMEM),
        cost_estimate=FREE,
        name="attend",
    )(qkv, *kept)


def attend_back_kernel(block, qkv_ref, lse_ref, grad_ref, *refs):
    out_ref, sum_ref, d_keys_ref, d_values_ref = refs[-4:]
    n = qkv_ref.shape[0]
    keys_small = qkv_ref[:, PAIR : 2 * PAIR] * jnp.asarray(HEAD**-0.5, BF)
    values = qkv_ref[:, 2 * PAIR :]
    first = lax.broadcasted_iota(jnp.int32, (1, PAIR), 1) < HEAD

    def chunk(here):
        queries = qkv_ref[here, :PAIR]
        grad = grad_ref[here]
        parts = []
        for own in (first, ~first):
            q_here = jnp.where(own, queries, jnp.zeros_like(queries))
            g_here = jnp.where(own, grad, jnp.zeros_like(grad))
            parts.append(
                (q_here, g_here, dot(keys_small, q_here, 1, 1), dot(values, g_here, 1, 1))
            )
        d_q, d_k, d_v = [], [], []
        for head, (q_here, g_here, scores, d_probs) in enumerate(parts):
            probs = jnp.exp(scores - lse_ref[0, head : head + 1, here])
            product = probs * d_probs
            row_sum = jnp.sum(product, axis=0, keepdims=True)
            d_scores = (product - probs * row_sum).astype(BF)
            d_v.append(dot(probs.astype(BF), g_here, 1, 0))
            d_k.append(dot(d_scores, q_here, 1, 0))
            d_q.append(dot(keys_small, d_scores, 0, 0))
        queries_t = jnp.concatenate([d_q[0][:HEAD], d_q[1][HEAD:]], axis=0)
        out_ref[here, :PAIR] = queries_t.T.astype(BF)
        return d_k[0] + d_k[1], d_v[0] + d_v[1]

    def finish(d_keys, d_values):
        out_ref[:, PAIR : 2 * PAIR] = (d_keys * HEAD**-0.5).astype(BF)
        out_ref[:, 2 * PAIR :] = d_values.astype(BF)
        for i in range(0, 3 * PAIR, PAIR):
            here = slice(i, i + PAIR)
            sum_ref[0, :, here] = total_rows(out_ref[:, here].astype(F32))

    if block == n:
        finish(*chunk(slice(None)))
        return

    d_keys_ref[...] = jnp.zeros_like(d_keys_ref)
    d_values_ref[...] = jnp.zeros_like(d_values_ref)

    @pl.loop(0, n // block)
    def _(i):
        d_keys, d_values = chunk(pl.ds(pl.multiple_of(i * block, block), block))
        d_keys_ref[...] += d_keys
        d_values_ref[...] += d_values

    finish(d_keys_ref[...], d_values_ref[...])


def attend_back(qkv, lse, grad, start, count, block, kept=()):
    n, width = qkv.shape
    pairs = width // (3 * PAIR)
    return pl.pallas_call(
        functools.partial(attend_back_kernel, block),
        grid=(count,),
        in_specs=[
            pl.BlockSpec((n, 3 * PAIR), lambda p: (0, p + start)),
            pl.BlockSpec((1, 2, n), lambda p: (p + start, 0, 0)),
            pl.BlockSpec((n, PAIR), lambda p: (0, p + start)),
        ]
        + [pl.BlockSpec(memory_space=pl.ANY)] * len(kept),
        out_specs=[
            pl.BlockSpec((n, 3 * PAIR), lambda p: (0, p + start)),
            pl.BlockSpec((1, 1, 3 * PAIR), lambda p: (p + start, 0, 0)),
        ],
        out_shape=[
            jax.ShapeDtypeStruct((n, width), BF),
            jax.ShapeDtypeStruct((pairs, 1, 3 * PAIR), F32),
        ],
        scratch_shapes=[pltpu.VMEM((n, PAIR), F32)] * 2,
        input_output_aliases={3 + i: i for i in range(len(kept))},
        compiler_params=pltpu.CompilerParams(vmem_limit_bytes=BACK_VMEM),
        cost_estimate=FREE,
        name="attend_back",
    )(qkv, lse, grad, *kept)


def rows_call(kernel, out_shape, name, scratch=()):
    return pl.pallas_call(
        kernel,
        out_shape=out_shape,
        scratch_shapes=scratch,
        cost_estimate=FREE,
        compiler_params=pltpu.CompilerParams(vmem_limit_bytes=ROWS_VMEM),
        name=name,
    )


def each_block(rows, step):
    @pl.loop(0, rows // ROW_BLOCK)
    def _(i):
        step(pl.ds(pl.multiple_of(i * ROW_BLOCK, ROW_BLOCK), ROW_BLOCK))


def pack_kernel(qkv_ref, out_ref, vectors_ref, packed_ref, small_ref):
    rows, wide = out_ref.shape
    for pair in range(wide // PAIR):
        for i in range(3):
            start = (3 * pair + i) * PAIR
            packed_ref[:, start : start + PAIR] = qkv_ref[i, :, pair * PAIR : (pair + 1) * PAIR]
    packed_ref[:, 3 * wide : 4 * wide] = out_ref[...]
    small_ref[...] = jnp.zeros_like(small_ref)
    small_ref[0:6, :rows] = vectors_ref[...].astype(F32)
    packed_ref[:, 4 * wide :] = jnp.zeros_like(packed_ref[:, 4 * wide :])
    packed_ref[:, 4 * wide : 4 * wide + 8] = small_ref[...].T[:rows].astype(BF)


def pack(qkv_weight, out_weight, gains, shifts):
    rows, wide = out_weight.shape
    args = (qkv_weight, out_weight, jnp.concatenate([gains, shifts], axis=0))
    shape = (rows, 4 * wide + PAIR)
    return pl.pallas_call(
        pack_kernel,
        out_shape=jax.ShapeDtypeStruct(shape, BF),
        scratch_shapes=[pltpu.VMEM((8, PAIR), F32)],
        cost_estimate=FREE,
        compiler_params=pltpu.CompilerParams(vmem_limit_bytes=4 * 2**20),
        name="pack",
    )(*args)


def finish_ff_kernel(kept_ref, got_ref, *out_refs):
    total = kept_ref[...] + got_ref[...].astype(F32)
    start = 0
    for out_ref in out_refs:
        columns = out_ref.shape[1]
        out_ref[...] = total[:, start : start + columns]
        start += columns


def finish_last_kernel(
    qkv_ref, qkv_got_ref, sums_ref, sums_got_ref, start_ref, *out_refs
):
    grad_ref, gains_ref, shifts_ref, qv_ref, bias_ref = out_refs
    pairs = qv_ref.shape[1] // PAIR
    grad = qkv_ref[...] + qkv_got_ref[...].astype(F32)
    for pair in range(pairs):
        for i in range(3):
            start = (3 * pair + i) * PAIR
            grad_ref[i, :, pair * PAIR : (pair + 1) * PAIR] = grad[:, start : start + PAIR]
    own = gains_ref.shape[1]
    total = sums_ref[...] + sums_got_ref[...]
    columns = total.shape[1]
    rows = pltpu.roll(total[:8], columns - start_ref[0], 1)[:, :own]
    gains_ref[...] = jnp.concatenate([rows[0:1], rows[2:3]], axis=0)
    shifts_ref[...] = jnp.concatenate([rows[1:2], rows[3:6]], axis=0)
    for pair in range(pairs):
        for i in range(2):
            here = slice(2 * i * PAIR, (2 * i + 1) * PAIR)
            qv_ref[i : i + 1, pair * PAIR : (pair + 1) * PAIR] = total[6 + pair : 7 + pair, here]
    for i in range(total.shape[0] - 6 - pairs):
        bias_ref[pl.ds(i * columns, columns)] = total[6 + pairs + i]


def finish_last(args, start, shapes):
    return pl.pallas_call(
        finish_last_kernel,
        in_specs=[pl.BlockSpec(memory_space=pltpu.VMEM)] * 4
        + [pl.BlockSpec(memory_space=pltpu.SMEM)],
        out_specs=[pl.BlockSpec(memory_space=pltpu.VMEM)] * 5,
        out_shape=[jax.ShapeDtypeStruct(x, F32) for x in shapes],
        cost_estimate=FREE,
        compiler_params=pltpu.CompilerParams(vmem_limit_bytes=4 * 2**20),
        name="finish_last",
    )(*args, start)


def finish(kernel, kept, got, shapes, name):
    return pl.pallas_call(
        kernel,
        out_shape=[jax.ShapeDtypeStruct(x, F32) for x in shapes],
        cost_estimate=FREE,
        compiler_params=pltpu.CompilerParams(vmem_limit_bytes=8 * 2**20),
        name=name,
    )(kept, got)


def join_kernel(mine_ref, other_ref, out_ref):
    half = mine_ref.shape[0]
    out_ref[:half] = mine_ref[...]
    out_ref[half:] = other_ref[...]


def join(mine, other):
    rows, columns = mine.shape
    shape = jax.ShapeDtypeStruct((2 * rows, columns), mine.dtype)
    return rows_call(join_kernel, shape, "join")(mine, other)


def standardized(x):
    center = x - jnp.mean(x, axis=-1, keepdims=True)
    inv_std = lax.rsqrt(jnp.mean(center * center, axis=-1, keepdims=True) + EPS)
    return center * inv_std, inv_std


def project_kernel(x_ref, weight_ref, bias_ref, normed_ref, qkv_ref, vectors_ref):
    width = qkv_ref.shape[1]
    small = weight_ref.shape[1] - PAIR
    vectors = weight_ref[:, small:].astype(F32).T[:8]
    vectors_ref[...] = vectors
    qv = bias_ref[...].astype(F32)
    none = jnp.zeros((1, PAIR), F32)
    bias = []
    for start in range(0, qv.shape[1], PAIR):
        bias += [qv[0:1, start : start + PAIR], none, qv[1:2, start : start + PAIR]]
    bias = jnp.concatenate(bias, axis=1)

    def step(here):
        unit, _ = standardized(x_ref[here].astype(F32))
        normed = (unit * vectors_ref[0:1] + vectors_ref[2:3]).astype(BF)
        normed_ref[here] = normed
        qkv_ref[here] = (dot(normed, weight_ref[:, :width], 1, 0) + bias).astype(BF)

    each_block(x_ref.shape[0], step)


def project(x, first_full, bias, width):
    rows, columns = x.shape
    shapes = [
        jax.ShapeDtypeStruct((rows, columns), BF),
        jax.ShapeDtypeStruct((rows, width), BF),
        jax.ShapeDtypeStruct((8, columns), F32),
    ]
    return rows_call(project_kernel, shapes, "project")(x, first_full, bias)


def halves_of(refs, others):
    half = others[0].shape[0]
    return [
        ([ref.at[pl.ds(i * half, half)] for ref in refs], others[1 - i]) for i in range(PIECES)
    ]


def mid_norm_kernel(x_ref, mine_ref, vectors_ref, *refs):
    others, (hidden_ref, normed_ref) = refs[:PIECES], refs[PIECES:]
    for refs, other_ref in halves_of((x_ref, mine_ref, hidden_ref, normed_ref), others):
        frames, mine, hidden_half, normed_half = refs

        def step(here):
            branch = mine[here].astype(F32) + other_ref[here].astype(F32)
            hidden = frames[here].astype(F32) + (branch + vectors_ref[3:4])
            hidden_half[here] = hidden
            unit, _ = standardized(hidden)
            normed_half[here] = (unit * vectors_ref[1:2] + vectors_ref[4:5]).astype(BF)

        each_block(other_ref.shape[0], step)


def mid_norm(x, mine, others, vectors):
    shapes = [jax.ShapeDtypeStruct(x.shape, t) for t in (F32, BF)]
    return rows_call(mid_norm_kernel, shapes, "mid_norm")(x, mine, vectors, *others)


def act_kernel(x_ref, weight_ref, bias_ref, act_ref, slope_ref, row_ref):
    row_ref[...] = bias_ref[...].astype(F32).reshape(1, bias_ref.shape[0])

    @pl.loop(0, act_ref.shape[1] // ACT_BLOCK)
    def _(i):
        here = pl.ds(pl.multiple_of(i * ACT_BLOCK, ACT_BLOCK), ACT_BLOCK)
        pre = dot(x_ref[...], weight_ref[:, here], 1, 0) + row_ref[:, here]
        cdf = 0.5 * (1.0 + lax.erf(pre * 0.5**0.5))
        act_ref[:, here] = (pre * cdf).astype(BF)
        slope = cdf + pre * jnp.exp(-0.5 * pre * pre) * 0.3989422804014327
        slope_ref[:, here] = slope.astype(BF)


def act(x, weight, bias):
    shape = jax.ShapeDtypeStruct((x.shape[0], weight.shape[1]), BF)
    scratch = [pltpu.VMEM((1, bias.shape[0]), F32)]
    return rows_call(act_kernel, [shape, shape], "act", scratch)(x, weight, bias)


def act_back_kernel(d_out_ref, weight_ref, slope_ref, d_pre_ref, sums_ref):
    @pl.loop(0, d_pre_ref.shape[1] // COLUMN_BLOCK)
    def _(i):
        here = pl.ds(pl.multiple_of(i * COLUMN_BLOCK, COLUMN_BLOCK), COLUMN_BLOCK)
        d_act = dot(d_out_ref[...], weight_ref[:, here], 1, 0)
        d_pre = (d_act * slope_ref[:, here].astype(F32)).astype(BF)
        d_pre_ref[:, here] = d_pre
        sums_ref[:, here] = total_rows(d_pre.astype(F32))


def act_back(d_out, weight, slope):
    shapes = [jax.ShapeDtypeStruct(slope.shape, BF), jax.ShapeDtypeStruct((1, slope.shape[1]), F32)]
    return rows_call(act_back_kernel, shapes, "act_back")(d_out, weight, slope)


def norm_back(unit, inv_std, gain, grad):
    scaled = grad * gain
    return inv_std * (
        scaled
        - jnp.mean(scaled, axis=-1, keepdims=True)
        - unit * jnp.mean(scaled * unit, axis=-1, keepdims=True)
    )


def total_rows(x):
    return jnp.sum(x, axis=0, keepdims=True)


def mid_norm_back_kernel(mine_ref, hidden_ref, d_out_ref, vectors_ref, *refs):
    others, (branch_ref, d_hidden_ref, sums_ref) = refs[:PIECES], refs[PIECES:]
    sums_ref[...] = jnp.zeros_like(sums_ref)
    halves = halves_of((mine_ref, hidden_ref, d_out_ref, branch_ref), others)
    for i, (refs, other_ref) in enumerate(halves):
        mine, hidden, d_outs, branch = refs

        def step(here):
            grad = mine[here].astype(F32) + other_ref[here].astype(F32)
            unit, inv_std = standardized(hidden[here])
            d_out = d_outs[here].astype(F32)
            d_hidden = d_out + norm_back(unit, inv_std, vectors_ref[1:2], grad)
            d_branch = d_hidden.astype(BF)
            branch[here] = d_branch
            if i == 0:
                d_hidden_ref[here] = d_hidden
                terms = (grad * unit, d_branch.astype(F32), grad, d_out)
                sums_ref[...] += jnp.concatenate([total_rows(x) for x in terms], axis=0)

        each_block(other_ref.shape[0], step)


def mid_norm_back(mine, others, hidden, d_out, vectors):
    rows, columns = hidden.shape
    shapes = [
        jax.ShapeDtypeStruct((rows, columns), BF),
        jax.ShapeDtypeStruct((rows // 2, columns), F32),
        jax.ShapeDtypeStruct((4, columns), F32),
    ]
    return rows_call(mid_norm_back_kernel, shapes, "mid_norm_back")(
        mine, hidden, d_out, vectors, *others
    )


def first_norm_back_kernel(
    qkv_ref, weight_ref, x_ref, d_hidden_ref, vectors_ref, first_ref, second_ref, grad_ref, sums_ref
):
    width = qkv_ref.shape[1]
    sums_ref[...] = jnp.zeros_like(sums_ref)

    @pl.loop(0, x_ref.shape[0] // ROW_BLOCK)
    def _(i):
        here = pl.ds(pl.multiple_of(i * ROW_BLOCK, ROW_BLOCK), ROW_BLOCK)
        other = jnp.where(i == 0, first_ref[...], second_ref[...]).astype(F32)
        grad = dot(qkv_ref[here], weight_ref[:, :width], 1, 1) + other
        unit, inv_std = standardized(x_ref[here].astype(F32))
        grad_ref[here] = d_hidden_ref[here] + norm_back(unit, inv_std, vectors_ref[0:1], grad)
        sums_ref[0:1] += total_rows(grad * unit)
        sums_ref[1:2] += total_rows(grad)


def first_norm_back(d_qkv, first_full, others, x, d_hidden, vectors):
    rows, columns = x.shape
    shapes = [jax.ShapeDtypeStruct((n, columns), F32) for n in (rows, 2)]
    return rows_call(first_norm_back_kernel, shapes, "first_norm_back")(
        d_qkv, first_full, x, d_hidden, vectors, *others
    )


def last_terms_kernel(d_qkv_ref, first_ref, act_ref, end_ref, d_other_ref, other_ref, mine_ref):
    half, columns = mine_ref.shape
    width = d_qkv_ref.shape[1]
    others = pl.ds(half, half)
    d_qkv, act_other = d_qkv_ref.at[others], act_ref.at[others]

    def step(here):
        d_other = dot(d_qkv[here], first_ref[:, :width], 1, 1)
        d_other_ref[here] = d_other.astype(BF)
        other_ref[here] = dot(act_other[here], end_ref[...], 1, 1).astype(BF)
        mine_ref[here] = dot(act_ref[here], end_ref[...], 1, 1)

    each_block(half, step)


def last_terms(d_qkv, first_full, hidden_act, end_full):
    shape = (d_qkv.shape[0] // 2, end_full.shape[0])
    shapes = [jax.ShapeDtypeStruct(shape, t) for t in (BF, BF, F32)]
    return rows_call(last_terms_kernel, shapes, "last_terms")(
        d_qkv, first_full, hidden_act, end_full
    )


def mm(spec, a, b):
    return jnp.einsum(spec, a, b, preferred_element_type=F32)


def body(
    inputs,
    cotangent,
    qkv_weight,
    out_weight,
    fc1_weight,
    fc2_weight,
    norm_gains,
    shifts,
    qv_bias,
    fc1_bias,
):
    inputs = inputs[0]
    cotangent = cotangent[0]
    own = norm_gains.shape[1]
    wide = qkv_weight.shape[2]
    pairs = wide // PAIR

    first_own = pack(qkv_weight, out_weight.T, norm_gains, shifts)
    at = position(own)
    half = inputs.shape[0]
    hidden_n = fc1_weight.shape[1]
    high = [stride for stride, _ in reversed(digits_of(lax.axis_size("dp"))[1:])]
    first_own, at = stage(first_own, at)
    first_part = gather_high_at_once(first_own, at)
    inputs_other = swap_core(inputs)

    ff_own = jnp.concatenate([fc1_weight, fc2_weight.T], axis=1)

    first_part, inputs_other, ff_part = stage(first_part, inputs_other, ff_own[None])
    first_near = gather_near(first_part)
    inputs_all = join(inputs, inputs_other)
    for stride in high:
        ff_part = place([ff_part, swap_dp(ff_part, stride)], stride, at)

    first_part, first_near, inputs_all = stage(first_part, first_near, inputs_all)
    first_far = gather_far(first_near)

    first_part, first_near, first_far, ff_part = stage(first_part, first_near, first_far, ff_part)
    ff_near = gather_near(ff_part)
    cotangent_other = swap_core(after(cotangent, first_part))
    first_full = all_rows([first_part, *first_near, *first_far], 0, first_part.shape[2], at)
    out_full = first_full[:, 3 * wide : 4 * wide]
    normed_all, qkv, vectors = project(inputs_all, first_full, qv_bias, 3 * wide)
    attended, log_sums = attend(qkv, 0, pairs)
    branch = mm("fe,de->fd", attended, out_full).astype(BF)
    branch_other = swap_pieces(branch, PIECES)
    hidden_all, normed_two_all = mid_norm(inputs_all, branch, branch_other, vectors)

    ff_part, ff_near, normed_two_all, cotangent_other = stage(
        ff_part, ff_near, normed_two_all, cotangent_other
    )
    mid_far = gather_far([x[:, :, :hidden_n] for x in ff_near])
    d_out_all = join(cotangent, cotangent_other)

    ff_part, ff_near, mid_far, d_out_all = stage(ff_part, ff_near, mid_far, d_out_all)
    end_far = gather_far([x[:, :, hidden_n:] for x in ff_near])
    mid_full = all_rows([ff_part, *ff_near, *mid_far], 0, hidden_n, at)
    hidden_act, slope = act(normed_two_all, mid_full, fc1_bias)
    hidden_act, slope, d_out_all = stage(hidden_act, slope, d_out_all)
    fc2_grad = mm("fd,fh->dh", d_out_all, hidden_act).astype(BF)
    fc2_parts, fc2_ops = scatter_operands(fc2_grad, at)

    ff_part, ff_near, end_far, d_out_all, fc2_ops = stage(
        ff_part, ff_near, end_far, d_out_all, fc2_ops
    )
    fc2_far = scatter_low_across(fc2_ops)
    end_full = all_rows([ff_part, *ff_near, *end_far], hidden_n, hidden_n, at)
    d_pre, fc1_bias_grad = act_back(d_out_all, end_full, slope)
    d_two = mm("fh,dh->fd", d_pre, mid_full).astype(BF)

    d_two, fc2_far, d_pre = stage(d_two, fc2_far, d_pre)
    fc2_ops = near_operands(fc2_parts, fc2_far)
    fc2_near = scatter_low_near(fc2_ops)
    d_two_other = swap_pieces(after(d_two, fc2_ops), PIECES)
    fc1_grad = mm("fd,fh->dh", normed_two_all, d_pre).astype(BF)
    d_branch_all, d_hidden, mid_sums = mid_norm_back(
        d_two, d_two_other, hidden_all, d_out_all, vectors
    )
    d_attended = mm("fd,de->fe", d_branch_all, out_full).astype(BF)
    out_grad = mm("fd,fe->de", d_branch_all, attended).astype(BF)
    mid_parts, mid_ops = scatter_operands(jnp.concatenate([fc1_grad, out_grad], axis=1), at)

    d_attended, mid_ops = stage(d_attended, mid_ops)
    mid_far = scatter_low_across(mid_ops)
    d_proj = attend_back(qkv, log_sums, d_attended, 0, pairs - 1, 2 * half)

    d_proj, mid_far, fc2_near = stage(d_proj, mid_far, fc2_near)
    mid_ops = near_operands(mid_parts, mid_far)
    mid_near = scatter_low_near(mid_ops)
    fc2_near = after(fc2_near, mid_ops)
    fc2_sum = scatter_high_step(high_operands(total_of(fc2_near), 0, at), 0)
    d_qkv, d_sums = attend_back(qkv, log_sums, d_attended, pairs - 1, 1, half, d_proj)
    qkv_grad = mm("fd,fe->de", normed_all, d_qkv).astype(BF)
    qkv_parts, qkv_ops = scatter_operands(qkv_grad, at)

    qkv_ops, d_qkv, fc2_sum, hidden_act = stage(qkv_ops, d_qkv, fc2_sum, hidden_act)
    qkv_far = scatter_low_across(qkv_ops)
    d_other, mlp_other, mlp_mine = last_terms(d_qkv, first_full, hidden_act, end_full)
    fc2_last = scatter_high_last(fc2_sum, 1, at)

    qkv_far, mid_near, d_other, mlp_other, mlp_mine, fc2_last = stage(
        qkv_far, mid_near, d_other, mlp_other, mlp_mine, fc2_last
    )
    qkv_ops = near_operands(qkv_parts, qkv_far)
    mid_near = after(mid_near, qkv_ops)
    qkv_near = scatter_low_near(qkv_ops)
    mid_kept, mid_sent = high_operands(total_of(mid_near), 0, at)
    mid_got = swap_dp(mid_sent, digits_of(lax.axis_size("dp"))[1][0])
    d_other_got = swap_pieces(d_other, 2)
    input_grad, first_sums = first_norm_back(
        d_qkv, first_full, d_other_got, inputs, d_hidden, vectors
    )
    rows = jnp.concatenate([first_sums, mid_sums], axis=0)
    rows = rows + swap_core(rows)

    mid_kept, mid_got, qkv_near, rows = stage(mid_kept, mid_got, qkv_near, rows)
    mid_sum = mid_kept + mid_got.astype(F32)
    width = rows.shape[1]
    flat = [rows, jnp.pad(d_sums[:, 0], ((0, 0), (0, width - 3 * PAIR)))]
    flat += [fc1_bias_grad[:, i : i + width] for i in range(0, fc1_bias_grad.shape[1], width)]
    flat = sum_over(jnp.concatenate(flat, axis=0), [1, 2])
    qkv_sum = scatter_high_step(high_operands(total_of(qkv_near), 0, at), 0)
    mlp_got = swap_core(mlp_other)
    mid_last = scatter_high_last(mid_sum, 1, at)

    qkv_sum, flat, mlp_got = stage(qkv_sum, flat, mlp_got)
    outputs = hidden_all[:half] + ((mlp_mine + mlp_got.astype(F32)) + vectors[5:6])
    flat = sum_over(flat, high[:0:-1])
    qkv_out, gains_out, shifts_out, qv_out, bias_out = finish_last(
        (*scatter_high_last(qkv_sum, 1, at), flat, swap_dp(flat, high[0])),
        at["start"],
        [qkv_weight.shape, norm_gains.shape, shifts.shape, qv_bias.shape, fc1_bias.shape],
    )
    mid_last = after(mid_last[0], qkv_sum), mid_last[1]
    (fc2_out,) = finish(finish_ff_kernel, *fc2_last, [(own, hidden_n)], "finish_fc2")
    fc1_out, out_out = finish(
        finish_ff_kernel, *mid_last, [(own, n) for n in (hidden_n, wide)], "finish_mid"
    )
    return (
        outputs[None],
        input_grad[None],
        qkv_out,
        out_out.T,
        fc1_out,
        fc2_out.T,
        gains_out,
        shifts_out,
        qv_out,
        bias_out,
    )


def solution(mesh):
    specs = (
        P("dp", "tensor", None),
        P("dp", "tensor", None),
        P(None, "dp", "tensor"),
        P("tensor", "dp"),
        P("dp", "tensor"),
        P("tensor", "dp"),
        P(None, "dp"),
        P(None, "dp"),
        P(None, "tensor"),
        P("tensor"),
    )
    return jax.shard_map(body, mesh=mesh, in_specs=specs, out_specs=specs, check_vma=False)
```
